256 devices in a mesh: dom: 32 (over y, z), band: 8 (over x, core).
Axes of the slice: x: 4, y: 4, z: 8, core: 2. Of those that a mesh axis runs over, the one named last changes fastest.
Arguments:
- orbitals: float32 [32, 128, 24, 576], P('dom', 'band'), may hold values from -6 to 6
- potential: float32 [32, 24, 576], P('dom'), may hold values from 0 to 3
- density_in: float32 [32, 24, 576], P('dom', 'band'), may hold values from 0.3 to 3
- occupation: float32 [128], replicated, may hold values from 0.5 to 2
- position: int32 [32], replicated, may hold values from 0 to 31, each once
- mixing: int32 [2], replicated, may hold values from 1 to 8
- correlation_weight: int32 [6], replicated, may hold values from 1 to 15
Outputs:
- orbitals_out: float32 [32, 128, 24, 576], P('dom', None, 'band')
- density: float32 [32, 24, 576], P('dom', 'band')
- hartree: float32 [32, 8, 8, 6], P('dom', 'band')
The draws below stay inside these ranges and needn't reach their ends.
Inputs may be any that keep to these rules, and one draw needn't show every extreme that they name: position is a permutation: every place along the chain holds exactly one domain.
All inputs are finite; a program needn't handle non-finite values.
Results may differ from the reference program's by a relative error of at most 0.0001.
Values sent between devices are 32-bit elements; how exact they have to be, the bound alone decides.
No kernel may reach another device: no remote copies, remote signals or barrier semaphores. Data moves between devices by JAX's collectives and lax.ppermute only.
A program may use at most 64 MiB of HBM per device.

```python
import math
import jax
import jax.numpy as jnp
from jax import lax

NB = 128
G = 24
BUFFER = 6
COARSEN = 3
DEGREE = 2
NS_STEPS = 2
DOMAINS = 32
CG = 8
CZ = 6
NZC = 192
N_DOM = 32


def with_ends(result, own_key, least, largest):
    shape = result.shape
    place = [jax.random.randint(jax.random.fold_in(own_key, axis), (), 0, shape[axis]) for axis in range(len(shape))]
    result = result.at[tuple(place)].set(least)
    longest = shape.index(max(shape))
    place[longest] = (place[longest] + 1) % shape[longest]
    return result.at[tuple(place)].set(largest)


def levels(key, shape, cuts, low, largest):
    level, own = 1.0, jax.random.fold_in(key, 6)
    for dim, shards_of in cuts:
        draws = jnp.exp(jax.random.uniform(jax.random.fold_in(own, dim), (shards_of,), jnp.float32, low / len(cuts), largest / len(cuts)))
        level = level * jnp.repeat(draws, shape[dim] // shards_of).reshape([-1 if axis == dim else 1 for axis in range(len(shape))])
    return level


def bell_draw(own_key, dims, deviation, most, cuts=(), kind=jnp.bfloat16):
    values = deviation * jax.random.normal(own_key, dims, jnp.float32)
    if cuts:
        values = values * levels(own_key, dims, cuts, -0.22, 0.18)
    return jnp.clip(values, -most, most).astype(kind)


def setup_inputs(seed: int = 0) -> dict:
    keys = jax.random.split(jax.random.key(seed), 8)
    return {
        "orbitals": bell_draw(keys[0], (DOMAINS, NB, G, G * G), 1.0, 6.0, ((0, 32), (1, 8)), jnp.float32),
        "potential": jnp.clip(3.0 * jax.random.uniform(keys[1], (DOMAINS, G, G * G), jnp.float32) ** levels(keys[1], (DOMAINS, G, G * G), ((0, 32),), -0.2, 0.2), 0.0, 3.0),
        "density_in": jnp.clip(jnp.exp(math.log(3.0) - 2.3025851 * jax.random.uniform(keys[2], (DOMAINS, G, G * G), jnp.float32) ** levels(keys[2], (DOMAINS, G, G * G), ((0, 32), (1, 8)), -0.2, 0.2)), 0.3, 3.0),
        "occupation": jnp.clip(jax.random.uniform(keys[3], (NB,), jnp.float32, 0.5, 2.0), 0.5, 2.0),
        "position": jax.random.permutation(keys[4], DOMAINS).astype(jnp.int32),
        "mixing": jax.random.randint(keys[5], (2,), 1, 9).astype(jnp.int32),
        "correlation_weight": with_ends(jax.random.randint(keys[6], (BUFFER,), 1, 16), jax.random.fold_in(keys[6], 1), 1, 15).astype(jnp.int32),
    }


HIGHEST = lax.Precision.HIGHEST
filter_low = 1.0
filter_high = 9.5
blend_total = 16.0

def sine_entries(row_values, col_values, extent):
    products = (row_values[:, None] + 1.0) * (col_values[None, :] + 1.0)
    return jnp.sqrt(2.0 / (extent + 1.0)) * jnp.sin(jnp.pi * products / (extent + 1.0))

def sine_table(extent):
    indices = jnp.arange(extent, dtype=jnp.float32)
    return sine_entries(indices, indices, extent)

def cosine_table(extent):
    indices = jnp.arange(extent, dtype=jnp.float32)
    entries = jnp.sqrt(2.0 / extent) * jnp.cos(jnp.pi * indices[:, None] * (indices[None, :] + 0.5) / extent)
    return entries * jnp.where(indices == 0.0, jnp.sqrt(0.5), 1.0)[:, None]

def lap_eigen(indices, extent, shift_by):
    half_angle = 0.5 * jnp.pi * (indices + shift_by) / (extent + shift_by)
    return 4.0 * jnp.sin(half_angle) ** 2

def kinetic_table(extent):
    indices = jnp.arange(extent, dtype=jnp.float32)
    single = 0.5 * lap_eigen(indices, extent, 1.0)
    plane_values = single[:, None] + single[None, :]
    return single[:, None] + plane_values.reshape(1, extent * extent)

def transform(values, sine_matrix, plane_matrix):
    values = jnp.einsum('bxc,xk->bkc', values, sine_matrix, precision=HIGHEST)
    return jnp.einsum('bxc,cd->bxd', values, plane_matrix, precision=HIGHEST)

def apply_hamil(values, potential_grid, sine_matrix, plane_matrix, kinetic):
    spectral = kinetic * transform(values, sine_matrix, plane_matrix)
    return transform(spectral, sine_matrix, plane_matrix) + potential_grid * values

def chebyshev(orbital_block, potential_grid, sine_matrix, plane_matrix, kinetic):
    center = 0.5 * (filter_high + filter_low)
    half_width = 0.5 * (filter_high - filter_low)

    def shifted(values):
        return (apply_hamil(values, potential_grid, sine_matrix, plane_matrix, kinetic) - center * values) / half_width
    before = orbital_block
    current = shifted(orbital_block)
    for repeat in range(DEGREE - 1):
        newest = 2.0 * shifted(current) - before
        before, current = (current, newest)
    return current

def reference(orbitals, potential, density_in, occupation, position, mixing, correlation_weight):
    sine_matrix = sine_table(G)
    plane_matrix = jnp.kron(sine_matrix, sine_matrix)
    kinetic = kinetic_table(G)
    points = float(G * G * G)

    def one_domain(inputs):
        orbital_block, potential_grid = inputs
        filtered = chebyshev(orbital_block, potential_grid, sine_matrix, plane_matrix, kinetic)
        flat_orbitals = filtered.reshape(NB, G * G * G)
        correlation_raw = jnp.dot(flat_orbitals, flat_orbitals.T, precision=HIGHEST)
        norm_fro = jnp.sqrt(jnp.sum(correlation_raw * correlation_raw))
        current = flat_orbitals * jnp.sqrt(points / norm_fro)
        correlation = correlation_raw / norm_fro
        for iteration in range(NS_STEPS):
            if iteration > 0:
                correlation = jnp.dot(current, current.T, precision=HIGHEST) / points
            current = 1.5 * current - 0.5 * jnp.dot(correlation, current, precision=HIGHEST)
        density_row = jnp.dot(occupation, current * current, precision=HIGHEST) / NB
        return (current.reshape(NB, G, G * G), density_row.reshape(G, G, G))
    orbitals_out, fresh_cube = lax.map(one_domain, (orbitals, potential))
    indices = jnp.arange(N_DOM, dtype=jnp.int32)
    left_of = lax.optimization_barrier(jnp.sum(jnp.where(position[None, :] == position[:, None] - 1, indices[None, :], 0), axis=1)).astype(jnp.int32)
    right_of = lax.optimization_barrier(jnp.sum(jnp.where(position[None, :] == position[:, None] + 1, indices[None, :], 0), axis=1)).astype(jnp.int32)
    has_left = (position > 0)[:, None, None, None]
    has_right = (position < N_DOM - 1)[:, None, None, None]
    weight_left = correlation_weight.astype(jnp.float32)
    own_low = fresh_cube[..., :BUFFER]
    own_high = fresh_cube[..., G - BUFFER:]
    left_high = jnp.take(fresh_cube, left_of, axis=0)[..., G - BUFFER:]
    right_low = jnp.take(fresh_cube, right_of, axis=0)[..., :BUFFER]
    blend_low = jnp.where(has_left, (weight_left * left_high + (blend_total - weight_left) * own_low) / blend_total, own_low)
    blend_high = jnp.where(has_right, (weight_left * own_high + (blend_total - weight_left) * right_low) / blend_total, own_high)
    blended = jnp.concatenate([blend_low, fresh_cube[..., BUFFER:G - BUFFER], blend_high], 3)
    mix_weights = mixing.astype(jnp.float32)
    inflow = density_in.reshape(N_DOM, G, G, G)
    mixed_density = (mix_weights[0] * blended + mix_weights[1] * inflow) / (mix_weights[0] + mix_weights[1])
    density = mixed_density.reshape(N_DOM, G, G * G)
    core_cells = mixed_density[..., :G - BUFFER].reshape(N_DOM, CG, COARSEN, CG, COARSEN, CZ, COARSEN)
    coarse = lax.optimization_barrier(jnp.sum(core_cells, axis=(2, 4, 6))) / float(COARSEN ** 3)
    dom_at = lax.optimization_barrier(jnp.sum(jnp.where(position[None, :] == indices[:, None], indices[None, :], 0), axis=1)).astype(jnp.int32)
    chain_grid = jnp.take(coarse, dom_at, axis=0)
    chain_grid = jnp.transpose(chain_grid, (1, 2, 0, 3)).reshape(CG * CG, NZC)
    sine_chain = sine_table(NZC)
    cross_table = jnp.kron(cosine_table(CG), cosine_table(CG))
    level_x = lap_eigen(jnp.arange(CG, dtype=jnp.float32), CG, 0.0)
    level_xy = (level_x[:, None] + level_x[None, :]).reshape(CG * CG)
    level_z = lap_eigen(jnp.arange(NZC, dtype=jnp.float32), NZC, 1.0)
    spectrum = jnp.dot(cross_table, jnp.dot(chain_grid, sine_chain, precision=HIGHEST), precision=HIGHEST)
    spectrum = spectrum / (level_xy[:, None] + level_z[None, :])
    field_grid = jnp.dot(cross_table.T, jnp.dot(spectrum, sine_chain, precision=HIGHEST), precision=HIGHEST)
    field_grid = field_grid * (8.0 / float(NZC * NZC))
    field_grid = field_grid.reshape(CG, CG, N_DOM, CZ)
    hartree = jnp.transpose(jnp.take(field_grid, position, axis=2), (2, 0, 1, 3))
    return (orbitals_out, density, hartree)
```

```python
import functools
import numpy as np
import jax
import jax.numpy as jnp
from jax import lax
from jax.experimental import pallas as pl
from jax.experimental.pallas import tpu as pltpu
from jax.sharding import PartitionSpec as P

NB = 128
G = 24
GG = G * G
BUFFER = 6
CG = 8
CZ = 6
NZC = 192
DOMS = 32
BANDS = 8
LOCAL = NB // BANDS
PLANES = G // BANDS
ROW = 640
SHARE = 1792
PACKED = 72
HALF_ROW = GG // 2
EDGE = GG + HALF_ROW
POINTS = float(G * G * G)
FILTER_LOW = 1.0
FILTER_HIGH = 9.5
CENTER = 0.5 * (FILTER_HIGH + FILTER_LOW)
HALF = 0.5 * (FILTER_HIGH - FILTER_LOW)
HIGHEST = lax.Precision.HIGHEST
F32 = jnp.float32
INTERPRET = False
LIMIT = pltpu.CompilerParams(vmem_limit_bytes=16 << 20)


def tables():
    k = np.arange(CG)
    cosine = np.sqrt(2.0 / CG) * np.cos(np.pi * k[:, None] * (k[None, :] + 0.5) / CG)
    cosine[0] *= np.sqrt(0.5)
    r = np.arange(NZC)
    sine = np.zeros((NZC + 8, NZC))
    sine[:NZC] = np.sqrt(2.0 / (NZC + 1)) * np.sin(np.pi * (r[:, None] + 1) * (r[None, :] + 1) / (NZC + 1))
    level_xy = 4.0 * np.sin(0.5 * np.pi * k / CG) ** 2
    level_z = 4.0 * np.sin(0.5 * np.pi * (r + 1) / (NZC + 1)) ** 2
    inverse = 1.0 / (level_xy[:, None, None] + level_xy[None, :, None] + level_z[None, None, :])
    scale = 8.0 / float(NZC * NZC)
    onto_x = np.broadcast_to((scale * cosine.T)[:, :, None], (CG, CG, NZC))
    lane = np.arange(GG)
    gather = np.zeros((ROW, 128))
    for ky in range(CG):
        gather[lane, ky * 8 + (lane % G) // 3] = cosine[ky, (lane // G) // 3]
    over_x = np.broadcast_to(cosine.T[:, :, None], (CG, CG, 128))
    over_y = np.broadcast_to(cosine[:, :, None], (CG, CG, 256))
    sine = np.stack([sine[CZ * place : CZ * place + 8] for place in range(DOMS)])
    as_f32 = lambda a: np.ascontiguousarray(a, dtype=np.float32)
    return tuple(as_f32(a) for a in (sine, inverse.reshape(CG * CG, NZC), onto_x, gather, over_x, over_y))


def halves(x):
    high = x.astype(jnp.bfloat16)
    return high, (x - high.astype(F32)).astype(jnp.bfloat16)


def dot3(x, y, dims=(((1,), (0,)), ((), ()))):
    x_high, x_low = halves(x)
    y_high, y_low = halves(y)
    dot = functools.partial(lax.dot_general, dimension_numbers=dims, preferred_element_type=F32)
    return dot(x_high, y_high) + (dot(x_high, y_low) + dot(x_low, y_high))


def rolled(x, shift):
    return pltpu.roll(x, shift % ROW, 1)


def lane_index(shape):
    lane = lax.broadcasted_iota(jnp.int32, shape, 1).astype(F32)
    return lane, lane - G * jnp.floor((lane + 0.5) * (1.0 / G))


def filter_kernel(orb_ref, pot_ref, out_ref, plane_ref, diag_ref):
    rows = orb_ref.shape[0]
    lane, z = lane_index((rows, ROW))
    inside = lane < GG
    not_first = jnp.where(z > 0.5, 1.0, 0.0)
    not_last = jnp.where(z < G - 1.5, 1.0, 0.0)
    step = jnp.where(inside, 0.5 / HALF, 0.0)
    plane_ref[...] = jnp.zeros_like(plane_ref)
    diag_ref[...] = jnp.zeros_like(diag_ref)
    diag_ref[:, :GG] = (pot_ref[...] + (3.0 - CENTER)) * (1.0 / HALF)
    zeros = jnp.zeros((rows, ROW), F32)

    def load(x):
        plane_ref[x, :, :GG] = orb_ref[:, x, :]
        return plane_ref[x]

    def near(v, below, above):
        sides = rolled(v, 1) * not_first + rolled(v, -1) * not_last
        return (sides + (rolled(v, G) + rolled(v, -G))) + (below + above)

    first = {-1: zeros, G: zeros}
    start = {-1: zeros, 0: load(0), G: zeros}
    for x in range(G + 1):
        if x < G:
            if x + 1 < G:
                start[x + 1] = load(x + 1)
            v = start[x]
            first[x] = diag_ref[x : x + 1, :] * v - step * near(v, start[x - 1], start[x + 1])
        w = x - 1
        if w >= 0:
            v = first[w]
            twice = diag_ref[w : w + 1, :] * v - step * near(v, first[w - 1], first[w + 1])
            second = 2.0 * twice - start[w]
            p = w % PLANES
            out_ref[w // PLANES, :, p * GG : (p + 1) * GG] = second[:, :GG]
            if p == PLANES - 1:
                out_ref[w // PLANES, :, PLANES * GG :] = jnp.zeros((rows, SHARE - PLANES * GG), F32)


def filtered_shares(orbitals, potential):
    rows = 8
    return pl.pallas_call(
        filter_kernel,
        out_shape=jax.ShapeDtypeStruct((BANDS, LOCAL, SHARE), F32),
        grid=(LOCAL // rows,),
        in_specs=[
            pl.BlockSpec((rows, G, GG), lambda i: (i, 0, 0)),
            pl.BlockSpec((G, GG), lambda i: (0, 0)),
        ],
        out_specs=pl.BlockSpec((BANDS, rows, SHARE), lambda i: (0, i, 0)),
        scratch_shapes=[pltpu.VMEM((G, rows, ROW), F32), pltpu.VMEM((G, ROW), F32)],
        compiler_params=LIMIT,
        interpret=INTERPRET,
        name="filter",
    )(orbitals, potential)


def gram_kernel(f_ref, out_ref):
    high, low = halves(f_ref[...])
    both = lax.dot_general(
        high, jnp.concatenate([high, low], 0), (((1,), (1,)), ((), ())), preferred_element_type=F32
    )
    cross = both[:, NB:]
    raw = both[:, :NB] + (cross + cross.T)
    row = lax.broadcasted_iota(jnp.int32, (64, NB), 0)
    col = lax.broadcasted_iota(jnp.int32, (64, NB), 1)
    lower = pltpu.roll(raw[64:], 64, 1)
    packed = jnp.where(col >= row, raw[:64], lower)
    diag = jnp.sum(jnp.where(col == row + 64, raw[64:], 0.0), axis=0, keepdims=True)
    diag = jnp.broadcast_to(diag, (8, NB))
    for k in range(BANDS):
        out_ref[k, :64] = packed
        out_ref[k, 64:] = diag


def packed_grams(flat):
    return pl.pallas_call(
        gram_kernel,
        out_shape=jax.ShapeDtypeStruct((BANDS, PACKED, NB), F32),
        compiler_params=LIMIT,
        interpret=INTERPRET,
        name="gram",
    )(flat)


def density_kernel(g_ref, f_ref, occ_ref, vec_ref, gather_ref, poly_ref, fresh_ref, coarse_ref):
    total = g_ref[0]
    for k in range(1, BANDS):
        total = total + g_ref[k]
    packed = total[:64]
    row = lax.broadcasted_iota(jnp.int32, (64, NB), 0)
    col = lax.broadcasted_iota(jnp.int32, (64, NB), 1)
    top = jnp.where(col > row, packed, jnp.where(col == row, 0.5 * packed, 0.0))
    low = pltpu.roll(jnp.where(col < row, packed, 0.0), 64, 1)
    low = low + jnp.where(col == row + 64, 0.5 * total[64:65], 0.0)
    half = jnp.concatenate([top, low], 0)
    raw = half + half.T
    norm = jnp.sqrt(jnp.sum(jnp.sum(raw * raw, axis=0, keepdims=True), axis=1, keepdims=True))
    a = raw / norm
    scaling = jnp.sqrt(POINTS / norm)
    eye = jnp.where(
        lax.broadcasted_iota(jnp.int32, (NB, NB), 0) == lax.broadcasted_iota(jnp.int32, (NB, NB), 1), 1.0, 0.0
    )
    square = dot3(a, a)
    tail = dot3(square, 0.0625 * square - 0.5625 * a)
    poly = scaling * (2.25 * eye + (1.6875 * square - 2.4375 * a) + tail)
    poly_ref[...] = poly
    poly_high, poly_low = halves(poly)
    both = jnp.concatenate([poly_high, poly_low], 1)
    dot = functools.partial(jnp.dot, preferred_element_type=F32)
    weight = jnp.broadcast_to(occ_ref[...] * (1.0 / NB), (NB, 256))
    for c in range(SHARE // 256):
        cols = slice(256 * c, 256 * (c + 1))
        high, low = halves(f_ref[:, cols])
        current = dot(both, jnp.concatenate([high, high], 0)) + dot(poly_high, low)
        line = jnp.sum(current * current * weight, axis=0, keepdims=True)
        fresh_ref[:, cols] = jnp.broadcast_to(line, (8, 256))
    planes = fresh_ref[:, :ROW] + fresh_ref[:, GG : GG + ROW] + fresh_ref[:, 2 * GG : 2 * GG + ROW]
    inside = lax.broadcasted_iota(jnp.int32, (8, ROW), 1) < GG
    cells = jnp.where(inside, vec_ref[0:1] * planes + vec_ref[1:2], 0.0)
    coarse_ref[...] = jnp.dot(cells, gather_ref[...], precision=HIGHEST, preferred_element_type=F32)


def density_rows(grams, flat, occupation, vectors, gather):
    return pl.pallas_call(
        density_kernel,
        out_shape=(
            jax.ShapeDtypeStruct((NB, NB), F32),
            jax.ShapeDtypeStruct((8, SHARE), F32),
            jax.ShapeDtypeStruct((8, 128), F32),
        ),
        compiler_params=LIMIT,
        interpret=INTERPRET,
        name="density",
    )(grams, flat, occupation, vectors, gather)


def output_kernel(poly_ref, f_ref, fresh_ref, vec_ref, out_ref, own_ref, edge_ref):
    poly_high, poly_low = halves(poly_ref[...])
    dot = functools.partial(jnp.dot, preferred_element_type=F32)
    for c in range(SHARE // 128):
        turned = f_ref[:, 128 * c : 128 * (c + 1)].T
        high, low = halves(turned)
        value = dot(high, poly_high) + (dot(high, poly_low) + dot(low, poly_high))
        count = min(128, PLANES * GG - 128 * c)
        out_ref[128 * c : 128 * c + count] = value[:count]
    lane, z = lane_index((8, ROW))
    low_edge = (z < BUFFER - 0.5) & (lane < GG)
    high_edge = (z > G - BUFFER - 0.5) & (lane < GG)
    middle = (z > BUFFER - 0.5) & (z < G - BUFFER - 0.5)
    edges = []
    for p in range(PLANES):
        plane = fresh_ref[:, p * GG : p * GG + ROW]
        own_ref[p] = (vec_ref[7:8] * plane + vec_ref[2 + p : 3 + p])[0:1]
        edges.append((jnp.where(low_edge, plane, 0.0), jnp.where(high_edge, plane, 0.0)))
    first = (edges[0][0] + edges[0][1]) + (rolled(edges[1][0], 12) + rolled(edges[1][1], -12))
    last = edges[2][0] + edges[2][1]
    lower = last + (rolled(edges[2][0], 12 - HALF_ROW) + rolled(edges[2][1], -12 - HALF_ROW))
    lower = jnp.where(lane < HALF_ROW, jnp.where(middle, 0.0, last) + jnp.where(middle, lower, 0.0), 0.0)
    first = first + rolled(jnp.where(lane < 64, lower, 0.0), GG)
    rest = rolled(lower, -64)
    edge_ref[0:1] = jnp.zeros((1, 128), F32)
    for t in range(7):
        source, at = (first, 128 * t) if t < 5 else (rest, 128 * (t - 5))
        edge_ref[t + 1 : t + 2] = source[0:1, at : at + 128]


def output_parts(poly, flat, fresh, vectors):
    return pl.pallas_call(
        output_kernel,
        out_shape=(
            jax.ShapeDtypeStruct((PLANES * GG, NB), F32),
            jax.ShapeDtypeStruct((PLANES, 1, ROW), F32),
            jax.ShapeDtypeStruct((8, 128), F32),
        ),
        cost_estimate=pl.CostEstimate(flops=200_000_000, bytes_accessed=2_000_000, transcendentals=0),
        compiler_params=LIMIT,
        interpret=INTERPRET,
        name="output",
    )(poly, flat, fresh, vectors)


def prepare_kernel(
    where_ref, pos_ref, mix_ref, corr_ref, din_ref, sine_ref, inverse_ref, onto_ref, vec_ref, side_ref, green_ref, left_ref, right_ref, din_row
):
    dom, band = where_ref[0], where_ref[1]
    own = pos_ref[dom]
    shape = (1, ROW)
    lane, z = lane_index(shape)
    corr = jnp.zeros(shape, F32)
    for j in range(BUFFER):
        here = (jnp.abs(z - j) < 0.5) | (jnp.abs(z - (G - BUFFER + j)) < 0.5)
        corr = jnp.where(here, corr_ref[j].astype(F32), corr)
    corr = corr * (1.0 / 16.0)
    fresh_weight = jnp.full(shape, mix_ref[0].astype(F32))
    input_weight = jnp.full(shape, mix_ref[1].astype(F32))
    both = fresh_weight + input_weight
    fresh_weight = fresh_weight / both
    input_weight = input_weight / both
    has_left = jnp.where(jnp.full(shape, own) > 0, 1.0, 0.0)
    has_right = jnp.where(jnp.full(shape, own) < DOMS - 1, 1.0, 0.0)
    low = z < BUFFER - 0.5
    high = z > G - BUFFER - 0.5
    from_left = jnp.where(low, corr * has_left, 0.0)
    from_right = jnp.where(high, (1.0 - corr) * has_right, 0.0)
    keep = 1.0 - from_left - from_right
    cell = 1.0 / 27.0
    vec_ref[0:1] = cell * fresh_weight * jnp.where(high, corr * has_right, keep)
    din_row[...] = jnp.zeros_like(din_row)
    for p in range(PLANES):
        din_row[p : p + 1, :GG] = din_ref[p]
    din_sum = din_row[0:1] + din_row[1:2] + din_row[2:3]
    vec_ref[1:2] = jnp.where(high, 0.0, cell * input_weight * din_sum)
    for p in range(PLANES):
        vec_ref[2 + p : 3 + p] = input_weight * din_row[p : p + 1]
    vec_ref[5:6] = fresh_weight * from_left
    vec_ref[6:7] = fresh_weight * from_right
    vec_ref[7:8] = fresh_weight * keep
    left, right = jnp.int32(0), jnp.int32(0)
    for d in range(DOMS):
        left = jnp.where(pos_ref[d] == own - 1, d, left)
        right = jnp.where(pos_ref[d] == own + 1, d, right)
        right_ref[8 * d : 8 * d + 8] = sine_ref[pos_ref[d]]
    side_ref[0] = left
    side_ref[1] = right
    mine = sine_ref[own]
    onto = onto_ref[band]
    for ky in range(CG):
        part = inverse_ref[8 * ky : 8 * ky + 8] * onto
        for j in range(8):
            at = ky * 64 + j * 8
            left_ref[at : at + 8] = part * mine[j : j + 1]
    green_ref[...] = lax.dot_general(
        left_ref[...], right_ref[...], (((1,), (1,)), ((), ())), precision=HIGHEST, preferred_element_type=F32
    )


def prepared(where, position, mixing, corr, din, sine, inverse, onto):
    smem = pl.BlockSpec(memory_space=pltpu.SMEM)
    vmem = pl.BlockSpec(memory_space=pltpu.VMEM)
    return pl.pallas_call(
        prepare_kernel,
        out_shape=(
            jax.ShapeDtypeStruct((8, ROW), F32),
            jax.ShapeDtypeStruct((2,), jnp.int32),
            jax.ShapeDtypeStruct((512, 256), F32),
        ),
        in_specs=[smem] * 4 + [vmem] * 4,
        out_specs=(vmem, smem, vmem),
        scratch_shapes=[pltpu.VMEM((512, NZC), F32), pltpu.VMEM((256, NZC), F32), pltpu.VMEM((8, ROW), F32)],
        cost_estimate=pl.CostEstimate(flops=400_000_000, bytes_accessed=2_000_000, transcendentals=0),
        compiler_params=LIMIT,
        interpret=INTERPRET,
        name="prepare",
    )(where, position, mixing, corr, din, sine, inverse, onto)


def share_kernel(rows_ref, green_ref, over_x_ref, over_y_ref, edge_ref, out_ref, turn_ref, line_ref):
    modes = over_x_ref[0] * rows_ref[0:1]
    for x in range(1, CG):
        modes = modes + over_x_ref[x] * rows_ref[x : x + 1]
    cells = jnp.zeros((8, 256), F32)
    for ky in range(CG):
        acc = jnp.zeros((8, 256), F32)
        for j in range(8):
            at = ky * 8 + j
            acc = acc + jnp.broadcast_to(modes[:, at : at + 1], (8, 256)) * green_ref[8 * at : 8 * at + 8]
        cells = cells + over_y_ref[ky] * jnp.sum(acc, axis=0, keepdims=True)
    turn_ref[...] = jnp.concatenate([cells, jnp.zeros((120, 256), F32)], 0).T
    line_ref[...] = jnp.zeros_like(line_ref)
    for j in range(CZ):
        line_ref[:, 8 * j : 8 * j + 8] = turn_ref[pl.ds(j, DOMS, stride=8), :][:, :8]
    head = lax.broadcasted_iota(jnp.int32, (8, 128), 0) == 0
    edge = edge_ref[...]
    for d in range(DOMS):
        out_ref[d] = jnp.where(head, line_ref[d : d + 1], edge)


def hartree_shares(rows, green, over_x, over_y, edges):
    return pl.pallas_call(
        share_kernel,
        out_shape=jax.ShapeDtypeStruct((DOMS, 8, 128), F32),
        scratch_shapes=[pltpu.VMEM((256, 128), F32), pltpu.VMEM((DOMS, 128), F32)],
        compiler_params=LIMIT,
        interpret=INTERPRET,
        name="share",
    )(rows, green, over_x, over_y, edges)


def final_kernel(side_ref, msg_ref, own_ref, vec_ref, dens_ref, hart_ref):
    total = msg_ref[0]
    for d in range(1, DOMS):
        total = total + msg_ref[d]
    for j in range(CZ):
        hart_ref[j] = total[0:1, 8 * j : 8 * j + 8]
    lane = lax.broadcasted_iota(jnp.int32, (8, ROW), 1)

    def rows(tile):
        spread = [jnp.broadcast_to(tile[t + 1 : t + 2], (8, 128)) for t in range(7)]
        front = jnp.concatenate(spread[:5], 1)
        back = jnp.concatenate(spread[4:] + spread[5:], 1)
        return front, rolled(back, -64)

    left0, left2 = rows(msg_ref[side_ref[0]])
    right0, right2 = rows(msg_ref[side_ref[1]])
    far = G - BUFFER
    left_last = jnp.where(lane < HALF_ROW, rolled(left2, -far), rolled(left2, HALF_ROW + 12 - far))
    right_last = jnp.where(lane < HALF_ROW, rolled(right2, far), rolled(right2, HALF_ROW - 12 + far))
    left_part = (rolled(left0, -far), rolled(left0, -6), left_last)
    right_part = (rolled(right0, far), rolled(right0, 6), right_last)
    for p in range(PLANES):
        mixed = own_ref[p] + vec_ref[5:6] * left_part[p][0:1] + vec_ref[6:7] * right_part[p][0:1]
        dens_ref[p] = mixed[:, :GG]


def final_parts(sides, msg, own, vectors):
    smem = pl.BlockSpec(memory_space=pltpu.SMEM)
    vmem = pl.BlockSpec(memory_space=pltpu.VMEM)
    return pl.pallas_call(
        final_kernel,
        out_shape=(
            jax.ShapeDtypeStruct((PLANES, 1, GG), F32),
            jax.ShapeDtypeStruct((CZ, 1, CG), F32),
        ),
        in_specs=[smem, vmem, vmem, vmem],
        out_specs=(vmem, vmem),
        compiler_params=LIMIT,
        interpret=INTERPRET,
        name="final",
    )(sides, msg, own, vectors)


def exchanged(x, axis):
    return lax.all_to_all(x, axis, split_axis=0, concat_axis=0, tiled=True)


def body(orbitals, potential, density_in, occupation, position, mixing, correlation_weight):
    sine, inverse, onto, gather, over_x, over_y = tables()
    shares = exchanged(filtered_shares(orbitals[0], potential[0]), "band")
    flat = shares.reshape(NB, SHARE)
    where = jnp.stack([lax.axis_index("dom"), lax.axis_index("band")]).astype(jnp.int32)
    din = jnp.transpose(density_in, (1, 0, 2))
    vectors, sides, green = prepared(where, position, mixing, correlation_weight, din, sine, inverse, onto)
    grams = exchanged(packed_grams(flat), "band")
    poly, fresh, coarse = density_rows(grams, flat, occupation.reshape(NB, 1), vectors, gather)
    rows = exchanged(coarse, "band")
    points, own, edges = output_parts(poly, flat, fresh, vectors)
    msg = exchanged(hartree_shares(rows, green, over_x, over_y, edges), "dom")
    dens, hart = final_parts(sides, msg, own, vectors)
    orbitals_out = jnp.transpose(points.reshape(PLANES, GG, NB), (2, 0, 1)).reshape(1, NB, PLANES, GG)
    density = jnp.transpose(dens, (1, 0, 2))
    hartree = jnp.transpose(hart, (1, 2, 0)).reshape(1, 1, CG, CZ)
    return orbitals_out, density, hartree


def solution(mesh):
    return jax.shard_map(
        body,
        mesh=mesh,
        in_specs=(
            P("dom", "band", None, None),
            P("dom", None, None),
            P("dom", "band", None),
            P(),
            P(),
            P(),
            P(),
        ),
        out_specs=(
            P("dom", None, "band", None),
            P("dom", "band", None),
            P("dom", "band", None, None),
        ),
        check_vma=False,
    )
```

```python
import functools
import numpy as np
import jax
import jax.numpy as jnp
from jax import lax
from jax.experimental import pallas as pl
from jax.experimental.pallas import tpu as pltpu
from jax.sharding import PartitionSpec as P

NB = 128
G = 24
GG = G * G
BUFFER = 6
CG = 8
CZ = 6
NZC = 192
DOMS = 32
BANDS = 8
LOCAL = NB // BANDS
PLANES = G // BANDS
ROW = 640
SHARE = 1792
PACKED = 72
HALF_ROW = GG // 2
EDGE = GG + HALF_ROW
POINTS = float(G * G * G)
FILTER_LOW = 1.0
FILTER_HIGH = 9.5
CENTER = 0.5 * (FILTER_HIGH + FILTER_LOW)
HALF = 0.5 * (FILTER_HIGH - FILTER_LOW)
HIGHEST = lax.Precision.HIGHEST
F32 = jnp.float32
INTERPRET = False
FILTER_LIMIT = pltpu.CompilerParams(vmem_limit_bytes=55_250_000)
LIMIT = pltpu.CompilerParams(vmem_limit_bytes=16 << 20)


def tables():
    k = np.arange(CG)
    cosine = np.sqrt(2.0 / CG) * np.cos(np.pi * k[:, None] * (k[None, :] + 0.5) / CG)
    cosine[0] *= np.sqrt(0.5)
    r = np.arange(NZC)
    sine = np.zeros((NZC + 8, NZC))
    sine[:NZC] = np.sqrt(2.0 / (NZC + 1)) * np.sin(np.pi * (r[:, None] + 1) * (r[None, :] + 1) / (NZC + 1))
    level_xy = 4.0 * np.sin(0.5 * np.pi * k / CG) ** 2
    level_z = 4.0 * np.sin(0.5 * np.pi * (r + 1) / (NZC + 1)) ** 2
    inverse = 1.0 / (level_xy[:, None, None] + level_xy[None, :, None] + level_z[None, None, :])
    scale = 8.0 / float(NZC * NZC)
    onto_x = np.broadcast_to((scale * cosine.T)[:, :, None], (CG, CG, NZC))
    lane = np.arange(GG)
    gather = np.zeros((ROW, 256))
    for ky in range(CG):
        gather[lane, ky * G + lane % G] = cosine[ky, (lane // G) // 3]
    over_x = np.broadcast_to(cosine.T[:, :, None], (CG, CG, 256))
    over_y = np.broadcast_to(cosine[:, :, None], (CG, CG, 256))
    sine = np.stack([sine[CZ * place : CZ * place + 8] for place in range(DOMS)])
    as_f32 = lambda a: np.ascontiguousarray(a, dtype=np.float32)
    return tuple(as_f32(a) for a in (sine, inverse.reshape(CG * CG, NZC), onto_x, gather, over_x, over_y))


def halves(x):
    high = x.astype(jnp.bfloat16)
    return high, (x - high.astype(F32)).astype(jnp.bfloat16)


def dot3(x, y, dims=(((1,), (0,)), ((), ()))):
    x_high, x_low = halves(x)
    y_high, y_low = halves(y)
    dot = functools.partial(lax.dot_general, dimension_numbers=dims, preferred_element_type=F32)
    return dot(x_high, y_high) + (dot(x_high, y_low) + dot(x_low, y_high))


def rolled(x, shift):
    return pltpu.roll(x, shift % ROW, 1)


def lane_index(shape):
    lane = lax.broadcasted_iota(jnp.int32, shape, 1).astype(F32)
    return lane, lane - G * jnp.floor((lane + 0.5) * (1.0 / G))


def neighbour_matrix(mat_ref):
    mat_ref[...] = jnp.zeros_like(mat_ref)
    for t in range(ROW // 128):
        top, end = max(0, 128 * t - 32), min(ROW, 128 * t + 160)
        shape = (end - top, 128)
        row = lax.broadcasted_iota(jnp.int32, shape, 0) + top
        col = lax.broadcasted_iota(jnp.int32, (8, 128), 1) + 128 * t
        _, z = lane_index((8, ROW))
        z = z[:, 128 * t : 128 * (t + 1)]
        before = jnp.where(z > 0.5, col - 1, -ROW)[0:1]
        after = jnp.where(z < G - 1.5, col + 1, -ROW)[0:1]
        col = col[0:1]
        hit = (row == before) | (row == after) | (row == col - G) | (row == col + G)
        hit = hit & (row < GG) & (col < GG)
        mat_ref[top:end, 128 * t : 128 * (t + 1)] = jnp.where(hit, 1.0, 0.0).astype(jnp.bfloat16)


def filter_kernel(orb_ref, pot_ref, out_ref, in_ref, pot_in, mat_ref, zero_ref, first_ref, side_ref, diag_ref, sems):
    copies = [pltpu.make_async_copy(pot_ref, pot_in, sems.at[3])]
    for c in range(3):
        part = pl.ds(8 * c, 8)
        copies.append(pltpu.make_async_copy(orb_ref.at[:, part, :], in_ref.at[c], sems.at[c]))
    for copy in copies:
        copy.start()
    neighbour_matrix(mat_ref)
    lane = lax.broadcasted_iota(jnp.int32, (1, ROW), 1)
    step = jnp.where(lane < GG, 0.5 / HALF, 0.0)
    diag_ref[:, GG - 64 :] = jnp.zeros((G, 128), F32)
    zero_ref[:, :, GG - 64 :] = jnp.zeros((G, LOCAL, 128), F32)
    copies[0].wait()
    diag_ref[:, :GG] = (pot_in[...] + (3.0 - CENTER)) * (1.0 / HALF)
    dot = functools.partial(jnp.dot, preferred_element_type=F32)

    def sum_sides(source, c):
        high, low = halves(source[8 * c : 8 * c + 8].reshape(8 * LOCAL, ROW))
        stack = jnp.concatenate([high, low], 0)
        for rows, cols in ((slice(0, 384), slice(0, 256)), (slice(128, 640), slice(256, 512)), (slice(384, 640), slice(512, 640))):
            both = dot(stack[:, rows], mat_ref[rows, cols])
            side = both[: 8 * LOCAL] + both[8 * LOCAL :]
            side_ref[8 * c : 8 * c + 8, :, cols] = side.reshape(8, LOCAL, cols.stop - cols.start)

    def applied(source, x):
        v = source[x]
        near = side_ref[x]
        if x > 0:
            near = near + source[x - 1]
        if x + 1 < G:
            near = near + source[x + 1]
        return diag_ref[x : x + 1] * v - step * near

    for c in range(3):
        copies[c + 1].wait()
        for x in range(8 * c, 8 * c + 8):
            zero_ref[x, :, :GG] = in_ref[c, :, x - 8 * c, :]
        sum_sides(zero_ref, c)
    for x in range(G):
        first_ref[x] = applied(zero_ref, x)
    for c in range(3):
        sum_sides(first_ref, c)
    for x in range(G):
        second = 2.0 * applied(first_ref, x) - zero_ref[x]
        p = x % PLANES
        out_ref[x // PLANES, :, p * GG : (p + 1) * GG] = second[:, :GG]
        if p == PLANES - 1:
            out_ref[x // PLANES, :, PLANES * GG :] = jnp.zeros((LOCAL, SHARE - PLANES * GG), F32)


def filtered_shares(orbitals, potential):
    return pl.pallas_call(
        filter_kernel,
        out_shape=jax.ShapeDtypeStruct((BANDS, LOCAL, SHARE), F32),
        in_specs=[pl.BlockSpec(memory_space=pltpu.HBM)] * 2,
        out_specs=pl.BlockSpec(memory_space=pltpu.VMEM),
        scratch_shapes=[
            pltpu.VMEM((3, LOCAL, 8, GG), F32),
            pltpu.VMEM((G, GG), F32),
            pltpu.VMEM((ROW, ROW), jnp.bfloat16),
            pltpu.VMEM((G, LOCAL, ROW), F32),
            pltpu.VMEM((G, LOCAL, ROW), F32),
            pltpu.VMEM((G, LOCAL, ROW), F32),
            pltpu.VMEM((G, ROW), F32),
            pltpu.SemaphoreType.DMA((4,)),
        ],
        compiler_params=FILTER_LIMIT,
        interpret=INTERPRET,
        name="filter",
    )(orbitals, potential)


def gram_kernel(f_ref, out_ref):
    high, low = halves(f_ref[...])
    both = lax.dot_general(
        high, jnp.concatenate([high, low], 0), (((1,), (1,)), ((), ())), preferred_element_type=F32
    )
    cross = both[:, NB:]
    raw = both[:, :NB] + (cross + cross.T)
    row = lax.broadcasted_iota(jnp.int32, (64, NB), 0)
    col = lax.broadcasted_iota(jnp.int32, (64, NB), 1)
    lower = pltpu.roll(raw[64:], 64, 1)
    packed = jnp.where(col >= row, raw[:64], lower)
    diag = jnp.sum(jnp.where(col == row + 64, raw[64:], 0.0), axis=0, keepdims=True)
    diag = jnp.broadcast_to(diag, (8, NB))
    for k in range(BANDS):
        out_ref[k, :64] = packed
        out_ref[k, 64:] = diag


def packed_grams(flat):
    return pl.pallas_call(
        gram_kernel,
        out_shape=jax.ShapeDtypeStruct((BANDS, PACKED, NB), F32),
        compiler_params=LIMIT,
        interpret=INTERPRET,
        name="gram",
    )(flat)


def density_kernel(g_ref, f_ref, occ_ref, din_ref, gather_ref, poly_ref, fresh_ref, coarse_ref, rows_ref):
    total = g_ref[0]
    for k in range(1, BANDS):
        total = total + g_ref[k]
    packed = total[:64]
    row = lax.broadcasted_iota(jnp.int32, (64, NB), 0)
    col = lax.broadcasted_iota(jnp.int32, (64, NB), 1)
    top = jnp.where(col > row, packed, jnp.where(col == row, 0.5 * packed, 0.0))
    low = pltpu.roll(jnp.where(col < row, packed, 0.0), 64, 1)
    low = low + jnp.where(col == row + 64, 0.5 * total[64:65], 0.0)
    half = jnp.concatenate([top, low], 0)
    raw = half + half.T
    norm = jnp.sqrt(jnp.sum(jnp.sum(raw * raw, axis=0, keepdims=True), axis=1, keepdims=True))
    a = raw / norm
    scaling = jnp.sqrt(POINTS / norm)
    eye = jnp.where(
        lax.broadcasted_iota(jnp.int32, (NB, NB), 0) == lax.broadcasted_iota(jnp.int32, (NB, NB), 1), 1.0, 0.0
    )
    square = dot3(a, a)
    tail = dot3(square, 0.0625 * square - 0.5625 * a)
    poly = scaling * (2.25 * eye + (1.6875 * square - 2.4375 * a) + tail)
    poly_ref[...] = poly
    poly_high, poly_low = halves(poly)
    both = jnp.concatenate([poly_high, poly_low], 1)
    dot = functools.partial(jnp.dot, preferred_element_type=F32)
    weight = jnp.sum(eye * (occ_ref[...] * (1.0 / NB)), axis=1, keepdims=True)
    weight = jnp.broadcast_to(weight, (NB, 256))
    for c in range(SHARE // 256):
        cols = slice(256 * c, 256 * (c + 1))
        high, low = halves(f_ref[:, cols])
        current = dot(both, jnp.concatenate([high, high], 0)) + dot(poly_high, low)
        line = jnp.sum(current * current * weight, axis=0, keepdims=True)
        fresh_ref[:, cols] = jnp.broadcast_to(line, (8, 256))
    planes = fresh_ref[:, :ROW] + fresh_ref[:, GG : GG + ROW] + fresh_ref[:, 2 * GG : 2 * GG + ROW]
    rows_ref[...] = jnp.zeros_like(rows_ref)
    rows_ref[0:8, :GG] = planes[:, :GG]
    rows_ref[8:9, :GG] = din_ref[0] + din_ref[1] + din_ref[2]
    cells = dot3(rows_ref[...], gather_ref[...])
    row = lax.broadcasted_iota(jnp.int32, (8, NB), 0)
    inputs = jnp.broadcast_to(cells[8:9], (8, 256))
    tile = jnp.where(row == 0, cells[:8, :128], cells[:8, 128:])
    tile = jnp.where(row == 2, inputs[:, :128], jnp.where(row == 3, inputs[:, 128:], tile))
    for k in range(BANDS):
        coarse_ref[k] = tile


def density_rows(grams, flat, occupation, din, gather):
    return pl.pallas_call(
        density_kernel,
        out_shape=(
            jax.ShapeDtypeStruct((NB, NB), F32),
            jax.ShapeDtypeStruct((8, SHARE), F32),
            jax.ShapeDtypeStruct((BANDS, 8, 128), F32),
        ),
        scratch_shapes=[pltpu.VMEM((16, ROW), F32)],
        compiler_params=LIMIT,
        interpret=INTERPRET,
        name="density",
    )(grams, flat, occupation, din, gather)


def output_kernel(
    pos_ref, mix_ref, corr_ref, poly_ref, f_ref, fresh_ref, din_ref, sine_ref, inverse_ref, onto_ref,
    out_ref, own_ref, edge_ref, vec_ref, side_ref, green_ref, left_ref, right_ref,
):
    poly_high, poly_low = halves(poly_ref[...])
    dot = functools.partial(jnp.dot, preferred_element_type=F32)
    for c in range(SHARE // 128):
        turned = f_ref[:, 128 * c : 128 * (c + 1)].T
        high, low = halves(turned)
        value = dot(high, poly_high) + (dot(high, poly_low) + dot(low, poly_high))
        count = min(128, PLANES * GG - 128 * c)
        out_ref[128 * c : 128 * c + count] = value[:count]

    if INTERPRET:
        dom, band = pos_ref[DOMS], pos_ref[DOMS + 1]
    else:
        dom, band = lax.axis_index("dom"), lax.axis_index("band")
    own = pos_ref[dom]
    lane, z = lane_index((8, ROW))
    corr = jnp.zeros((8, ROW), F32)
    for j in range(BUFFER):
        here = (jnp.abs(z - j) < 0.5) | (jnp.abs(z - (G - BUFFER + j)) < 0.5)
        corr = jnp.where(here, corr_ref[j].astype(F32), corr)
    corr = corr * (1.0 / 16.0)
    fresh_weight = jnp.full((8, ROW), mix_ref[0].astype(F32))
    input_weight = jnp.full((8, ROW), mix_ref[1].astype(F32))
    both = fresh_weight + input_weight
    fresh_weight = fresh_weight / both
    input_weight = input_weight / both
    has_left = jnp.where(jnp.full((8, ROW), own) > 0, 1.0, 0.0)
    has_right = jnp.where(jnp.full((8, ROW), own) < DOMS - 1, 1.0, 0.0)
    low_z = z < BUFFER - 0.5
    high_z = z > G - BUFFER - 0.5
    middle = (z > BUFFER - 0.5) & (z < G - BUFFER - 0.5)
    from_left = jnp.where(low_z, corr * has_left, 0.0)
    from_right = jnp.where(high_z, (1.0 - corr) * has_right, 0.0)
    keep = 1.0 - from_left - from_right
    cell = 1.0 / 27.0
    vec_ref[0:1] = (cell * fresh_weight * jnp.where(high_z, corr * has_right, keep))[0:1]
    vec_ref[1:2] = jnp.where(high_z, 0.0, cell * input_weight)[0:1]
    vec_ref[2:3] = (fresh_weight * from_left)[0:1]
    vec_ref[3:4] = (fresh_weight * from_right)[0:1]

    low_edge = low_z & (lane < GG)
    high_edge = high_z & (lane < GG)
    edges = []
    for p in range(PLANES):
        plane = fresh_ref[:, p * GG : p * GG + ROW]
        own_ref[p] = (fresh_weight * keep * plane)[0:1, :GG] + input_weight[0:1, :GG] * din_ref[p]
        edges.append((jnp.where(low_edge, plane, 0.0), jnp.where(high_edge, plane, 0.0)))
    first = (edges[0][0] + edges[0][1]) + (rolled(edges[1][0], 12) + rolled(edges[1][1], -12))
    last = edges[2][0] + edges[2][1]
    moved = rolled(edges[2][0], 12 - HALF_ROW) + rolled(edges[2][1], -12 - HALF_ROW)
    last = jnp.where(lane < HALF_ROW, jnp.where(middle, moved, last), 0.0)
    first = first + rolled(jnp.where(lane < 64, last, 0.0), GG)
    rest = rolled(last, -64)
    edge_ref[0:1] = jnp.zeros((1, 128), F32)
    for t in range(7):
        source, at = (first, 128 * t) if t < 5 else (rest, 128 * (t - 5))
        edge_ref[t + 1 : t + 2] = source[0:1, at : at + 128]

    left, right = jnp.int32(0), jnp.int32(0)
    for d in range(DOMS):
        left = jnp.where(pos_ref[d] == own - 1, d, left)
        right = jnp.where(pos_ref[d] == own + 1, d, right)
        right_ref[8 * d : 8 * d + 8] = sine_ref[pos_ref[d]]
    side_ref[0] = left
    side_ref[1] = right
    mine = sine_ref[own]
    onto = onto_ref[band]
    for ky in range(CG):
        part = inverse_ref[8 * ky : 8 * ky + 8] * onto
        for j in range(8):
            at = ky * 64 + j * 8
            left_ref[at : at + 8] = part * mine[j : j + 1]
    green_ref[...] = dot3(left_ref[...], right_ref[...], (((1,), (1,)), ((), ())))


def output_parts(position, mixing, corr, poly, flat, fresh, din, sine, inverse, onto):
    if INTERPRET:
        position = jnp.append(position, jnp.stack([lax.axis_index("dom"), lax.axis_index("band")]))
    smem = pl.BlockSpec(memory_space=pltpu.SMEM)
    vmem = pl.BlockSpec(memory_space=pltpu.VMEM)
    return pl.pallas_call(
        output_kernel,
        out_shape=(
            jax.ShapeDtypeStruct((PLANES * GG, NB), F32),
            jax.ShapeDtypeStruct((PLANES, 1, GG), F32),
            jax.ShapeDtypeStruct((8, 128), F32),
            jax.ShapeDtypeStruct((8, ROW), F32),
            jax.ShapeDtypeStruct((2,), jnp.int32),
            jax.ShapeDtypeStruct((512, 256), F32),
        ),
        in_specs=[smem] * 3 + [vmem] * 7,
        out_specs=(vmem, vmem, vmem, vmem, smem, vmem),
        scratch_shapes=[pltpu.VMEM((512, NZC), F32), pltpu.VMEM((256, NZC), F32)],
        cost_estimate=pl.CostEstimate(flops=500_000_000, bytes_accessed=4_000_000, transcendentals=0),
        compiler_params=LIMIT,
        interpret=INTERPRET,
        name="output",
    )(position, mixing, corr, poly, flat, fresh, din, sine, inverse, onto)


def share_kernel(rows_ref, vec_ref, green_ref, over_x_ref, over_y_ref, edge_ref, out_ref, turn_ref, line_ref):
    fresh = jnp.concatenate([rows_ref[:, 0, :], rows_ref[:, 1, :]], 1)
    inputs = jnp.concatenate([rows_ref[:, 2, :], rows_ref[:, 3, :]], 1)
    cells = fresh * vec_ref[0:1, :256] + inputs * vec_ref[1:2, :256]
    cells = cells + (pltpu.roll(cells, 255, 1) + pltpu.roll(cells, 254, 1))
    modes = over_x_ref[0] * cells[0:1]
    for x in range(1, CG):
        modes = modes + over_x_ref[x] * cells[x : x + 1]
    cells = jnp.zeros((8, 256), F32)
    for ky in range(CG):
        acc = jnp.zeros((8, 256), F32)
        for j in range(8):
            at = ky * 8 + j
            acc = acc + jnp.broadcast_to(modes[:, G * ky + 3 * j : G * ky + 3 * j + 1], (8, 256)) * green_ref[8 * at : 8 * at + 8]
        cells = cells + over_y_ref[ky] * jnp.sum(acc, axis=0, keepdims=True)
    turn_ref[...] = jnp.concatenate([cells, jnp.zeros((120, 256), F32)], 0).T
    line_ref[...] = jnp.zeros_like(line_ref)
    for j in range(CZ):
        line_ref[:, 8 * j : 8 * j + 8] = turn_ref[pl.ds(j, DOMS, stride=8), :][:, :8]
    head = lax.broadcasted_iota(jnp.int32, (8, 128), 0) == 0
    edge = edge_ref[...]
    for d in range(DOMS):
        out_ref[d] = jnp.where(head, line_ref[d : d + 1], edge)


def hartree_shares(rows, vectors, green, over_x, over_y, edges):
    return pl.pallas_call(
        share_kernel,
        out_shape=jax.ShapeDtypeStruct((DOMS, 8, 128), F32),
        scratch_shapes=[pltpu.VMEM((256, 128), F32), pltpu.VMEM((DOMS, 128), F32)],
        compiler_params=LIMIT,
        interpret=INTERPRET,
        name="share",
    )(rows, vectors, green, over_x, over_y, edges)


def final_kernel(side_ref, msg_ref, own_ref, vec_ref, dens_ref, hart_ref):
    total = msg_ref[0]
    for d in range(1, DOMS):
        total = total + msg_ref[d]
    for j in range(CZ):
        hart_ref[j] = total[0:1, 8 * j : 8 * j + 8]
    lane = lax.broadcasted_iota(jnp.int32, (8, ROW), 1)

    def rows(tile):
        spread = [jnp.broadcast_to(tile[t + 1 : t + 2], (8, 128)) for t in range(7)]
        front = jnp.concatenate(spread[:5], 1)
        back = jnp.concatenate(spread[4:] + spread[5:], 1)
        return front, rolled(back, -64)

    left0, left2 = rows(msg_ref[side_ref[0]])
    right0, right2 = rows(msg_ref[side_ref[1]])
    far = G - BUFFER
    left_last = jnp.where(lane < HALF_ROW, rolled(left2, -far), rolled(left2, HALF_ROW + 12 - far))
    right_last = jnp.where(lane < HALF_ROW, rolled(right2, far), rolled(right2, HALF_ROW - 12 + far))
    left_part = (rolled(left0, -far), rolled(left0, -6), left_last)
    right_part = (rolled(right0, far), rolled(right0, 6), right_last)
    for p in range(PLANES):
        mixed = own_ref[p] + vec_ref[2:3, :GG] * left_part[p][0:1, :GG]
        dens_ref[p] = mixed + vec_ref[3:4, :GG] * right_part[p][0:1, :GG]


def final_parts(sides, msg, own, vectors):
    smem = pl.BlockSpec(memory_space=pltpu.SMEM)
    vmem = pl.BlockSpec(memory_space=pltpu.VMEM)
    return pl.pallas_call(
        final_kernel,
        out_shape=(
            jax.ShapeDtypeStruct((PLANES, 1, GG), F32),
            jax.ShapeDtypeStruct((CZ, 1, CG), F32),
        ),
        in_specs=[smem, vmem, vmem, vmem],
        out_specs=(vmem, vmem),
        compiler_params=LIMIT,
        interpret=INTERPRET,
        name="final",
    )(sides, msg, own, vectors)


def exchanged(x, axis):
    return lax.all_to_all(x, axis, split_axis=0, concat_axis=0, tiled=True)


def body(orbitals, potential, density_in, occupation, position, mixing, correlation_weight):
    sine, inverse, onto, gather, over_x, over_y = tables()
    shares = exchanged(filtered_shares(orbitals[0], potential[0]), "band")
    flat = shares.reshape(NB, SHARE)
    din = jnp.transpose(density_in, (1, 0, 2))
    grams = exchanged(packed_grams(flat), "band")
    poly, fresh, coarse = density_rows(grams, flat, occupation.reshape(1, NB), din, gather)
    rows = exchanged(coarse, "band")
    points, own, edges, vectors, sides, green = output_parts(
        position, mixing, correlation_weight, poly, flat, fresh, din, sine, inverse, onto
    )
    msg = exchanged(hartree_shares(rows, vectors, green, over_x, over_y, edges), "dom")
    dens, hart = final_parts(sides, msg, own, vectors)
    orbitals_out = jnp.transpose(points.reshape(PLANES, GG, NB), (2, 0, 1)).reshape(1, NB, PLANES, GG)
    density = jnp.transpose(dens, (1, 0, 2))
    hartree = jnp.transpose(hart, (1, 2, 0)).reshape(1, 1, CG, CZ)
    return orbitals_out, density, hartree


def solution(mesh):
    return jax.shard_map(
        body,
        mesh=mesh,
        in_specs=(
            P("dom", "band", None, None),
            P("dom", None, None),
            P("dom", "band", None),
            P(),
            P(),
            P(),
            P(),
        ),
        out_specs=(
            P("dom", None, "band", None),
            P("dom", "band", None),
            P("dom", "band", None, None),
        ),
        check_vma=False,
    )
```

```python
import functools
import numpy as np
import jax
import jax.numpy as jnp
from jax import lax
from jax.experimental import pallas as pl
from jax.experimental.pallas import tpu as pltpu
from jax.sharding import PartitionSpec as P

NB = 128
G = 24
GG = G * G
BUFFER = 6
CG = 8
CZ = 6
NZC = 192
DOMS = 32
BANDS = 8
LOCAL = NB // BANDS
PLANES = G // BANDS
ROW = 640
SHARE = 1792
PACKED = 72
HALF_ROW = GG // 2
EDGE = GG + HALF_ROW
POINTS = float(G * G * G)
FILTER_LOW = 1.0
FILTER_HIGH = 9.5
CENTER = 0.5 * (FILTER_HIGH + FILTER_LOW)
HALF = 0.5 * (FILTER_HIGH - FILTER_LOW)
HIGHEST = lax.Precision.HIGHEST
F32 = jnp.float32
INTERPRET = False
LIMIT = pltpu.CompilerParams(vmem_limit_bytes=16 << 20)


def tables():
    k = np.arange(CG)
    cosine = np.sqrt(2.0 / CG) * np.cos(np.pi * k[:, None] * (k[None, :] + 0.5) / CG)
    cosine[0] *= np.sqrt(0.5)
    r = np.arange(NZC)
    sine = np.zeros((NZC + 8, NZC))
    sine[:NZC] = np.sqrt(2.0 / (NZC + 1)) * np.sin(np.pi * (r[:, None] + 1) * (r[None, :] + 1) / (NZC + 1))
    level_xy = 4.0 * np.sin(0.5 * np.pi * k / CG) ** 2
    level_z = 4.0 * np.sin(0.5 * np.pi * (r + 1) / (NZC + 1)) ** 2
    inverse = 1.0 / (level_xy[:, None, None] + level_xy[None, :, None] + level_z[None, None, :])
    scale = 8.0 / float(NZC * NZC)
    onto_x = np.broadcast_to((scale * cosine.T)[:, :, None], (CG, CG, NZC))
    lane = np.arange(GG)
    gather = np.zeros((ROW, 256))
    for ky in range(CG):
        gather[lane, ky * G + lane % G] = cosine[ky, (lane // G) // 3]
    over_x = np.broadcast_to(cosine.T[:, :, None], (CG, CG, 256))
    over_y = np.broadcast_to(cosine[:, :, None], (CG, CG, 256))
    sine = np.stack([sine[CZ * place : CZ * place + 8] for place in range(DOMS)])
    as_f32 = lambda a: np.ascontiguousarray(a, dtype=np.float32)
    return tuple(as_f32(a) for a in (sine, inverse.reshape(CG * CG, NZC), onto_x, gather, over_x, over_y))


def halves(x):
    high = x.astype(jnp.bfloat16)
    return high, (x - high.astype(F32)).astype(jnp.bfloat16)


def dot3(x, y, dims=(((1,), (0,)), ((), ()))):
    x_high, x_low = halves(x)
    y_high, y_low = halves(y)
    dot = functools.partial(lax.dot_general, dimension_numbers=dims, preferred_element_type=F32)
    return dot(x_high, y_high) + (dot(x_high, y_low) + dot(x_low, y_high))


def rolled(x, shift):
    return pltpu.roll(x, shift % ROW, 1)


def lane_index(shape):
    lane = lax.broadcasted_iota(jnp.int32, shape, 1).astype(F32)
    return lane, lane - G * jnp.floor((lane + 0.5) * (1.0 / G))


def neighbour_matrix(mat_ref):
    mat_ref[...] = jnp.zeros_like(mat_ref)
    for t in range(ROW // 128):
        top, end = max(0, 128 * t - 32), min(ROW, 128 * t + 160)
        shape = (end - top, 128)
        row = lax.broadcasted_iota(jnp.int32, shape, 0) + top
        col = lax.broadcasted_iota(jnp.int32, (8, 128), 1) + 128 * t
        _, z = lane_index((8, ROW))
        z = z[:, 128 * t : 128 * (t + 1)]
        before = jnp.where(z > 0.5, col - 1, -ROW)[0:1]
        after = jnp.where(z < G - 1.5, col + 1, -ROW)[0:1]
        col = col[0:1]
        hit = (row == before) | (row == after) | (row == col - G) | (row == col + G)
        hit = hit & (row < GG) & (col < GG)
        mat_ref[top:end, 128 * t : 128 * (t + 1)] = jnp.where(hit, 1.0, 0.0).astype(jnp.bfloat16)


def filter_kernel(orb_ref, pot_ref, mat_ref, occ_ref, out_ref, weight_ref, zero_ref, first_ref, side_ref, diag_ref):
    eye = lax.broadcasted_iota(jnp.int32, (NB, NB), 0) == lax.broadcasted_iota(jnp.int32, (NB, NB), 1)
    weight = jnp.sum(jnp.where(eye, occ_ref[...] * (1.0 / NB), 0.0), axis=1, keepdims=True)
    weight_ref[...] = jnp.broadcast_to(weight, (NB, 256))
    diag_ref[:, GG - 64 :] = jnp.zeros((G, 128), F32)
    zero_ref[:, :, GG - 64 :] = jnp.zeros((G, LOCAL, 128), F32)
    diag_ref[:, :GG] = (pot_ref[...] + (3.0 - CENTER)) * 2.0
    dot = functools.partial(jnp.dot, preferred_element_type=F32)

    def sum_sides(source, c):
        high, low = halves(source[8 * c : 8 * c + 8].reshape(8 * LOCAL, ROW))
        stack = jnp.concatenate([high, low], 0)
        for rows, cols in ((slice(0, 384), slice(0, 256)), (slice(128, 640), slice(256, 512)), (slice(384, 640), slice(512, 640))):
            both = dot(stack[:, rows], mat_ref[rows, cols])
            side = both[: 8 * LOCAL] + both[8 * LOCAL :]
            side_ref[8 * c : 8 * c + 8, :, cols] = side.reshape(8, LOCAL, cols.stop - cols.start)

    def applied(source, x):
        v = source[x]
        near = side_ref[x]
        if x > 0:
            near = near + source[x - 1]
        if x + 1 < G:
            near = near + source[x + 1]
        return diag_ref[x : x + 1] * v - near

    for c in range(3):
        for x in range(8 * c, 8 * c + 8):
            zero_ref[x, :, :GG] = orb_ref[:, x, :]
        sum_sides(zero_ref, c)
    for x in range(G):
        first_ref[x] = applied(zero_ref, x)
    for c in range(3):
        sum_sides(first_ref, c)
    for x in range(G):
        second = (0.5 / HALF**2) * applied(first_ref, x) - zero_ref[x]
        p = x % PLANES
        out_ref[x // PLANES, :, p * GG : (p + 1) * GG] = second[:, :GG]
        if p == PLANES - 1:
            out_ref[x // PLANES, :, PLANES * GG :] = jnp.zeros((LOCAL, SHARE - PLANES * GG), F32)


def filtered_shares(orbitals, potential, occupation):
    matrix = pl.pallas_call(
        neighbour_matrix,
        out_shape=jax.ShapeDtypeStruct((ROW, ROW), jnp.bfloat16),
        cost_estimate=pl.CostEstimate(flops=20_000_000_000, bytes_accessed=4_000_000, transcendentals=0),
        compiler_params=LIMIT,
        interpret=INTERPRET,
        name="matrix",
    )()
    return pl.pallas_call(
        filter_kernel,
        out_shape=(
            jax.ShapeDtypeStruct((BANDS, LOCAL, SHARE), F32),
            jax.ShapeDtypeStruct((NB, 256), F32),
        ),
        scratch_shapes=[
            pltpu.VMEM((G, LOCAL, ROW), F32),
            pltpu.VMEM((G, LOCAL, ROW), F32),
            pltpu.VMEM((G, LOCAL, ROW), F32),
            pltpu.VMEM((G, ROW), F32),
        ],
        compiler_params=LIMIT,
        interpret=INTERPRET,
        name="filter",
    )(orbitals, potential, matrix, occupation)


def gram_kernel(f_ref, out_ref):
    high, low = halves(f_ref[...])
    both = lax.dot_general(
        high, jnp.concatenate([high, low], 0), (((1,), (1,)), ((), ())), preferred_element_type=F32
    )
    cross = both[:, NB:]
    raw = both[:, :NB] + (cross + cross.T)
    row = lax.broadcasted_iota(jnp.int32, (64, NB), 0)
    col = lax.broadcasted_iota(jnp.int32, (64, NB), 1)
    lower = pltpu.roll(raw[64:], 64, 1)
    packed = jnp.where(col >= row, raw[:64], lower)
    diag = jnp.sum(jnp.where(col == row + 64, raw[64:], 0.0), axis=0, keepdims=True)
    diag = jnp.broadcast_to(diag, (8, NB))
    for k in range(BANDS):
        out_ref[k, :64] = packed
        out_ref[k, 64:] = diag


def packed_grams(flat):
    return pl.pallas_call(
        gram_kernel,
        out_shape=jax.ShapeDtypeStruct((BANDS, PACKED, NB), F32),
        compiler_params=LIMIT,
        interpret=INTERPRET,
        name="gram",
    )(flat)


def density_kernel(g_ref, f_ref, weight_ref, din_ref, gather_ref, poly_ref, fresh_ref, coarse_ref, rows_ref):
    total = g_ref[0]
    for k in range(1, BANDS):
        total = total + g_ref[k]
    packed = total[:64]
    row = lax.broadcasted_iota(jnp.int32, (64, NB), 0)
    col = lax.broadcasted_iota(jnp.int32, (64, NB), 1)
    top = jnp.where(col > row, packed, jnp.where(col == row, 0.5 * packed, 0.0))
    low = pltpu.roll(jnp.where(col < row, packed, 0.0), 64, 1)
    low = low + jnp.where(col == row + 64, 0.5 * total[64:65], 0.0)
    half = jnp.concatenate([top, low], 0)
    raw = half + half.T
    norm = jnp.sqrt(jnp.sum(jnp.sum(raw * raw, axis=0, keepdims=True), axis=1, keepdims=True))
    a = raw / norm
    scaling = jnp.sqrt(POINTS / norm)
    eye = jnp.where(
        lax.broadcasted_iota(jnp.int32, (NB, NB), 0) == lax.broadcasted_iota(jnp.int32, (NB, NB), 1), 1.0, 0.0
    )
    square = dot3(a, a)
    tail = dot3(square, 0.0625 * square - 0.5625 * a)
    poly = scaling * (2.25 * eye + (1.6875 * square - 2.4375 * a) + tail)
    poly_ref[...] = poly
    poly_high, poly_low = halves(poly)
    both = jnp.concatenate([poly_high, poly_low], 1)
    dot = functools.partial(jnp.dot, preferred_element_type=F32)
    for c in range(SHARE // 256):
        cols = slice(256 * c, 256 * (c + 1))
        high, low = halves(f_ref[:, cols])
        current = dot(both, jnp.concatenate([high, high], 0)) + dot(poly_high, low)
        line = jnp.sum(current * current * weight_ref[...], axis=0, keepdims=True)
        fresh_ref[:, cols] = jnp.broadcast_to(line, (8, 256))
    planes = fresh_ref[:, :ROW] + fresh_ref[:, GG : GG + ROW] + fresh_ref[:, 2 * GG : 2 * GG + ROW]
    rows_ref[...] = jnp.zeros_like(rows_ref)
    rows_ref[0:8, :GG] = planes[:, :GG]
    rows_ref[8:9, :GG] = din_ref[0] + din_ref[1] + din_ref[2]
    cells = dot3(rows_ref[...], gather_ref[...])
    row = lax.broadcasted_iota(jnp.int32, (8, NB), 0)
    inputs = jnp.broadcast_to(cells[8:9], (8, 256))
    tile = jnp.where(row == 0, cells[:8, :128], cells[:8, 128:])
    tile = jnp.where(row == 2, inputs[:, :128], jnp.where(row == 3, inputs[:, 128:], tile))
    for k in range(BANDS):
        coarse_ref[k] = tile


def density_rows(grams, flat, weight, din, gather):
    return pl.pallas_call(
        density_kernel,
        out_shape=(
            jax.ShapeDtypeStruct((NB, NB), F32),
            jax.ShapeDtypeStruct((8, SHARE), F32),
            jax.ShapeDtypeStruct((BANDS, 8, 128), F32),
        ),
        scratch_shapes=[pltpu.VMEM((16, ROW), F32)],
        compiler_params=LIMIT,
        interpret=INTERPRET,
        name="density",
    )(grams, flat, weight, din, gather)


def output_kernel(
    pos_ref, mix_ref, corr_ref, poly_ref, f_ref, fresh_ref, din_ref, sine_ref, inverse_ref, onto_ref,
    out_ref, own_ref, edge_ref, vec_ref, side_ref, green_ref, left_ref, right_ref,
):
    poly_high, poly_low = halves(poly_ref[...])
    dot = functools.partial(jnp.dot, preferred_element_type=F32)
    for c in range(SHARE // 128):
        turned = f_ref[:, 128 * c : 128 * (c + 1)].T
        high, low = halves(turned)
        value = dot(high, poly_high) + (dot(high, poly_low) + dot(low, poly_high))
        count = min(128, PLANES * GG - 128 * c)
        out_ref[128 * c : 128 * c + count] = value[:count]

    if INTERPRET:
        dom, band = pos_ref[DOMS], pos_ref[DOMS + 1]
    else:
        dom, band = lax.axis_index("dom"), lax.axis_index("band")
    own = pos_ref[dom]
    lane, z = lane_index((8, ROW))
    corr = jnp.zeros((8, ROW), F32)
    for j in range(BUFFER):
        here = (jnp.abs(z - j) < 0.5) | (jnp.abs(z - (G - BUFFER + j)) < 0.5)
        corr = jnp.where(here, corr_ref[j].astype(F32), corr)
    corr = corr * (1.0 / 16.0)
    fresh_weight = jnp.full((8, ROW), mix_ref[0].astype(F32))
    input_weight = jnp.full((8, ROW), mix_ref[1].astype(F32))
    both = fresh_weight + input_weight
    fresh_weight = fresh_weight / both
    input_weight = input_weight / both
    has_left = jnp.where(jnp.full((8, ROW), own) > 0, 1.0, 0.0)
    has_right = jnp.where(jnp.full((8, ROW), own) < DOMS - 1, 1.0, 0.0)
    low_z = z < BUFFER - 0.5
    high_z = z > G - BUFFER - 0.5
    middle = (z > BUFFER - 0.5) & (z < G - BUFFER - 0.5)
    from_left = jnp.where(low_z, corr * has_left, 0.0)
    from_right = jnp.where(high_z, (1.0 - corr) * has_right, 0.0)
    keep = 1.0 - from_left - from_right
    cell = 1.0 / 27.0
    vec_ref[0:1] = (cell * fresh_weight * jnp.where(high_z, corr * has_right, keep))[0:1]
    vec_ref[1:2] = jnp.where(high_z, 0.0, cell * input_weight)[0:1]
    vec_ref[2:3] = (fresh_weight * from_left)[0:1]
    vec_ref[3:4] = (fresh_weight * from_right)[0:1]

    low_edge = low_z & (lane < GG)
    high_edge = high_z & (lane < GG)
    edges = []
    for p in range(PLANES):
        plane = fresh_ref[:, p * GG : p * GG + ROW]
        own_ref[p] = (fresh_weight * keep * plane)[0:1, :GG] + input_weight[0:1, :GG] * din_ref[p]
        edges.append((jnp.where(low_edge, plane, 0.0), jnp.where(high_edge, plane, 0.0)))
    first = (edges[0][0] + edges[0][1]) + (rolled(edges[1][0], 12) + rolled(edges[1][1], -12))
    last = edges[2][0] + edges[2][1]
    moved = rolled(edges[2][0], 12 - HALF_ROW) + rolled(edges[2][1], -12 - HALF_ROW)
    last = jnp.where(lane < HALF_ROW, jnp.where(middle, moved, last), 0.0)
    first = first + rolled(jnp.where(lane < 64, last, 0.0), GG)
    rest = rolled(last, -64)
    edge_ref[0:1] = jnp.zeros((1, 128), F32)
    for t in range(7):
        source, at = (first, 128 * t) if t < 5 else (rest, 128 * (t - 5))
        edge_ref[t + 1 : t + 2] = source[0:1, at : at + 128]

    left, right = jnp.int32(0), jnp.int32(0)
    for d in range(DOMS):
        left = jnp.where(pos_ref[d] == own - 1, d, left)
        right = jnp.where(pos_ref[d] == own + 1, d, right)
        right_ref[8 * d : 8 * d + 8] = sine_ref[pos_ref[d]]
    side_ref[0] = left
    side_ref[1] = right
    mine = sine_ref[own]
    onto = onto_ref[band]
    for ky in range(CG):
        part = inverse_ref[8 * ky : 8 * ky + 8] * onto
        for j in range(8):
            at = ky * 64 + j * 8
            left_ref[at : at + 8] = part * mine[j : j + 1]
    green_ref[...] = dot3(left_ref[...], right_ref[...], (((1,), (1,)), ((), ())))


def output_parts(position, mixing, corr, poly, flat, fresh, din, sine, inverse, onto):
    if INTERPRET:
        position = jnp.append(position, jnp.stack([lax.axis_index("dom"), lax.axis_index("band")]))
    smem = pl.BlockSpec(memory_space=pltpu.SMEM)
    vmem = pl.BlockSpec(memory_space=pltpu.VMEM)
    return pl.pallas_call(
        output_kernel,
        out_shape=(
            jax.ShapeDtypeStruct((PLANES * GG, NB), F32),
            jax.ShapeDtypeStruct((PLANES, 1, GG), F32),
            jax.ShapeDtypeStruct((8, 128), F32),
            jax.ShapeDtypeStruct((8, ROW), F32),
            jax.ShapeDtypeStruct((2,), jnp.int32),
            jax.ShapeDtypeStruct((512, 256), F32),
        ),
        in_specs=[smem] * 3 + [vmem] * 7,
        out_specs=(vmem, vmem, vmem, vmem, smem, vmem),
        scratch_shapes=[pltpu.VMEM((512, NZC), F32), pltpu.VMEM((256, NZC), F32)],
        cost_estimate=pl.CostEstimate(flops=500_000_000, bytes_accessed=4_000_000, transcendentals=0),
        compiler_params=LIMIT,
        interpret=INTERPRET,
        name="output",
    )(position, mixing, corr, poly, flat, fresh, din, sine, inverse, onto)


def share_kernel(rows_ref, vec_ref, green_ref, over_x_ref, over_y_ref, edge_ref, out_ref, turn_ref, line_ref):
    fresh = jnp.concatenate([rows_ref[:, 0, :], rows_ref[:, 1, :]], 1)
    inputs = jnp.concatenate([rows_ref[:, 2, :], rows_ref[:, 3, :]], 1)
    cells = fresh * vec_ref[0:1, :256] + inputs * vec_ref[1:2, :256]
    cells = cells + (pltpu.roll(cells, 255, 1) + pltpu.roll(cells, 254, 1))
    modes = over_x_ref[0] * cells[0:1]
    for x in range(1, CG):
        modes = modes + over_x_ref[x] * cells[x : x + 1]
    cells = jnp.zeros((8, 256), F32)
    for ky in range(CG):
        acc = jnp.zeros((8, 256), F32)
        for j in range(8):
            at = ky * 8 + j
            acc = acc + jnp.broadcast_to(modes[:, G * ky + 3 * j : G * ky + 3 * j + 1], (8, 256)) * green_ref[8 * at : 8 * at + 8]
        cells = cells + over_y_ref[ky] * jnp.sum(acc, axis=0, keepdims=True)
    turn_ref[...] = jnp.concatenate([cells, jnp.zeros((120, 256), F32)], 0).T
    line_ref[...] = jnp.zeros_like(line_ref)
    for j in range(CZ):
        line_ref[:, 8 * j : 8 * j + 8] = turn_ref[pl.ds(j, DOMS, stride=8), :][:, :8]
    head = lax.broadcasted_iota(jnp.int32, (8, 128), 0) == 0
    edge = edge_ref[...]
    for d in range(DOMS):
        out_ref[d] = jnp.where(head, line_ref[d : d + 1], edge)


def hartree_shares(rows, vectors, green, over_x, over_y, edges):
    return pl.pallas_call(
        share_kernel,
        out_shape=jax.ShapeDtypeStruct((DOMS, 8, 128), F32),
        scratch_shapes=[pltpu.VMEM((256, 128), F32), pltpu.VMEM((DOMS, 128), F32)],
        compiler_params=LIMIT,
        interpret=INTERPRET,
        name="share",
    )(rows, vectors, green, over_x, over_y, edges)


def final_kernel(side_ref, msg_ref, own_ref, vec_ref, dens_ref, hart_ref):
    total = msg_ref[0]
    for d in range(1, DOMS):
        total = total + msg_ref[d]
    for j in range(CZ):
        hart_ref[j] = total[0:1, 8 * j : 8 * j + 8]
    lane = lax.broadcasted_iota(jnp.int32, (8, ROW), 1)

    def rows(tile):
        spread = [jnp.broadcast_to(tile[t + 1 : t + 2], (8, 128)) for t in range(7)]
        front = jnp.concatenate(spread[:5], 1)
        back = jnp.concatenate(spread[4:] + spread[5:], 1)
        return front, rolled(back, -64)

    left0, left2 = rows(msg_ref[side_ref[0]])
    right0, right2 = rows(msg_ref[side_ref[1]])
    far = G - BUFFER
    left_last = jnp.where(lane < HALF_ROW, rolled(left2, -far), rolled(left2, HALF_ROW + 12 - far))
    right_last = jnp.where(lane < HALF_ROW, rolled(right2, far), rolled(right2, HALF_ROW - 12 + far))
    left_part = (rolled(left0, -far), rolled(left0, -6), left_last)
    right_part = (rolled(right0, far), rolled(right0, 6), right_last)
    for p in range(PLANES):
        mixed = own_ref[p] + vec_ref[2:3, :GG] * left_part[p][0:1, :GG]
        dens_ref[p] = mixed + vec_ref[3:4, :GG] * right_part[p][0:1, :GG]


def final_parts(sides, msg, own, vectors):
    smem = pl.BlockSpec(memory_space=pltpu.SMEM)
    vmem = pl.BlockSpec(memory_space=pltpu.VMEM)
    return pl.pallas_call(
        final_kernel,
        out_shape=(
            jax.ShapeDtypeStruct((PLANES, 1, GG), F32),
            jax.ShapeDtypeStruct((CZ, 1, CG), F32),
        ),
        in_specs=[smem, vmem, vmem, vmem],
        out_specs=(vmem, vmem),
        compiler_params=LIMIT,
        interpret=INTERPRET,
        name="final",
    )(sides, msg, own, vectors)


def exchanged(x, axis):
    return lax.all_to_all(x, axis, split_axis=0, concat_axis=0, tiled=True)


def body(orbitals, potential, density_in, occupation, position, mixing, correlation_weight):
    sine, inverse, onto, gather, over_x, over_y = tables()
    filtered, weight = filtered_shares(orbitals[0], potential[0], occupation.reshape(1, NB))
    shares = exchanged(filtered, "band")
    flat = shares.reshape(NB, SHARE)
    din = jnp.transpose(density_in, (1, 0, 2))
    grams = exchanged(packed_grams(flat), "band")
    poly, fresh, coarse = density_rows(grams, flat, weight, din, gather)
    rows = exchanged(coarse, "band")
    points, own, edges, vectors, sides, green = output_parts(
        position, mixing, correlation_weight, poly, flat, fresh, din, sine, inverse, onto
    )
    msg = exchanged(hartree_shares(rows, vectors, green, over_x, over_y, edges), "dom")
    dens, hart = final_parts(sides, msg, own, vectors)
    orbitals_out = jnp.transpose(points.reshape(PLANES, GG, NB), (2, 0, 1)).reshape(1, NB, PLANES, GG)
    density = jnp.transpose(dens, (1, 0, 2))
    hartree = jnp.transpose(hart, (1, 2, 0)).reshape(1, 1, CG, CZ)
    return orbitals_out, density, hartree


def solution(mesh):
    return jax.shard_map(
        body,
        mesh=mesh,
        in_specs=(
            P("dom", "band", None, None),
            P("dom", None, None),
            P("dom", "band", None),
            P(),
            P(),
            P(),
            P(),
        ),
        out_specs=(
            P("dom", None, "band", None),
            P("dom", "band", None),
            P("dom", "band", None, None),
        ),
        check_vma=False,
    )
```

```python
import functools
import numpy as np
import jax
import jax.numpy as jnp
from jax import lax
from jax.experimental import pallas as pl
from jax.experimental.pallas import tpu as pltpu
from jax.sharding import PartitionSpec as P

NB = 128
G = 24
GG = G * G
BUFFER = 6
CG = 8
CZ = 6
NZC = 192
DOMS = 32
BANDS = 8
LOCAL = NB // BANDS
PLANES = G // BANDS
ROW = 640
SHARE = 1792
PACKED = 72
HALF_ROW = GG // 2
EDGE = GG + HALF_ROW
POINTS = float(G * G * G)
FILTER_LOW = 1.0
FILTER_HIGH = 9.5
CENTER = 0.5 * (FILTER_HIGH + FILTER_LOW)
HALF = 0.5 * (FILTER_HIGH - FILTER_LOW)
HIGHEST = lax.Precision.HIGHEST
F32 = jnp.float32
INTERPRET = False
LIMIT = pltpu.CompilerParams(vmem_limit_bytes=16 << 20)


def tables():
    k = np.arange(CG)
    cosine = np.sqrt(2.0 / CG) * np.cos(np.pi * k[:, None] * (k[None, :] + 0.5) / CG)
    cosine[0] *= np.sqrt(0.5)
    r = np.arange(NZC)
    sine = np.zeros((NZC + 8, NZC))
    sine[:NZC] = np.sqrt(2.0 / (NZC + 1)) * np.sin(np.pi * (r[:, None] + 1) * (r[None, :] + 1) / (NZC + 1))
    level_xy = 4.0 * np.sin(0.5 * np.pi * k / CG) ** 2
    level_z = 4.0 * np.sin(0.5 * np.pi * (r + 1) / (NZC + 1)) ** 2
    inverse = 1.0 / (level_xy[:, None, None] + level_xy[None, :, None] + level_z[None, None, :])
    scale = 8.0 / float(NZC * NZC)
    onto_x = np.broadcast_to((scale * cosine.T)[:, :, None], (CG, CG, NZC))
    lane = np.arange(GG)
    gather = np.zeros((ROW, 256))
    for ky in range(CG):
        gather[lane, ky * G + lane % G] = cosine[ky, (lane // G) // 3]
    over_x = np.broadcast_to(cosine.T[:, :, None], (CG, CG, 256))
    over_y = np.broadcast_to(cosine[:, :, None], (CG, CG, 256))
    sine = np.stack([sine[CZ * place : CZ * place + 8] for place in range(DOMS)])
    as_f32 = lambda a: np.ascontiguousarray(a, dtype=np.float32)
    return tuple(as_f32(a) for a in (sine, inverse.reshape(CG * CG, NZC), onto_x, gather, over_x, over_y))


def halves(x):
    high = x.astype(jnp.bfloat16)
    return high, (x - high.astype(F32)).astype(jnp.bfloat16)


def dot3(x, y, dims=(((1,), (0,)), ((), ()))):
    x_high, x_low = halves(x)
    y_high, y_low = halves(y)
    dot = functools.partial(lax.dot_general, dimension_numbers=dims, preferred_element_type=F32)
    return dot(x_high, y_high) + (dot(x_high, y_low) + dot(x_low, y_high))


def rolled(x, shift):
    return pltpu.roll(x, shift % ROW, 1)


def lane_index(shape):
    lane = lax.broadcasted_iota(jnp.int32, shape, 1).astype(F32)
    return lane, lane - G * jnp.floor((lane + 0.5) * (1.0 / G))


def neighbour_matrix(mat_ref):
    mat_ref[...] = jnp.zeros_like(mat_ref)
    for t in range(ROW // 128):
        top, end = max(0, 128 * t - 32), min(ROW, 128 * t + 160)
        shape = (end - top, 128)
        row = lax.broadcasted_iota(jnp.int32, shape, 0) + top
        col = lax.broadcasted_iota(jnp.int32, (8, 128), 1) + 128 * t
        _, z = lane_index((8, ROW))
        z = z[:, 128 * t : 128 * (t + 1)]
        before = jnp.where(z > 0.5, col - 1, -ROW)[0:1]
        after = jnp.where(z < G - 1.5, col + 1, -ROW)[0:1]
        col = col[0:1]
        hit = (row == before) | (row == after) | (row == col - G) | (row == col + G)
        hit = hit & (row < GG) & (col < GG)
        mat_ref[top:end, 128 * t : 128 * (t + 1)] = jnp.where(hit, 1.0, 0.0).astype(jnp.bfloat16)


def filter_kernel(orb_ref, pot_ref, mat_ref, vec_ref, out_ref, zero_ref, first_ref, side_ref, diag_ref):
    diag_ref[:, GG - 64 :] = jnp.zeros((G, 128), F32)
    zero_ref[:, :, GG - 64 :] = jnp.zeros((G, LOCAL, 128), F32)
    diag_ref[:, :GG] = (pot_ref[...] + (3.0 - CENTER)) * 2.0
    dot = functools.partial(jnp.dot, preferred_element_type=F32)

    def sum_sides(source, c):
        high, low = halves(source[8 * c : 8 * c + 8].reshape(8 * LOCAL, ROW))
        stack = jnp.concatenate([high, low], 0)
        for rows, cols in ((slice(0, 384), slice(0, 256)), (slice(128, 640), slice(256, 512)), (slice(384, 640), slice(512, 640))):
            both = dot(stack[:, rows], mat_ref[rows, cols])
            side = both[: 8 * LOCAL] + both[8 * LOCAL :]
            side_ref[8 * c : 8 * c + 8, :, cols] = side.reshape(8, LOCAL, cols.stop - cols.start)

    def applied(source, x):
        v = source[x]
        near = side_ref[x]
        if x > 0:
            near = near + source[x - 1]
        if x + 1 < G:
            near = near + source[x + 1]
        return diag_ref[x : x + 1] * v - near

    for c in range(3):
        for x in range(8 * c, 8 * c + 8):
            zero_ref[x, :, :GG] = orb_ref[:, x, :]
        sum_sides(zero_ref, c)
    for x in range(G):
        first_ref[x] = applied(zero_ref, x)
    for c in range(3):
        sum_sides(first_ref, c)
    for x in range(G):
        second = (0.5 / HALF**2) * applied(first_ref, x) - zero_ref[x]
        p = x % PLANES
        out_ref[x // PLANES, :, p * GG : (p + 1) * GG] = second[:, :GG]
        if p == PLANES - 1:
            out_ref[x // PLANES, :, PLANES * GG :] = jnp.zeros((LOCAL, SHARE - PLANES * GG), F32)


def filtered_shares(orbitals, potential, vectors):
    matrix = pl.pallas_call(
        neighbour_matrix,
        out_shape=jax.ShapeDtypeStruct((ROW, ROW), jnp.bfloat16),
        cost_estimate=pl.CostEstimate(flops=20_000_000_000, bytes_accessed=4_000_000, transcendentals=0),
        compiler_params=LIMIT,
        interpret=INTERPRET,
        name="matrix",
    )()
    return pl.pallas_call(
        filter_kernel,
        out_shape=jax.ShapeDtypeStruct((BANDS, LOCAL, SHARE), F32),
        scratch_shapes=[
            pltpu.VMEM((G, LOCAL, ROW), F32),
            pltpu.VMEM((G, LOCAL, ROW), F32),
            pltpu.VMEM((G, LOCAL, ROW), F32),
            pltpu.VMEM((G, ROW), F32),
        ],
        compiler_params=LIMIT,
        interpret=INTERPRET,
        name="filter",
    )(orbitals, potential, matrix, vectors)


def gram_kernel(f_ref, out_ref):
    high, low = halves(f_ref[...])
    both = lax.dot_general(
        high, jnp.concatenate([high, low], 0), (((1,), (1,)), ((), ())), preferred_element_type=F32
    )
    cross = both[:, NB:]
    raw = both[:, :NB] + (cross + cross.T)
    row = lax.broadcasted_iota(jnp.int32, (64, NB), 0)
    col = lax.broadcasted_iota(jnp.int32, (64, NB), 1)
    lower = pltpu.roll(raw[64:], 64, 1)
    packed = jnp.where(col >= row, raw[:64], lower)
    diag = jnp.sum(jnp.where(col == row + 64, raw[64:], 0.0), axis=0, keepdims=True)
    diag = jnp.broadcast_to(diag, (8, NB))
    for k in range(BANDS):
        out_ref[k, :64] = packed
        out_ref[k, 64:] = diag


def packed_grams(flat):
    return pl.pallas_call(
        gram_kernel,
        out_shape=jax.ShapeDtypeStruct((BANDS, PACKED, NB), F32),
        compiler_params=LIMIT,
        interpret=INTERPRET,
        name="gram",
    )(flat)


def density_kernel(
    g_ref, f_ref, weight_ref, din_ref, gather_ref, vec_ref,
    out_ref, coarse_ref, own_ref, edge_ref,
    point_ref, fresh_ref, rows_ref, sems,
):
    total = g_ref[0]
    for k in range(1, BANDS):
        total = total + g_ref[k]
    packed = total[:64]
    row = lax.broadcasted_iota(jnp.int32, (64, NB), 0)
    col = lax.broadcasted_iota(jnp.int32, (64, NB), 1)
    top = jnp.where(col > row, packed, jnp.where(col == row, 0.5 * packed, 0.0))
    low = pltpu.roll(jnp.where(col < row, packed, 0.0), 64, 1)
    low = low + jnp.where(col == row + 64, 0.5 * total[64:65], 0.0)
    half = jnp.concatenate([top, low], 0)
    raw = half + half.T
    norm = jnp.sqrt(jnp.sum(jnp.sum(raw * raw, axis=0, keepdims=True), axis=1, keepdims=True))
    a = raw / norm
    scaling = jnp.sqrt(POINTS / norm)
    eye = jnp.where(
        lax.broadcasted_iota(jnp.int32, (NB, NB), 0) == lax.broadcasted_iota(jnp.int32, (NB, NB), 1), 1.0, 0.0
    )
    square = dot3(a, a)
    tail = dot3(square, 0.0625 * square - 0.5625 * a)
    poly = scaling * (2.25 * eye + (1.6875 * square - 2.4375 * a) + tail)
    poly_high, poly_low = halves(poly)
    dot = functools.partial(jnp.dot, preferred_element_type=F32)

    copies = []
    for c in range(7):
        start, count = 256 * c, min(256, PLANES * GG - 256 * c)
        for at in range(start, start + count, 128):
            high, low = halves(f_ref[:, at : at + 128].T)
            value = dot(high, poly_high) + (dot(high, poly_low) + dot(low, poly_high))
            point_ref[at : at + 128] = value
        part = pl.ds(start, count)
        copies.append(pltpu.make_async_copy(point_ref.at[part], out_ref.at[part], sems.at[c]))
        copies[-1].start()

    both = jnp.concatenate([poly_high, poly_low], 1)
    for c in range(SHARE // 256):
        cols = slice(256 * c, 256 * (c + 1))
        high, low = halves(f_ref[:, cols])
        current = dot(both, jnp.concatenate([high, high], 0)) + dot(poly_high, low)
        line = jnp.sum(current * current * weight_ref[...], axis=0, keepdims=True)
        fresh_ref[:, cols] = jnp.broadcast_to(line, (8, 256))
    planes = [fresh_ref[:, p * GG : p * GG + ROW] for p in range(PLANES)]

    rows_ref[...] = jnp.zeros_like(rows_ref)
    rows_ref[0:8, :GG] = (planes[0] + planes[1] + planes[2])[:, :GG]
    rows_ref[8:9, :GG] = din_ref[0] + din_ref[1] + din_ref[2]
    cells = dot3(rows_ref[...], gather_ref[...])
    row = lax.broadcasted_iota(jnp.int32, (8, NB), 0)
    inputs = jnp.broadcast_to(cells[8:9], (8, 256))
    tile = jnp.where(row == 0, cells[:8, :128], cells[:8, 128:])
    tile = jnp.where(row == 2, inputs[:, :128], jnp.where(row == 3, inputs[:, 128:], tile))
    for k in range(BANDS):
        coarse_ref[k] = tile

    lane, z = lane_index((8, ROW))
    low_edge = (z < BUFFER - 0.5) & (lane < GG)
    high_edge = (z > G - BUFFER - 0.5) & (lane < GG)
    middle = (z > BUFFER - 0.5) & (z < G - BUFFER - 0.5)
    edges = []
    for p in range(PLANES):
        own_ref[p] = vec_ref[4:5, :GG] * planes[p][0:1, :GG] + vec_ref[5:6, :GG] * din_ref[p]
        edges.append((jnp.where(low_edge, planes[p], 0.0), jnp.where(high_edge, planes[p], 0.0)))
    first = (edges[0][0] + edges[0][1]) + (rolled(edges[1][0], 12) + rolled(edges[1][1], -12))
    last = edges[2][0] + edges[2][1]
    moved = rolled(edges[2][0], 12 - HALF_ROW) + rolled(edges[2][1], -12 - HALF_ROW)
    last = jnp.where(lane < HALF_ROW, jnp.where(middle, moved, last), 0.0)
    first = first + rolled(jnp.where(lane < 64, last, 0.0), GG)
    rest = rolled(last, -64)
    edge_ref[0:1] = jnp.zeros((1, 128), F32)
    for t in range(7):
        source, at = (first, 128 * t) if t < 5 else (rest, 128 * (t - 5))
        edge_ref[t + 1 : t + 2] = source[0:1, at : at + 128]
    for copy in copies:
        copy.wait()


def density_parts(grams, flat, weight, din, gather, vectors):
    vmem = pl.BlockSpec(memory_space=pltpu.VMEM)
    return pl.pallas_call(
        density_kernel,
        out_shape=(
            jax.ShapeDtypeStruct((PLANES * GG, NB), F32),
            jax.ShapeDtypeStruct((BANDS, 8, 128), F32),
            jax.ShapeDtypeStruct((PLANES, 1, GG), F32),
            jax.ShapeDtypeStruct((8, 128), F32),
        ),
        in_specs=[vmem] * 6,
        out_specs=(pl.BlockSpec(memory_space=pltpu.HBM), vmem, vmem, vmem),
        scratch_shapes=[
            pltpu.VMEM((SHARE, NB), F32),
            pltpu.VMEM((8, SHARE), F32),
            pltpu.VMEM((16, ROW), F32),
            pltpu.SemaphoreType.DMA((7,)),
        ],
        compiler_params=LIMIT,
        interpret=INTERPRET,
        name="density",
    )(grams, flat, weight, din, gather, vectors)


def place_kernel(
    pos_ref, mix_ref, corr_ref, occ_ref, sine_ref, inverse_ref, onto_ref,
    vec_ref, side_ref, green_ref, weight_ref, left_ref, right_ref,
):
    if INTERPRET:
        dom, band = pos_ref[DOMS], pos_ref[DOMS + 1]
    else:
        dom, band = lax.axis_index("dom"), lax.axis_index("band")
    own = pos_ref[dom]
    shape = (8, ROW)
    _, z = lane_index(shape)
    corr = jnp.zeros(shape, F32)
    for j in range(BUFFER):
        here = (jnp.abs(z - j) < 0.5) | (jnp.abs(z - (G - BUFFER + j)) < 0.5)
        corr = jnp.where(here, corr_ref[j].astype(F32), corr)
    corr = corr * (1.0 / 16.0)
    fresh_weight = jnp.full(shape, mix_ref[0].astype(F32))
    input_weight = jnp.full(shape, mix_ref[1].astype(F32))
    both = fresh_weight + input_weight
    fresh_weight = fresh_weight / both
    input_weight = input_weight / both
    has_left = jnp.where(jnp.full(shape, own) > 0, 1.0, 0.0)
    has_right = jnp.where(jnp.full(shape, own) < DOMS - 1, 1.0, 0.0)
    low_z = z < BUFFER - 0.5
    high_z = z > G - BUFFER - 0.5
    from_left = jnp.where(low_z, corr * has_left, 0.0)
    from_right = jnp.where(high_z, (1.0 - corr) * has_right, 0.0)
    keep = 1.0 - from_left - from_right
    cell = 1.0 / 27.0
    vec_ref[0:1] = (cell * fresh_weight * jnp.where(high_z, corr * has_right, keep))[0:1]
    vec_ref[1:2] = jnp.where(high_z, 0.0, cell * input_weight)[0:1]
    vec_ref[2:3] = (fresh_weight * from_left)[0:1]
    vec_ref[3:4] = (fresh_weight * from_right)[0:1]
    vec_ref[4:5] = (fresh_weight * keep)[0:1]
    vec_ref[5:6] = input_weight[0:1]

    left, right = jnp.int32(0), jnp.int32(0)
    for d in range(DOMS):
        left = jnp.where(pos_ref[d] == own - 1, d, left)
        right = jnp.where(pos_ref[d] == own + 1, d, right)
        right_ref[8 * d : 8 * d + 8] = sine_ref[pos_ref[d]]
    side_ref[0] = left
    side_ref[1] = right
    mine = sine_ref[own]
    onto = onto_ref[band]
    for ky in range(CG):
        part = inverse_ref[8 * ky : 8 * ky + 8] * onto
        for j in range(8):
            at = ky * 64 + j * 8
            left_ref[at : at + 8] = part * mine[j : j + 1]
    eye = lax.broadcasted_iota(jnp.int32, (NB, NB), 0) == lax.broadcasted_iota(jnp.int32, (NB, NB), 1)
    weight = jnp.sum(jnp.where(eye, occ_ref[...] * (1.0 / NB), 0.0), axis=1, keepdims=True)
    weight_ref[...] = jnp.broadcast_to(weight, (NB, 256))
    green_ref[...] = dot3(left_ref[...], right_ref[...], (((1,), (1,)), ((), ())))


def placed(position, mixing, corr, occupation, sine, inverse, onto):
    if INTERPRET:
        position = jnp.append(position, jnp.stack([lax.axis_index("dom"), lax.axis_index("band")]))
    smem = pl.BlockSpec(memory_space=pltpu.SMEM)
    vmem = pl.BlockSpec(memory_space=pltpu.VMEM)
    return pl.pallas_call(
        place_kernel,
        out_shape=(
            jax.ShapeDtypeStruct((8, ROW), F32),
            jax.ShapeDtypeStruct((2,), jnp.int32),
            jax.ShapeDtypeStruct((512, 256), F32),
            jax.ShapeDtypeStruct((NB, 256), F32),
        ),
        in_specs=[smem] * 3 + [vmem] * 4,
        out_specs=(vmem, smem, vmem, vmem),
        scratch_shapes=[pltpu.VMEM((512, NZC), F32), pltpu.VMEM((256, NZC), F32)],
        cost_estimate=pl.CostEstimate(flops=1_000_000, bytes_accessed=100_000, transcendentals=0),
        compiler_params=LIMIT,
        interpret=INTERPRET,
        name="place",
    )(position, mixing, corr, occupation, sine, inverse, onto)


def share_kernel(rows_ref, vec_ref, green_ref, over_x_ref, over_y_ref, edge_ref, out_ref, turn_ref, line_ref):
    fresh = jnp.concatenate([rows_ref[:, 0, :], rows_ref[:, 1, :]], 1)
    inputs = jnp.concatenate([rows_ref[:, 2, :], rows_ref[:, 3, :]], 1)
    cells = fresh * vec_ref[0:1, :256] + inputs * vec_ref[1:2, :256]
    cells = cells + (pltpu.roll(cells, 255, 1) + pltpu.roll(cells, 254, 1))
    modes = over_x_ref[0] * cells[0:1]
    for x in range(1, CG):
        modes = modes + over_x_ref[x] * cells[x : x + 1]
    cells = jnp.zeros((8, 256), F32)
    for ky in range(CG):
        acc = jnp.zeros((8, 256), F32)
        for j in range(8):
            at = ky * 8 + j
            acc = acc + jnp.broadcast_to(modes[:, G * ky + 3 * j : G * ky + 3 * j + 1], (8, 256)) * green_ref[8 * at : 8 * at + 8]
        cells = cells + over_y_ref[ky] * jnp.sum(acc, axis=0, keepdims=True)
    turn_ref[...] = jnp.concatenate([cells, jnp.zeros((120, 256), F32)], 0).T
    line_ref[...] = jnp.zeros_like(line_ref)
    for j in range(CZ):
        line_ref[:, 8 * j : 8 * j + 8] = turn_ref[pl.ds(j, DOMS, stride=8), :][:, :8]
    head = lax.broadcasted_iota(jnp.int32, (8, 128), 0) == 0
    edge = edge_ref[...]
    for d in range(DOMS):
        out_ref[d] = jnp.where(head, line_ref[d : d + 1], edge)


def hartree_shares(rows, vectors, green, over_x, over_y, edges):
    return pl.pallas_call(
        share_kernel,
        out_shape=jax.ShapeDtypeStruct((DOMS, 8, 128), F32),
        scratch_shapes=[pltpu.VMEM((256, 128), F32), pltpu.VMEM((DOMS, 128), F32)],
        compiler_params=LIMIT,
        interpret=INTERPRET,
        name="share",
    )(rows, vectors, green, over_x, over_y, edges)


def final_kernel(side_ref, msg_ref, own_ref, vec_ref, dens_ref, hart_ref):
    total = msg_ref[0]
    for d in range(1, DOMS):
        total = total + msg_ref[d]
    for j in range(CZ):
        hart_ref[j] = total[0:1, 8 * j : 8 * j + 8]
    lane = lax.broadcasted_iota(jnp.int32, (8, ROW), 1)

    def rows(tile):
        spread = [jnp.broadcast_to(tile[t + 1 : t + 2], (8, 128)) for t in range(7)]
        front = jnp.concatenate(spread[:5], 1)
        back = jnp.concatenate(spread[4:] + spread[5:], 1)
        return front, rolled(back, -64)

    left0, left2 = rows(msg_ref[side_ref[0]])
    right0, right2 = rows(msg_ref[side_ref[1]])
    far = G - BUFFER
    left_last = jnp.where(lane < HALF_ROW, rolled(left2, -far), rolled(left2, HALF_ROW + 12 - far))
    right_last = jnp.where(lane < HALF_ROW, rolled(right2, far), rolled(right2, HALF_ROW - 12 + far))
    left_part = (rolled(left0, -far), rolled(left0, -6), left_last)
    right_part = (rolled(right0, far), rolled(right0, 6), right_last)
    for p in range(PLANES):
        mixed = own_ref[p] + vec_ref[2:3, :GG] * left_part[p][0:1, :GG]
        dens_ref[p] = mixed + vec_ref[3:4, :GG] * right_part[p][0:1, :GG]


def final_parts(sides, msg, own, vectors):
    smem = pl.BlockSpec(memory_space=pltpu.SMEM)
    vmem = pl.BlockSpec(memory_space=pltpu.VMEM)
    return pl.pallas_call(
        final_kernel,
        out_shape=(
            jax.ShapeDtypeStruct((PLANES, 1, GG), F32),
            jax.ShapeDtypeStruct((CZ, 1, CG), F32),
        ),
        in_specs=[smem, vmem, vmem, vmem],
        out_specs=(vmem, vmem),
        compiler_params=LIMIT,
        interpret=INTERPRET,
        name="final",
    )(sides, msg, own, vectors)


def exchanged(x, axis):
    return lax.all_to_all(x, axis, split_axis=0, concat_axis=0, tiled=True)


def body(orbitals, potential, density_in, occupation, position, mixing, correlation_weight):
    sine, inverse, onto, gather, over_x, over_y = tables()
    din = jnp.transpose(density_in, (1, 0, 2))
    vectors, sides, green, weight = placed(
        position, mixing, correlation_weight, occupation.reshape(1, NB), sine, inverse, onto
    )
    filtered = filtered_shares(orbitals[0], potential[0], vectors)
    flat = exchanged(filtered, "band").reshape(NB, SHARE)
    grams = exchanged(packed_grams(flat), "band")
    points, coarse, own, edges = density_parts(grams, flat, weight, din, gather, vectors)
    rows = exchanged(coarse, "band")
    msg = exchanged(hartree_shares(rows, vectors, green, over_x, over_y, edges), "dom")
    dens, hart = final_parts(sides, msg, own, vectors)
    orbitals_out = jnp.transpose(points.reshape(PLANES, GG, NB), (2, 0, 1)).reshape(1, NB, PLANES, GG)
    density = jnp.transpose(dens, (1, 0, 2))
    hartree = jnp.transpose(hart, (1, 2, 0)).reshape(1, 1, CG, CZ)
    return orbitals_out, density, hartree


def solution(mesh):
    return jax.shard_map(
        body,
        mesh=mesh,
        in_specs=(
            P("dom", "band", None, None),
            P("dom", None, None),
            P("dom", "band", None),
            P(),
            P(),
            P(),
            P(),
        ),
        out_specs=(
            P("dom", None, "band", None),
            P("dom", "band", None),
            P("dom", "band", None, None),
        ),
        check_vma=False,
    )
```

```python
import functools
import numpy as np
import jax
import jax.numpy as jnp
from jax import lax
from jax.experimental import pallas as pl
from jax.experimental.pallas import tpu as pltpu
from jax.sharding import PartitionSpec as P

NB = 128
G = 24
GG = G * G
BUFFER = 6
CG = 8
CZ = 6
NZC = 192
DOMS = 32
BANDS = 8
LOCAL = NB // BANDS
PLANES = G // BANDS
ROW = 640
SHARE = 1792
PACKED = 72
HALF_ROW = GG // 2
EDGE = GG + HALF_ROW
POINTS = float(G * G * G)
FILTER_LOW = 1.0
FILTER_HIGH = 9.5
CENTER = 0.5 * (FILTER_HIGH + FILTER_LOW)
HALF = 0.5 * (FILTER_HIGH - FILTER_LOW)
HIGHEST = lax.Precision.HIGHEST
F32 = jnp.float32
INTERPRET = False
LIMIT = pltpu.CompilerParams(vmem_limit_bytes=16 << 20)


def tables():
    k = np.arange(CG)
    cosine = np.sqrt(2.0 / CG) * np.cos(np.pi * k[:, None] * (k[None, :] + 0.5) / CG)
    cosine[0] *= np.sqrt(0.5)
    r = np.arange(NZC)
    sine = np.zeros((NZC + 8, NZC))
    sine[:NZC] = np.sqrt(2.0 / (NZC + 1)) * np.sin(np.pi * (r[:, None] + 1) * (r[None, :] + 1) / (NZC + 1))
    level_xy = 4.0 * np.sin(0.5 * np.pi * k / CG) ** 2
    level_z = 4.0 * np.sin(0.5 * np.pi * (r + 1) / (NZC + 1)) ** 2
    inverse = 1.0 / (level_xy[:, None, None] + level_xy[None, :, None] + level_z[None, None, :])
    scale = 8.0 / float(NZC * NZC)
    onto_x = np.broadcast_to((scale * cosine.T)[:, :, None], (CG, CG, NZC))
    lane = np.arange(GG)
    gather = np.zeros((ROW, 256))
    for ky in range(CG):
        gather[lane, ky * G + lane % G] = cosine[ky, (lane // G) // 3]
    over_x = np.broadcast_to(cosine.T[:, :, None], (CG, CG, 256))
    over_y = np.broadcast_to(cosine[:, :, None], (CG, CG, 256))
    sine = np.stack([sine[CZ * place : CZ * place + 8] for place in range(DOMS)])
    as_f32 = lambda a: np.ascontiguousarray(a, dtype=np.float32)
    return tuple(as_f32(a) for a in (sine, inverse.reshape(CG * CG, NZC), onto_x, gather, over_x, over_y))


def halves(x):
    high = x.astype(jnp.bfloat16)
    return high, (x - high.astype(F32)).astype(jnp.bfloat16)


def dot3(x, y, dims=(((1,), (0,)), ((), ()))):
    x_high, x_low = halves(x)
    y_high, y_low = halves(y)
    dot = functools.partial(lax.dot_general, dimension_numbers=dims, preferred_element_type=F32)
    return dot(x_high, y_high) + (dot(x_high, y_low) + dot(x_low, y_high))


def rolled(x, shift):
    return pltpu.roll(x, shift % ROW, 1)


def lane_index(shape):
    lane = lax.broadcasted_iota(jnp.int32, shape, 1).astype(F32)
    return lane, lane - G * jnp.floor((lane + 0.5) * (1.0 / G))


def neighbour_matrix(mat_ref):
    mat_ref[...] = jnp.zeros_like(mat_ref)
    for t in range(ROW // 128):
        top, end = max(0, 128 * t - 32), min(ROW, 128 * t + 160)
        shape = (end - top, 128)
        row = lax.broadcasted_iota(jnp.int32, shape, 0) + top
        col = lax.broadcasted_iota(jnp.int32, (8, 128), 1) + 128 * t
        _, z = lane_index((8, ROW))
        z = z[:, 128 * t : 128 * (t + 1)]
        before = jnp.where(z > 0.5, col - 1, -ROW)[0:1]
        after = jnp.where(z < G - 1.5, col + 1, -ROW)[0:1]
        col = col[0:1]
        hit = (row == before) | (row == after) | (row == col - G) | (row == col + G)
        hit = hit & (row < GG) & (col < GG)
        mat_ref[top:end, 128 * t : 128 * (t + 1)] = jnp.where(hit, 1.0, 0.0).astype(jnp.bfloat16)


def filter_kernel(orb_ref, pot_ref, mat_ref, occ_ref, out_ref, weight_ref, zero_ref, first_ref, side_ref, diag_ref):
    eye = lax.broadcasted_iota(jnp.int32, (NB, NB), 0) == lax.broadcasted_iota(jnp.int32, (NB, NB), 1)
    weight = jnp.sum(jnp.where(eye, occ_ref[...] * (1.0 / NB), 0.0), axis=1, keepdims=True)
    weight_ref[...] = jnp.broadcast_to(weight, (NB, 256))
    diag_ref[:, GG - 64 :] = jnp.zeros((G, 128), F32)
    zero_ref[:, :, GG - 64 :] = jnp.zeros((G, LOCAL, 128), F32)
    diag_ref[:, :GG] = (pot_ref[...] + (3.0 - CENTER)) * 2.0
    dot = functools.partial(jnp.dot, preferred_element_type=F32)

    def sum_sides(source, c):
        high, low = halves(source[8 * c : 8 * c + 8].reshape(8 * LOCAL, ROW))
        stack = jnp.concatenate([high, low], 0)
        for rows, cols in ((slice(0, 384), slice(0, 256)), (slice(128, 640), slice(256, 512)), (slice(384, 640), slice(512, 640))):
            both = dot(stack[:, rows], mat_ref[rows, cols])
            side = both[: 8 * LOCAL] + both[8 * LOCAL :]
            side_ref[8 * c : 8 * c + 8, :, cols] = side.reshape(8, LOCAL, cols.stop - cols.start)

    def applied(source, x):
        v = source[x]
        near = side_ref[x]
        if x > 0:
            near = near + source[x - 1]
        if x + 1 < G:
            near = near + source[x + 1]
        return diag_ref[x : x + 1] * v - near

    for c in range(3):
        for x in range(8 * c, 8 * c + 8):
            zero_ref[x, :, :GG] = orb_ref[:, x, :]
        sum_sides(zero_ref, c)
    for x in range(G):
        first_ref[x] = applied(zero_ref, x)
    for c in range(3):
        sum_sides(first_ref, c)
    for x in range(G):
        second = (0.5 / HALF**2) * applied(first_ref, x) - zero_ref[x]
        p = x % PLANES
        out_ref[x // PLANES, :, p * GG : (p + 1) * GG] = second[:, :GG]
        if p == PLANES - 1:
            out_ref[x // PLANES, :, PLANES * GG :] = jnp.zeros((LOCAL, SHARE - PLANES * GG), F32)


def filtered_shares(orbitals, potential, occupation):
    matrix = pl.pallas_call(
        neighbour_matrix,
        out_shape=jax.ShapeDtypeStruct((ROW, ROW), jnp.bfloat16),
        cost_estimate=pl.CostEstimate(flops=20_000_000_000, bytes_accessed=4_000_000, transcendentals=0),
        compiler_params=LIMIT,
        interpret=INTERPRET,
        name="matrix",
    )()
    return pl.pallas_call(
        filter_kernel,
        out_shape=(
            jax.ShapeDtypeStruct((BANDS, LOCAL, SHARE), F32),
            jax.ShapeDtypeStruct((NB, 256), F32),
        ),
        scratch_shapes=[
            pltpu.VMEM((G, LOCAL, ROW), F32),
            pltpu.VMEM((G, LOCAL, ROW), F32),
            pltpu.VMEM((G, LOCAL, ROW), F32),
            pltpu.VMEM((G, ROW), F32),
        ],
        compiler_params=LIMIT,
        interpret=INTERPRET,
        name="filter",
    )(orbitals, potential, matrix, occupation)


def gram_kernel(f_ref, out_ref):
    high, low = halves(f_ref[...])
    both = lax.dot_general(
        high, jnp.concatenate([high, low], 0), (((1,), (1,)), ((), ())), preferred_element_type=F32
    )
    cross = both[:, NB:]
    raw = both[:, :NB] + (cross + cross.T)
    row = lax.broadcasted_iota(jnp.int32, (64, NB), 0)
    col = lax.broadcasted_iota(jnp.int32, (64, NB), 1)
    lower = pltpu.roll(raw[64:], 64, 1)
    packed = jnp.where(col >= row, raw[:64], lower)
    diag = jnp.sum(jnp.where(col == row + 64, raw[64:], 0.0), axis=0, keepdims=True)
    diag = jnp.broadcast_to(diag, (8, NB))
    for k in range(BANDS):
        out_ref[k, :64] = packed
        out_ref[k, 64:] = diag


def packed_grams(flat):
    return pl.pallas_call(
        gram_kernel,
        out_shape=jax.ShapeDtypeStruct((BANDS, PACKED, NB), F32),
        cost_estimate=pl.CostEstimate(flops=20_000_000_000, bytes_accessed=4_000_000, transcendentals=0),
        compiler_params=LIMIT,
        interpret=INTERPRET,
        name="gram",
    )(flat)


def density_kernel(g_ref, f_ref, weight_ref, din_ref, gather_ref, poly_ref, fresh_ref, coarse_ref, rows_ref):
    total = g_ref[0]
    for k in range(1, BANDS):
        total = total + g_ref[k]
    packed = total[:64]
    row = lax.broadcasted_iota(jnp.int32, (64, NB), 0)
    col = lax.broadcasted_iota(jnp.int32, (64, NB), 1)
    top = jnp.where(col > row, packed, jnp.where(col == row, 0.5 * packed, 0.0))
    low = pltpu.roll(jnp.where(col < row, packed, 0.0), 64, 1)
    low = low + jnp.where(col == row + 64, 0.5 * total[64:65], 0.0)
    half = jnp.concatenate([top, low], 0)
    raw = half + half.T
    norm = jnp.sqrt(jnp.sum(jnp.sum(raw * raw, axis=0, keepdims=True), axis=1, keepdims=True))
    a = raw / norm
    scaling = jnp.sqrt(POINTS / norm)
    eye = jnp.where(
        lax.broadcasted_iota(jnp.int32, (NB, NB), 0) == lax.broadcasted_iota(jnp.int32, (NB, NB), 1), 1.0, 0.0
    )
    square = dot3(a, a)
    tail = dot3(square, 0.0625 * square - 0.5625 * a)
    poly = scaling * (2.25 * eye + (1.6875 * square - 2.4375 * a) + tail)
    poly_ref[...] = poly
    poly_high, poly_low = halves(poly)
    both = jnp.concatenate([poly_high, poly_low], 1)
    dot = functools.partial(jnp.dot, preferred_element_type=F32)
    for c in range(SHARE // 256):
        cols = slice(256 * c, 256 * (c + 1))
        high, low = halves(f_ref[:, cols])
        current = dot(both, jnp.concatenate([high, high], 0)) + dot(poly_high, low)
        line = jnp.sum(current * current * weight_ref[...], axis=0, keepdims=True)
        fresh_ref[:, cols] = jnp.broadcast_to(line, (8, 256))
    planes = fresh_ref[:, :ROW] + fresh_ref[:, GG : GG + ROW] + fresh_ref[:, 2 * GG : 2 * GG + ROW]
    rows_ref[...] = jnp.zeros_like(rows_ref)
    rows_ref[0:8, :GG] = planes[:, :GG]
    rows_ref[8:9, :GG] = din_ref[0] + din_ref[1] + din_ref[2]
    cells = dot3(rows_ref[...], gather_ref[...])
    row = lax.broadcasted_iota(jnp.int32, (8, NB), 0)
    inputs = jnp.broadcast_to(cells[8:9], (8, 256))
    tile = jnp.where(row == 0, cells[:8, :128], cells[:8, 128:])
    tile = jnp.where(row == 2, inputs[:, :128], jnp.where(row == 3, inputs[:, 128:], tile))
    for k in range(BANDS):
        coarse_ref[k] = tile


def density_rows(grams, flat, weight, din, gather):
    return pl.pallas_call(
        density_kernel,
        out_shape=(
            jax.ShapeDtypeStruct((NB, NB), F32),
            jax.ShapeDtypeStruct((8, SHARE), F32),
            jax.ShapeDtypeStruct((BANDS, 8, 128), F32),
        ),
        scratch_shapes=[pltpu.VMEM((16, ROW), F32)],
        cost_estimate=pl.CostEstimate(flops=20_000_000_000, bytes_accessed=4_000_000, transcendentals=0),
        compiler_params=LIMIT,
        interpret=INTERPRET,
        name="density",
    )(grams, flat, weight, din, gather)


def output_kernel(
    pos_ref, mix_ref, corr_ref, poly_ref, f_ref, fresh_ref, din_ref, sine_ref, inverse_ref, onto_ref,
    out_ref, own_ref, edge_ref, vec_ref, side_ref, green_ref, left_ref, right_ref, point_ref, sems,
):
    poly_high, poly_low = halves(poly_ref[...])
    dot = functools.partial(jnp.dot, preferred_element_type=F32)
    copies = []
    for c in range(7):
        start, count = 256 * c, min(256, PLANES * GG - 256 * c)
        for at in range(start, start + count, 128):
            high, low = halves(f_ref[:, at : at + 128].T)
            value = dot(high, poly_high) + (dot(high, poly_low) + dot(low, poly_high))
            point_ref[at : at + 128] = value
        part = pl.ds(start, count)
        copies.append(pltpu.make_async_copy(point_ref.at[part], out_ref.at[part], sems.at[c]))
        copies[-1].start()

    if INTERPRET:
        dom, band = pos_ref[DOMS], pos_ref[DOMS + 1]
    else:
        dom, band = lax.axis_index("dom"), lax.axis_index("band")
    own = pos_ref[dom]
    lane, z = lane_index((8, ROW))
    corr = jnp.zeros((8, ROW), F32)
    for j in range(BUFFER):
        here = (jnp.abs(z - j) < 0.5) | (jnp.abs(z - (G - BUFFER + j)) < 0.5)
        corr = jnp.where(here, corr_ref[j].astype(F32), corr)
    corr = corr * (1.0 / 16.0)
    fresh_weight = jnp.full((8, ROW), mix_ref[0].astype(F32))
    input_weight = jnp.full((8, ROW), mix_ref[1].astype(F32))
    both = fresh_weight + input_weight
    fresh_weight = fresh_weight / both
    input_weight = input_weight / both
    has_left = jnp.where(jnp.full((8, ROW), own) > 0, 1.0, 0.0)
    has_right = jnp.where(jnp.full((8, ROW), own) < DOMS - 1, 1.0, 0.0)
    low_z = z < BUFFER - 0.5
    high_z = z > G - BUFFER - 0.5
    middle = (z > BUFFER - 0.5) & (z < G - BUFFER - 0.5)
    from_left = jnp.where(low_z, corr * has_left, 0.0)
    from_right = jnp.where(high_z, (1.0 - corr) * has_right, 0.0)
    keep = 1.0 - from_left - from_right
    cell = 1.0 / 27.0
    vec_ref[0:1] = (cell * fresh_weight * jnp.where(high_z, corr * has_right, keep))[0:1]
    vec_ref[1:2] = jnp.where(high_z, 0.0, cell * input_weight)[0:1]
    vec_ref[2:3] = (fresh_weight * from_left)[0:1]
    vec_ref[3:4] = (fresh_weight * from_right)[0:1]

    low_edge = low_z & (lane < GG)
    high_edge = high_z & (lane < GG)
    edges = []
    for p in range(PLANES):
        plane = fresh_ref[:, p * GG : p * GG + ROW]
        own_ref[p] = (fresh_weight * keep * plane)[0:1, :GG] + input_weight[0:1, :GG] * din_ref[p]
        edges.append((jnp.where(low_edge, plane, 0.0), jnp.where(high_edge, plane, 0.0)))
    first = (edges[0][0] + edges[0][1]) + (rolled(edges[1][0], 12) + rolled(edges[1][1], -12))
    last = edges[2][0] + edges[2][1]
    moved = rolled(edges[2][0], 12 - HALF_ROW) + rolled(edges[2][1], -12 - HALF_ROW)
    last = jnp.where(lane < HALF_ROW, jnp.where(middle, moved, last), 0.0)
    first = first + rolled(jnp.where(lane < 64, last, 0.0), GG)
    rest = rolled(last, -64)
    edge_ref[0:1] = jnp.zeros((1, 128), F32)
    for t in range(7):
        source, at = (first, 128 * t) if t < 5 else (rest, 128 * (t - 5))
        edge_ref[t + 1 : t + 2] = source[0:1, at : at + 128]

    for d in range(DOMS):
        place = jnp.full((1, 128), pos_ref[d])
        side_ref[0, d : d + 1] = jnp.where(place == own - 1, 1.0, 0.0)
        side_ref[1, d : d + 1] = jnp.where(place == own + 1, 1.0, 0.0)
        right_ref[8 * d : 8 * d + 8] = sine_ref[pos_ref[d]]
    mine = sine_ref[own]
    onto = onto_ref[band]
    for ky in range(CG):
        part = inverse_ref[8 * ky : 8 * ky + 8] * onto
        for j in range(8):
            at = ky * 64 + j * 8
            left_ref[at : at + 8] = part * mine[j : j + 1]
    green_ref[...] = dot3(left_ref[...], right_ref[...], (((1,), (1,)), ((), ())))
    for copy in copies:
        copy.wait()


def output_parts(position, mixing, corr, poly, flat, fresh, din, sine, inverse, onto):
    if INTERPRET:
        position = jnp.append(position, jnp.stack([lax.axis_index("dom"), lax.axis_index("band")]))
    smem = pl.BlockSpec(memory_space=pltpu.SMEM)
    vmem = pl.BlockSpec(memory_space=pltpu.VMEM)
    return pl.pallas_call(
        output_kernel,
        out_shape=(
            jax.ShapeDtypeStruct((PLANES * GG, NB), F32),
            jax.ShapeDtypeStruct((PLANES, 1, GG), F32),
            jax.ShapeDtypeStruct((8, 128), F32),
            jax.ShapeDtypeStruct((8, ROW), F32),
            jax.ShapeDtypeStruct((2, DOMS, 128), F32),
            jax.ShapeDtypeStruct((512, 256), F32),
        ),
        in_specs=[smem] * 3 + [vmem] * 7,
        out_specs=(pl.BlockSpec(memory_space=pltpu.HBM), vmem, vmem, vmem, vmem, vmem),
        scratch_shapes=[
            pltpu.VMEM((512, NZC), F32),
            pltpu.VMEM((256, NZC), F32),
            pltpu.VMEM((SHARE, NB), F32),
            pltpu.SemaphoreType.DMA((7,)),
        ],
        cost_estimate=pl.CostEstimate(flops=500_000_000, bytes_accessed=4_000_000, transcendentals=0),
        compiler_params=LIMIT,
        interpret=INTERPRET,
        name="output",
    )(position, mixing, corr, poly, flat, fresh, din, sine, inverse, onto)


def share_kernel(rows_ref, vec_ref, green_ref, over_x_ref, over_y_ref, edge_ref, out_ref, turn_ref, line_ref):
    fresh = jnp.concatenate([rows_ref[:, 0, :], rows_ref[:, 1, :]], 1)
    inputs = jnp.concatenate([rows_ref[:, 2, :], rows_ref[:, 3, :]], 1)
    cells = fresh * vec_ref[0:1, :256] + inputs * vec_ref[1:2, :256]
    cells = cells + (pltpu.roll(cells, 255, 1) + pltpu.roll(cells, 254, 1))
    modes = over_x_ref[0] * cells[0:1]
    for x in range(1, CG):
        modes = modes + over_x_ref[x] * cells[x : x + 1]
    cells = jnp.zeros((8, 256), F32)
    for ky in range(CG):
        acc = jnp.zeros((8, 256), F32)
        for j in range(8):
            at = ky * 8 + j
            acc = acc + jnp.broadcast_to(modes[:, G * ky + 3 * j : G * ky + 3 * j + 1], (8, 256)) * green_ref[8 * at : 8 * at + 8]
        cells = cells + over_y_ref[ky] * jnp.sum(acc, axis=0, keepdims=True)
    turn_ref[...] = jnp.concatenate([cells, jnp.zeros((120, 256), F32)], 0).T
    line_ref[...] = jnp.zeros_like(line_ref)
    for j in range(CZ):
        line_ref[:, 8 * j : 8 * j + 8] = turn_ref[pl.ds(j, DOMS, stride=8), :][:, :8]
    head = lax.broadcasted_iota(jnp.int32, (8, 128), 0) == 0
    edge = edge_ref[...]
    for d in range(DOMS):
        out_ref[d] = jnp.where(head, line_ref[d : d + 1], edge)


def hartree_shares(rows, vectors, green, over_x, over_y, edges):
    return pl.pallas_call(
        share_kernel,
        out_shape=jax.ShapeDtypeStruct((DOMS, 8, 128), F32),
        scratch_shapes=[pltpu.VMEM((256, 128), F32), pltpu.VMEM((DOMS, 128), F32)],
        compiler_params=LIMIT,
        interpret=INTERPRET,
        name="share",
    )(rows, vectors, green, over_x, over_y, edges)


def final_kernel(side_ref, msg_ref, own_ref, vec_ref, dens_ref, hart_ref):
    total = msg_ref[0]
    for d in range(1, DOMS):
        total = total + msg_ref[d]
    for j in range(CZ):
        hart_ref[j] = total[0:1, 8 * j : 8 * j + 8]
    lane = lax.broadcasted_iota(jnp.int32, (8, ROW), 1)

    def picked(side):
        tile = jnp.zeros((8, 128), F32)
        for d in range(DOMS):
            tile = tile + side_ref[side, d : d + 1] * msg_ref[d]
        return tile

    def rows(tile):
        spread = [jnp.broadcast_to(tile[t + 1 : t + 2], (8, 128)) for t in range(7)]
        front = jnp.concatenate(spread[:5], 1)
        back = jnp.concatenate(spread[4:] + spread[5:], 1)
        return front, rolled(back, -64)

    left0, left2 = rows(picked(0))
    right0, right2 = rows(picked(1))
    far = G - BUFFER
    left_last = jnp.where(lane < HALF_ROW, rolled(left2, -far), rolled(left2, HALF_ROW + 12 - far))
    right_last = jnp.where(lane < HALF_ROW, rolled(right2, far), rolled(right2, HALF_ROW - 12 + far))
    left_part = (rolled(left0, -far), rolled(left0, -6), left_last)
    right_part = (rolled(right0, far), rolled(right0, 6), right_last)
    for p in range(PLANES):
        mixed = own_ref[p] + vec_ref[2:3, :GG] * left_part[p][0:1, :GG]
        dens_ref[p] = mixed + vec_ref[3:4, :GG] * right_part[p][0:1, :GG]


def final_parts(sides, msg, own, vectors):
    return pl.pallas_call(
        final_kernel,
        out_shape=(
            jax.ShapeDtypeStruct((PLANES, 1, GG), F32),
            jax.ShapeDtypeStruct((CZ, 1, CG), F32),
        ),
        compiler_params=LIMIT,
        interpret=INTERPRET,
        name="final",
    )(sides, msg, own, vectors)


def exchanged(x, axis):
    return lax.all_to_all(x, axis, split_axis=0, concat_axis=0, tiled=True)


def body(orbitals, potential, density_in, occupation, position, mixing, correlation_weight):
    sine, inverse, onto, gather, over_x, over_y = tables()
    filtered, weight = filtered_shares(orbitals[0], potential[0], occupation.reshape(1, NB))
    shares = exchanged(filtered, "band")
    flat = shares.reshape(NB, SHARE)
    din = jnp.transpose(density_in, (1, 0, 2))
    grams = exchanged(packed_grams(flat), "band")
    poly, fresh, coarse = density_rows(grams, flat, weight, din, gather)
    rows = exchanged(coarse, "band")
    points, own, edges, vectors, sides, green = output_parts(
        position, mixing, correlation_weight, poly, flat, fresh, din, sine, inverse, onto
    )
    msg = exchanged(hartree_shares(rows, vectors, green, over_x, over_y, edges), "dom")
    dens, hart = final_parts(sides, msg, own, vectors)
    orbitals_out = jnp.transpose(points.reshape(PLANES, GG, NB), (2, 0, 1)).reshape(1, NB, PLANES, GG)
    density = jnp.transpose(dens, (1, 0, 2))
    hartree = jnp.transpose(hart, (1, 2, 0)).reshape(1, 1, CG, CZ)
    return orbitals_out, density, hartree


def solution(mesh):
    return jax.shard_map(
        body,
        mesh=mesh,
        in_specs=(
            P("dom", "band", None, None),
            P("dom", None, None),
            P("dom", "band", None),
            P(),
            P(),
            P(),
            P(),
        ),
        out_specs=(
            P("dom", None, "band", None),
            P("dom", "band", None),
            P("dom", "band", None, None),
        ),
        check_vma=False,
    )
```

```python
import functools
import numpy as np
import jax
import jax.numpy as jnp
from jax import lax
from jax.experimental import pallas as pl
from jax.experimental.pallas import tpu as pltpu
from jax.sharding import PartitionSpec as P

NB = 128
G = 24
GG = G * G
BUFFER = 6
CG = 8
CZ = 6
NZC = 192
DOMS = 32
BANDS = 8
LOCAL = NB // BANDS
PLANES = G // BANDS
ROW = 640
SHARE = 1792
PACKED = 72
HALF_ROW = GG // 2
EDGE = GG + HALF_ROW
POINTS = float(G * G * G)
FILTER_LOW = 1.0
FILTER_HIGH = 9.5
CENTER = 0.5 * (FILTER_HIGH + FILTER_LOW)
HALF = 0.5 * (FILTER_HIGH - FILTER_LOW)
HIGHEST = lax.Precision.HIGHEST
F32 = jnp.float32
INTERPRET = False
LIMIT = pltpu.CompilerParams(vmem_limit_bytes=16 << 20)


def tables():
    k = np.arange(CG)
    cosine = np.sqrt(2.0 / CG) * np.cos(np.pi * k[:, None] * (k[None, :] + 0.5) / CG)
    cosine[0] *= np.sqrt(0.5)
    r = np.arange(NZC)
    sine = np.zeros((NZC + 8, NZC))
    sine[:NZC] = np.sqrt(2.0 / (NZC + 1)) * np.sin(np.pi * (r[:, None] + 1) * (r[None, :] + 1) / (NZC + 1))
    level_xy = 4.0 * np.sin(0.5 * np.pi * k / CG) ** 2
    level_z = 4.0 * np.sin(0.5 * np.pi * (r + 1) / (NZC + 1)) ** 2
    inverse = 1.0 / (level_xy[:, None, None] + level_xy[None, :, None] + level_z[None, None, :])
    scale = 8.0 / float(NZC * NZC)
    onto_x = np.broadcast_to((scale * cosine.T)[:, :, None], (CG, CG, NZC))
    lane = np.arange(GG)
    gather = np.zeros((ROW, 256))
    for ky in range(CG):
        gather[lane, ky * G + lane % G] = cosine[ky, (lane // G) // 3]
    over_x = np.broadcast_to(cosine.T[:, :, None], (CG, CG, 256))
    over_y = np.broadcast_to(cosine[:, :, None], (CG, CG, 256))
    sine = np.stack([sine[CZ * place : CZ * place + 8] for place in range(DOMS)])
    as_f32 = lambda a: np.ascontiguousarray(a, dtype=np.float32)
    return tuple(as_f32(a) for a in (sine, inverse.reshape(CG * CG, NZC), onto_x, gather, over_x, over_y))


def halves(x):
    high = x.astype(jnp.bfloat16)
    return high, (x - high.astype(F32)).astype(jnp.bfloat16)


def dot3(x, y, dims=(((1,), (0,)), ((), ()))):
    x_high, x_low = halves(x)
    y_high, y_low = halves(y)
    dot = functools.partial(lax.dot_general, dimension_numbers=dims, preferred_element_type=F32)
    return dot(x_high, y_high) + (dot(x_high, y_low) + dot(x_low, y_high))


def rolled(x, shift):
    return pltpu.roll(x, shift % ROW, 1)


def lane_index(shape):
    lane = lax.broadcasted_iota(jnp.int32, shape, 1).astype(F32)
    return lane, lane - G * jnp.floor((lane + 0.5) * (1.0 / G))


def neighbour_matrix(mat_ref):
    mat_ref[...] = jnp.zeros_like(mat_ref)
    for t in range(ROW // 128):
        top, end = max(0, 128 * t - 32), min(ROW, 128 * t + 160)
        shape = (end - top, 128)
        row = lax.broadcasted_iota(jnp.int32, shape, 0) + top
        col = lax.broadcasted_iota(jnp.int32, (8, 128), 1) + 128 * t
        _, z = lane_index((8, ROW))
        z = z[:, 128 * t : 128 * (t + 1)]
        before = jnp.where(z > 0.5, col - 1, -ROW)[0:1]
        after = jnp.where(z < G - 1.5, col + 1, -ROW)[0:1]
        col = col[0:1]
        hit = (row == before) | (row == after) | (row == col - G) | (row == col + G)
        hit = hit & (row < GG) & (col < GG)
        mat_ref[top:end, 128 * t : 128 * (t + 1)] = jnp.where(hit, 1.0, 0.0).astype(jnp.bfloat16)


def filter_kernel(
    orb_ref, pot_ref, mat_ref, occ_ref, pos_ref, mix_ref, corr_ref,
    out_ref, weight_ref, int_ref, zero_ref, first_ref, side_ref, diag_ref,
):
    eye = lax.broadcasted_iota(jnp.int32, (NB, NB), 0) == lax.broadcasted_iota(jnp.int32, (NB, NB), 1)
    weight = jnp.sum(jnp.where(eye, occ_ref[...] * (1.0 / NB), 0.0), axis=1, keepdims=True)
    weight_ref[...] = jnp.broadcast_to(weight, (NB, 256))
    int_ref[...] = jnp.zeros((8, 128), jnp.int32)
    int_ref[0:1, :DOMS] = pos_ref[...]
    int_ref[1:2, :2] = mix_ref[...]
    int_ref[2:3, :BUFFER] = corr_ref[...]
    diag_ref[:, GG - 64 :] = jnp.zeros((G, 128), F32)
    zero_ref[:, :, GG - 64 :] = jnp.zeros((G, LOCAL, 128), F32)
    diag_ref[:, :GG] = (pot_ref[...] + (3.0 - CENTER)) * 2.0
    dot = functools.partial(jnp.dot, preferred_element_type=F32)

    def sum_sides(source, c):
        high, low = halves(source[8 * c : 8 * c + 8].reshape(8 * LOCAL, ROW))
        stack = jnp.concatenate([high, low], 0)
        for rows, cols in ((slice(0, 384), slice(0, 256)), (slice(128, 640), slice(256, 512)), (slice(384, 640), slice(512, 640))):
            both = dot(stack[:, rows], mat_ref[rows, cols])
            side = both[: 8 * LOCAL] + both[8 * LOCAL :]
            side_ref[8 * c : 8 * c + 8, :, cols] = side.reshape(8, LOCAL, cols.stop - cols.start)

    def applied(source, x):
        v = source[x]
        near = side_ref[x]
        if x > 0:
            near = near + source[x - 1]
        if x + 1 < G:
            near = near + source[x + 1]
        return diag_ref[x : x + 1] * v - near

    for c in range(3):
        for x in range(8 * c, 8 * c + 8):
            zero_ref[x, :, :GG] = orb_ref[:, x, :]
        sum_sides(zero_ref, c)
    for x in range(G):
        first_ref[x] = applied(zero_ref, x)
    for c in range(3):
        sum_sides(first_ref, c)
    for x in range(G):
        second = (0.5 / HALF**2) * applied(first_ref, x) - zero_ref[x]
        p = x % PLANES
        out_ref[x // PLANES, :, p * GG : (p + 1) * GG] = second[:, :GG]
        if p == PLANES - 1:
            out_ref[x // PLANES, :, PLANES * GG :] = jnp.zeros((LOCAL, SHARE - PLANES * GG), F32)


def filtered_shares(orbitals, potential, occupation, *integers):
    matrix = pl.pallas_call(
        neighbour_matrix,
        out_shape=jax.ShapeDtypeStruct((ROW, ROW), jnp.bfloat16),
        cost_estimate=pl.CostEstimate(flops=20_000_000_000, bytes_accessed=4_000_000, transcendentals=0),
        compiler_params=LIMIT,
        interpret=INTERPRET,
        name="matrix",
    )()
    return pl.pallas_call(
        filter_kernel,
        out_shape=(
            jax.ShapeDtypeStruct((BANDS, LOCAL, SHARE), F32),
            jax.ShapeDtypeStruct((NB, 256), F32),
            jax.ShapeDtypeStruct((8, 128), jnp.int32),
        ),
        scratch_shapes=[
            pltpu.VMEM((G, LOCAL, ROW), F32),
            pltpu.VMEM((G, LOCAL, ROW), F32),
            pltpu.VMEM((G, LOCAL, ROW), F32),
            pltpu.VMEM((G, ROW), F32),
        ],
        compiler_params=LIMIT,
        interpret=INTERPRET,
        name="filter",
    )(orbitals, potential, matrix, occupation, *integers)


def gram_kernel(f_ref, out_ref):
    high, low = halves(f_ref[...])
    both = lax.dot_general(
        high, jnp.concatenate([high, low], 0), (((1,), (1,)), ((), ())), preferred_element_type=F32
    )
    cross = both[:, NB:]
    raw = both[:, :NB] + (cross + cross.T)
    row = lax.broadcasted_iota(jnp.int32, (64, NB), 0)
    col = lax.broadcasted_iota(jnp.int32, (64, NB), 1)
    lower = pltpu.roll(raw[64:], 64, 1)
    packed = jnp.where(col >= row, raw[:64], lower)
    diag = jnp.sum(jnp.where(col == row + 64, raw[64:], 0.0), axis=0, keepdims=True)
    diag = jnp.broadcast_to(diag, (8, NB))
    for k in range(BANDS):
        out_ref[k, :64] = packed
        out_ref[k, 64:] = diag


def packed_grams(flat):
    return pl.pallas_call(
        gram_kernel,
        out_shape=jax.ShapeDtypeStruct((BANDS, PACKED, NB), F32),
        cost_estimate=pl.CostEstimate(flops=20_000_000_000, bytes_accessed=4_000_000, transcendentals=0),
        compiler_params=LIMIT,
        interpret=INTERPRET,
        name="gram",
    )(flat)


def lane_weights(int_ref, own, vec_ref):
    shape = (8, ROW)
    _, z = lane_index(shape)
    corr = jnp.zeros(shape, F32)
    for j in range(BUFFER):
        here = (jnp.abs(z - j) < 0.5) | (jnp.abs(z - (G - BUFFER + j)) < 0.5)
        corr = jnp.where(here, int_ref[2, j].astype(F32), corr)
    corr = corr * (1.0 / 16.0)
    fresh_weight = jnp.full(shape, int_ref[1, 0].astype(F32))
    input_weight = jnp.full(shape, int_ref[1, 1].astype(F32))
    both = fresh_weight + input_weight
    fresh_weight = fresh_weight / both
    input_weight = input_weight / both
    has_left = jnp.where(jnp.full(shape, own) > 0, 1.0, 0.0)
    has_right = jnp.where(jnp.full(shape, own) < DOMS - 1, 1.0, 0.0)
    low_z = z < BUFFER - 0.5
    high_z = z > G - BUFFER - 0.5
    from_left = jnp.where(low_z, corr * has_left, 0.0)
    from_right = jnp.where(high_z, (1.0 - corr) * has_right, 0.0)
    keep = 1.0 - from_left - from_right
    cell = 1.0 / 27.0
    vec_ref[0:1] = (cell * fresh_weight * jnp.where(high_z, corr * has_right, keep))[0:1]
    vec_ref[1:2] = jnp.where(high_z, 0.0, cell * input_weight)[0:1]
    vec_ref[2:3] = (fresh_weight * from_left)[0:1]
    vec_ref[3:4] = (fresh_weight * from_right)[0:1]
    vec_ref[4:5] = (fresh_weight * keep)[0:1]
    vec_ref[5:6] = input_weight[0:1]


def poisson_operator(int_ref, own, band, sine_ref, inverse_ref, onto_ref, side_ref, green_ref, left_ref, right_ref):
    for d in range(DOMS):
        place = jnp.full((1, 128), int_ref[0, d])
        side_ref[0, d : d + 1] = jnp.where(place == own - 1, 1.0, 0.0)
        side_ref[1, d : d + 1] = jnp.where(place == own + 1, 1.0, 0.0)
        right_ref[8 * d : 8 * d + 8] = sine_ref[int_ref[0, d]]
    mine = sine_ref[own]
    onto = onto_ref[band]
    for ky in range(CG):
        part = inverse_ref[8 * ky : 8 * ky + 8] * onto
        for j in range(8):
            at = ky * 64 + j * 8
            left_ref[at : at + 8] = part * mine[j : j + 1]
    green_ref[...] = dot3(left_ref[...], right_ref[...], (((1,), (1,)), ((), ())))


def density_kernel(
    g_ref, f_ref, weight_ref, din_ref, gather_ref, int_ref, sine_ref, inverse_ref, onto_ref,
    out_ref, coarse_ref, own_ref, edge_ref, vec_ref, side_ref, green_ref,
    point_ref, fresh_ref, rows_ref, left_ref, right_ref, scalar_ref, sems,
):
    scalars = pltpu.make_async_copy(int_ref, scalar_ref, sems.at[7])
    scalars.start()
    total = g_ref[0]
    for k in range(1, BANDS):
        total = total + g_ref[k]
    packed = total[:64]
    row = lax.broadcasted_iota(jnp.int32, (64, NB), 0)
    col = lax.broadcasted_iota(jnp.int32, (64, NB), 1)
    top = jnp.where(col > row, packed, jnp.where(col == row, 0.5 * packed, 0.0))
    low = pltpu.roll(jnp.where(col < row, packed, 0.0), 64, 1)
    low = low + jnp.where(col == row + 64, 0.5 * total[64:65], 0.0)
    half = jnp.concatenate([top, low], 0)
    raw = half + half.T
    norm = jnp.sqrt(jnp.sum(jnp.sum(raw * raw, axis=0, keepdims=True), axis=1, keepdims=True))
    a = raw / norm
    scaling = jnp.sqrt(POINTS / norm)
    eye = jnp.where(
        lax.broadcasted_iota(jnp.int32, (NB, NB), 0) == lax.broadcasted_iota(jnp.int32, (NB, NB), 1), 1.0, 0.0
    )
    square = dot3(a, a)
    tail = dot3(square, 0.0625 * square - 0.5625 * a)
    poly = scaling * (2.25 * eye + (1.6875 * square - 2.4375 * a) + tail)
    poly_high, poly_low = halves(poly)
    dot = functools.partial(jnp.dot, preferred_element_type=F32)

    copies = []
    for c in range(7):
        start, count = 256 * c, min(256, PLANES * GG - 256 * c)
        for at in range(start, start + count, 128):
            high, low = halves(f_ref[:, at : at + 128].T)
            value = dot(high, poly_high) + (dot(high, poly_low) + dot(low, poly_high))
            point_ref[at : at + 128] = value
        part = pl.ds(start, count)
        copies.append(pltpu.make_async_copy(point_ref.at[part], out_ref.at[part], sems.at[c]))
        copies[-1].start()

    both = jnp.concatenate([poly_high, poly_low], 1)
    for c in range(SHARE // 256):
        cols = slice(256 * c, 256 * (c + 1))
        high, low = halves(f_ref[:, cols])
        current = dot(both, jnp.concatenate([high, high], 0)) + dot(poly_high, low)
        line = jnp.sum(current * current * weight_ref[...], axis=0, keepdims=True)
        fresh_ref[:, cols] = jnp.broadcast_to(line, (8, 256))
    planes = [fresh_ref[:, p * GG : p * GG + ROW] for p in range(PLANES)]

    rows_ref[...] = jnp.zeros_like(rows_ref)
    rows_ref[0:8, :GG] = (planes[0] + planes[1] + planes[2])[:, :GG]
    rows_ref[8:9, :GG] = din_ref[0] + din_ref[1] + din_ref[2]
    cells = dot3(rows_ref[...], gather_ref[...])
    row = lax.broadcasted_iota(jnp.int32, (8, NB), 0)
    inputs = jnp.broadcast_to(cells[8:9], (8, 256))
    tile = jnp.where(row == 0, cells[:8, :128], cells[:8, 128:])
    tile = jnp.where(row == 2, inputs[:, :128], jnp.where(row == 3, inputs[:, 128:], tile))
    for k in range(BANDS):
        coarse_ref[k] = tile

    scalars.wait()
    if INTERPRET:
        dom, band = scalar_ref[3, 0], scalar_ref[3, 1]
    else:
        dom, band = lax.axis_index("dom"), lax.axis_index("band")
    own = scalar_ref[0, dom]
    lane_weights(scalar_ref, own, vec_ref)
    lane, z = lane_index((8, ROW))
    low_edge = (z < BUFFER - 0.5) & (lane < GG)
    high_edge = (z > G - BUFFER - 0.5) & (lane < GG)
    middle = (z > BUFFER - 0.5) & (z < G - BUFFER - 0.5)
    edges = []
    for p in range(PLANES):
        own_ref[p] = vec_ref[4:5, :GG] * planes[p][0:1, :GG] + vec_ref[5:6, :GG] * din_ref[p]
        edges.append((jnp.where(low_edge, planes[p], 0.0), jnp.where(high_edge, planes[p], 0.0)))
    first = (edges[0][0] + edges[0][1]) + (rolled(edges[1][0], 12) + rolled(edges[1][1], -12))
    last = edges[2][0] + edges[2][1]
    moved = rolled(edges[2][0], 12 - HALF_ROW) + rolled(edges[2][1], -12 - HALF_ROW)
    last = jnp.where(lane < HALF_ROW, jnp.where(middle, moved, last), 0.0)
    first = first + rolled(jnp.where(lane < 64, last, 0.0), GG)
    rest = rolled(last, -64)
    edge_ref[0:1] = jnp.zeros((1, 128), F32)
    for t in range(7):
        source, at = (first, 128 * t) if t < 5 else (rest, 128 * (t - 5))
        edge_ref[t + 1 : t + 2] = source[0:1, at : at + 128]
    poisson_operator(
        scalar_ref, own, band, sine_ref, inverse_ref, onto_ref, side_ref, green_ref, left_ref, right_ref
    )
    for copy in copies:
        copy.wait()


def density_parts(grams, flat, weight, din, gather, integers, sine, inverse, onto):
    if INTERPRET:
        axes = jnp.stack([lax.axis_index("dom"), lax.axis_index("band")])
        integers = integers.at[3, :2].set(axes)
    vmem = pl.BlockSpec(memory_space=pltpu.VMEM)
    return pl.pallas_call(
        density_kernel,
        out_shape=(
            jax.ShapeDtypeStruct((PLANES * GG, NB), F32),
            jax.ShapeDtypeStruct((BANDS, 8, 128), F32),
            jax.ShapeDtypeStruct((PLANES, 1, GG), F32),
            jax.ShapeDtypeStruct((8, 128), F32),
            jax.ShapeDtypeStruct((8, ROW), F32),
            jax.ShapeDtypeStruct((2, DOMS, 128), F32),
            jax.ShapeDtypeStruct((512, 256), F32),
        ),
        in_specs=[vmem] * 9,
        out_specs=(pl.BlockSpec(memory_space=pltpu.HBM), vmem, vmem, vmem, vmem, vmem, vmem),
        scratch_shapes=[
            pltpu.VMEM((SHARE, NB), F32),
            pltpu.VMEM((8, SHARE), F32),
            pltpu.VMEM((16, ROW), F32),
            pltpu.VMEM((512, NZC), F32),
            pltpu.VMEM((256, NZC), F32),
            pltpu.SMEM((8, 128), jnp.int32),
            pltpu.SemaphoreType.DMA((8,)),
        ],
        compiler_params=LIMIT,
        interpret=INTERPRET,
        name="density",
    )(grams, flat, weight, din, gather, integers, sine, inverse, onto)


def share_kernel(rows_ref, vec_ref, green_ref, over_x_ref, over_y_ref, edge_ref, out_ref, turn_ref, line_ref):
    fresh = jnp.concatenate([rows_ref[:, 0, :], rows_ref[:, 1, :]], 1)
    inputs = jnp.concatenate([rows_ref[:, 2, :], rows_ref[:, 3, :]], 1)
    cells = fresh * vec_ref[0:1, :256] + inputs * vec_ref[1:2, :256]
    cells = cells + (pltpu.roll(cells, 255, 1) + pltpu.roll(cells, 254, 1))
    modes = over_x_ref[0] * cells[0:1]
    for x in range(1, CG):
        modes = modes + over_x_ref[x] * cells[x : x + 1]
    cells = jnp.zeros((8, 256), F32)
    for ky in range(CG):
        acc = jnp.zeros((8, 256), F32)
        for j in range(8):
            at = ky * 8 + j
            acc = acc + jnp.broadcast_to(modes[:, G * ky + 3 * j : G * ky + 3 * j + 1], (8, 256)) * green_ref[8 * at : 8 * at + 8]
        cells = cells + over_y_ref[ky] * jnp.sum(acc, axis=0, keepdims=True)
    turn_ref[...] = jnp.concatenate([cells, jnp.zeros((120, 256), F32)], 0).T
    line_ref[...] = jnp.zeros_like(line_ref)
    for j in range(CZ):
        line_ref[:, 8 * j : 8 * j + 8] = turn_ref[pl.ds(j, DOMS, stride=8), :][:, :8]
    head = lax.broadcasted_iota(jnp.int32, (8, 128), 0) == 0
    edge = edge_ref[...]
    for d in range(DOMS):
        out_ref[d] = jnp.where(head, line_ref[d : d + 1], edge)


def hartree_shares(rows, vectors, green, over_x, over_y, edges):
    return pl.pallas_call(
        share_kernel,
        out_shape=jax.ShapeDtypeStruct((DOMS, 8, 128), F32),
        scratch_shapes=[pltpu.VMEM((256, 128), F32), pltpu.VMEM((DOMS, 128), F32)],
        compiler_params=LIMIT,
        interpret=INTERPRET,
        name="share",
    )(rows, vectors, green, over_x, over_y, edges)


def final_kernel(side_ref, msg_ref, own_ref, vec_ref, dens_ref, hart_ref):
    total = msg_ref[0]
    for d in range(1, DOMS):
        total = total + msg_ref[d]
    for j in range(CZ):
        hart_ref[j] = total[0:1, 8 * j : 8 * j + 8]
    lane = lax.broadcasted_iota(jnp.int32, (8, ROW), 1)

    def picked(side):
        tile = jnp.zeros((8, 128), F32)
        for d in range(DOMS):
            tile = tile + side_ref[side, d : d + 1] * msg_ref[d]
        return tile

    def rows(tile):
        spread = [jnp.broadcast_to(tile[t + 1 : t + 2], (8, 128)) for t in range(7)]
        front = jnp.concatenate(spread[:5], 1)
        back = jnp.concatenate(spread[4:] + spread[5:], 1)
        return front, rolled(back, -64)

    left0, left2 = rows(picked(0))
    right0, right2 = rows(picked(1))
    far = G - BUFFER
    left_last = jnp.where(lane < HALF_ROW, rolled(left2, -far), rolled(left2, HALF_ROW + 12 - far))
    right_last = jnp.where(lane < HALF_ROW, rolled(right2, far), rolled(right2, HALF_ROW - 12 + far))
    left_part = (rolled(left0, -far), rolled(left0, -6), left_last)
    right_part = (rolled(right0, far), rolled(right0, 6), right_last)
    for p in range(PLANES):
        mixed = own_ref[p] + vec_ref[2:3, :GG] * left_part[p][0:1, :GG]
        dens_ref[p] = mixed + vec_ref[3:4, :GG] * right_part[p][0:1, :GG]


def final_parts(sides, msg, own, vectors):
    return pl.pallas_call(
        final_kernel,
        out_shape=(
            jax.ShapeDtypeStruct((PLANES, 1, GG), F32),
            jax.ShapeDtypeStruct((CZ, 1, CG), F32),
        ),
        compiler_params=LIMIT,
        interpret=INTERPRET,
        name="final",
    )(sides, msg, own, vectors)


def exchanged(x, axis):
    return lax.all_to_all(x, axis, split_axis=0, concat_axis=0, tiled=True)


def body(orbitals, potential, density_in, occupation, position, mixing, correlation_weight):
    sine, inverse, onto, gather, over_x, over_y = tables()
    din = jnp.transpose(density_in, (1, 0, 2))
    small = [v.reshape(1, -1) for v in (occupation, position, mixing, correlation_weight)]
    filtered, weight, integers = filtered_shares(orbitals[0], potential[0], *small)
    flat = exchanged(filtered, "band").reshape(NB, SHARE)
    grams = exchanged(packed_grams(flat), "band")
    points, coarse, own, edges, vectors, sides, green = density_parts(
        grams, flat, weight, din, gather, integers, sine, inverse, onto
    )
    rows = exchanged(coarse, "band")
    msg = exchanged(hartree_shares(rows, vectors, green, over_x, over_y, edges), "dom")
    dens, hart = final_parts(sides, msg, own, vectors)
    orbitals_out = jnp.transpose(points.reshape(PLANES, GG, NB), (2, 0, 1)).reshape(1, NB, PLANES, GG)
    density = jnp.transpose(dens, (1, 0, 2))
    hartree = jnp.transpose(hart, (1, 2, 0)).reshape(1, 1, CG, CZ)
    return orbitals_out, density, hartree


def solution(mesh):
    return jax.shard_map(
        body,
        mesh=mesh,
        in_specs=(
            P("dom", "band", None, None),
            P("dom", None, None),
            P("dom", "band", None),
            P(),
            P(),
            P(),
            P(),
        ),
        out_specs=(
            P("dom", None, "band", None),
            P("dom", "band", None),
            P("dom", "band", None, None),
        ),
        check_vma=False,
    )
```

```python
import functools
import numpy as np
import jax
import jax.numpy as jnp
from jax import lax
from jax.experimental import pallas as pl
from jax.experimental.pallas import tpu as pltpu
from jax.sharding import PartitionSpec as P

NB = 128
G = 24
GG = G * G
BUFFER = 6
CG = 8
CZ = 6
NZC = 192
DOMS = 32
BANDS = 8
LOCAL = NB // BANDS
PLANES = G // BANDS
ROW = 640
SHARE = 1792
PACKED = 72
HALF_ROW = GG // 2
EDGE = GG + HALF_ROW
POINTS = float(G * G * G)
FILTER_LOW = 1.0
FILTER_HIGH = 9.5
CENTER = 0.5 * (FILTER_HIGH + FILTER_LOW)
HALF = 0.5 * (FILTER_HIGH - FILTER_LOW)
HIGHEST = lax.Precision.HIGHEST
F32 = jnp.float32
EARLY = range(4)
LATE = range(4, 7)
INTERPRET = False
LIMIT = pltpu.CompilerParams(vmem_limit_bytes=16 << 20)


def tables():
    k = np.arange(CG)
    cosine = np.sqrt(2.0 / CG) * np.cos(np.pi * k[:, None] * (k[None, :] + 0.5) / CG)
    cosine[0] *= np.sqrt(0.5)
    r = np.arange(NZC)
    sine = np.zeros((NZC + 8, NZC))
    sine[:NZC] = np.sqrt(2.0 / (NZC + 1)) * np.sin(np.pi * (r[:, None] + 1) * (r[None, :] + 1) / (NZC + 1))
    level_xy = 4.0 * np.sin(0.5 * np.pi * k / CG) ** 2
    level_z = 4.0 * np.sin(0.5 * np.pi * (r + 1) / (NZC + 1)) ** 2
    inverse = 1.0 / (level_xy[:, None, None] + level_xy[None, :, None] + level_z[None, None, :])
    scale = 8.0 / float(NZC * NZC)
    onto_x = np.broadcast_to((scale * cosine.T)[:, :, None], (CG, CG, NZC))
    lane = np.arange(GG)
    gather = np.zeros((ROW, 256))
    for ky in range(CG):
        gather[lane, ky * G + lane % G] = cosine[ky, (lane // G) // 3]
    over_x = np.broadcast_to(cosine.T[:, :, None], (CG, CG, 256))
    over_y = np.broadcast_to(cosine[:, :, None], (CG, CG, 256))
    sine = np.stack([sine[CZ * place : CZ * place + 8] for place in range(DOMS)])
    as_f32 = lambda a: np.ascontiguousarray(a, dtype=np.float32)
    return tuple(as_f32(a) for a in (sine, inverse.reshape(CG * CG, NZC), onto_x, gather, over_x, over_y))


def halves(x):
    high = x.astype(jnp.bfloat16)
    return high, (x - high.astype(F32)).astype(jnp.bfloat16)


def dot3(x, y, dims=(((1,), (0,)), ((), ()))):
    x_high, x_low = halves(x)
    y_high, y_low = halves(y)
    dot = functools.partial(lax.dot_general, dimension_numbers=dims, preferred_element_type=F32)
    return dot(x_high, y_high) + (dot(x_high, y_low) + dot(x_low, y_high))


def rolled(x, shift):
    return pltpu.roll(x, shift % ROW, 1)


def lane_index(shape):
    lane = lax.broadcasted_iota(jnp.int32, shape, 1).astype(F32)
    return lane, lane - G * jnp.floor((lane + 0.5) * (1.0 / G))


def neighbour_matrix(mat_ref):
    mat_ref[...] = jnp.zeros_like(mat_ref)
    for t in range(ROW // 128):
        top, end = max(0, 128 * t - 32), min(ROW, 128 * t + 160)
        shape = (end - top, 128)
        row = lax.broadcasted_iota(jnp.int32, shape, 0) + top
        col = lax.broadcasted_iota(jnp.int32, (8, 128), 1) + 128 * t
        _, z = lane_index((8, ROW))
        z = z[:, 128 * t : 128 * (t + 1)]
        before = jnp.where(z > 0.5, col - 1, -ROW)[0:1]
        after = jnp.where(z < G - 1.5, col + 1, -ROW)[0:1]
        col = col[0:1]
        hit = (row == before) | (row == after) | (row == col - G) | (row == col + G)
        hit = hit & (row < GG) & (col < GG)
        mat_ref[top:end, 128 * t : 128 * (t + 1)] = jnp.where(hit, 1.0, 0.0).astype(jnp.bfloat16)


def filter_kernel(
    orb_ref, pot_ref, mat_ref, occ_ref, pos_ref, mix_ref, corr_ref,
    out_ref, weight_ref, int_ref, zero_ref, first_ref, side_ref, diag_ref,
):
    eye = lax.broadcasted_iota(jnp.int32, (NB, NB), 0) == lax.broadcasted_iota(jnp.int32, (NB, NB), 1)
    weight = jnp.sum(jnp.where(eye, occ_ref[...] * (1.0 / NB), 0.0), axis=1, keepdims=True)
    weight_ref[...] = jnp.broadcast_to(weight, (NB, 256))
    int_ref[...] = jnp.zeros((8, 128), jnp.int32)
    int_ref[0:1, :DOMS] = pos_ref[...]
    int_ref[1:2, :2] = mix_ref[...]
    int_ref[2:3, :BUFFER] = corr_ref[...]
    diag_ref[:, GG - 64 :] = jnp.zeros((G, 128), F32)
    zero_ref[:, :, GG - 64 :] = jnp.zeros((G, LOCAL, 128), F32)
    diag_ref[:, :GG] = (pot_ref[...] + (3.0 - CENTER)) * 2.0
    dot = functools.partial(jnp.dot, preferred_element_type=F32)

    def sum_sides(source, c):
        high, low = halves(source[8 * c : 8 * c + 8].reshape(8 * LOCAL, ROW))
        stack = jnp.concatenate([high, low], 0)
        for rows, cols in ((slice(0, 384), slice(0, 256)), (slice(128, 640), slice(256, 512)), (slice(384, 640), slice(512, 640))):
            both = dot(stack[:, rows], mat_ref[rows, cols])
            side = both[: 8 * LOCAL] + both[8 * LOCAL :]
            side_ref[8 * c : 8 * c + 8, :, cols] = side.reshape(8, LOCAL, cols.stop - cols.start)

    def applied(source, x):
        v = source[x]
        near = side_ref[x]
        if x > 0:
            near = near + source[x - 1]
        if x + 1 < G:
            near = near + source[x + 1]
        return diag_ref[x : x + 1] * v - near

    for c in range(3):
        for x in range(8 * c, 8 * c + 8):
            zero_ref[x, :, :GG] = orb_ref[:, x, :]
        sum_sides(zero_ref, c)
    for x in range(G):
        first_ref[x] = applied(zero_ref, x)
    for c in range(3):
        sum_sides(first_ref, c)
    for x in range(G):
        second = (0.5 / HALF**2) * applied(first_ref, x) - zero_ref[x]
        p = x % PLANES
        out_ref[x // PLANES, :, p * GG : (p + 1) * GG] = second[:, :GG]
        if p == PLANES - 1:
            out_ref[x // PLANES, :, PLANES * GG :] = jnp.zeros((LOCAL, SHARE - PLANES * GG), F32)


def filtered_shares(orbitals, potential, occupation, *integers):
    matrix = pl.pallas_call(
        neighbour_matrix,
        out_shape=jax.ShapeDtypeStruct((ROW, ROW), jnp.bfloat16),
        cost_estimate=pl.CostEstimate(flops=20_000_000_000, bytes_accessed=4_000_000, transcendentals=0),
        compiler_params=LIMIT,
        interpret=INTERPRET,
        name="matrix",
    )()
    return pl.pallas_call(
        filter_kernel,
        out_shape=(
            jax.ShapeDtypeStruct((BANDS, LOCAL, SHARE), F32),
            jax.ShapeDtypeStruct((NB, 256), F32),
            jax.ShapeDtypeStruct((8, 128), jnp.int32),
        ),
        scratch_shapes=[
            pltpu.VMEM((G, LOCAL, ROW), F32),
            pltpu.VMEM((G, LOCAL, ROW), F32),
            pltpu.VMEM((G, LOCAL, ROW), F32),
            pltpu.VMEM((G, ROW), F32),
        ],
        compiler_params=LIMIT,
        interpret=INTERPRET,
        name="filter",
    )(orbitals, potential, matrix, occupation, *integers)


def gram_kernel(f_ref, out_ref):
    high, low = halves(f_ref[...])
    both = lax.dot_general(
        high, jnp.concatenate([high, low], 0), (((1,), (1,)), ((), ())), preferred_element_type=F32
    )
    cross = both[:, NB:]
    raw = both[:, :NB] + (cross + cross.T)
    row = lax.broadcasted_iota(jnp.int32, (64, NB), 0)
    col = lax.broadcasted_iota(jnp.int32, (64, NB), 1)
    lower = pltpu.roll(raw[64:], 64, 1)
    packed = jnp.where(col >= row, raw[:64], lower)
    diag = jnp.sum(jnp.where(col == row + 64, raw[64:], 0.0), axis=0, keepdims=True)
    diag = jnp.broadcast_to(diag, (8, NB))
    for k in range(BANDS):
        out_ref[k, :64] = packed
        out_ref[k, 64:] = diag


def packed_grams(flat):
    return pl.pallas_call(
        gram_kernel,
        out_shape=jax.ShapeDtypeStruct((BANDS, PACKED, NB), F32),
        cost_estimate=pl.CostEstimate(flops=20_000_000_000, bytes_accessed=4_000_000, transcendentals=0),
        compiler_params=LIMIT,
        interpret=INTERPRET,
        name="gram",
    )(flat)


def lane_weights(int_ref, own, vec_ref):
    shape = (8, ROW)
    _, z = lane_index(shape)
    corr = jnp.zeros(shape, F32)
    for j in range(BUFFER):
        here = (jnp.abs(z - j) < 0.5) | (jnp.abs(z - (G - BUFFER + j)) < 0.5)
        corr = jnp.where(here, int_ref[2, j].astype(F32), corr)
    corr = corr * (1.0 / 16.0)
    fresh_weight = jnp.full(shape, int_ref[1, 0].astype(F32))
    input_weight = jnp.full(shape, int_ref[1, 1].astype(F32))
    both = fresh_weight + input_weight
    fresh_weight = fresh_weight / both
    input_weight = input_weight / both
    has_left = jnp.where(jnp.full(shape, own) > 0, 1.0, 0.0)
    has_right = jnp.where(jnp.full(shape, own) < DOMS - 1, 1.0, 0.0)
    low_z = z < BUFFER - 0.5
    high_z = z > G - BUFFER - 0.5
    from_left = jnp.where(low_z, corr * has_left, 0.0)
    from_right = jnp.where(high_z, (1.0 - corr) * has_right, 0.0)
    keep = 1.0 - from_left - from_right
    cell = 1.0 / 27.0
    vec_ref[0:1] = (cell * fresh_weight * jnp.where(high_z, corr * has_right, keep))[0:1]
    vec_ref[1:2] = jnp.where(high_z, 0.0, cell * input_weight)[0:1]
    vec_ref[2:3] = (fresh_weight * from_left)[0:1]
    vec_ref[3:4] = (fresh_weight * from_right)[0:1]
    vec_ref[4:5] = (fresh_weight * keep)[0:1]
    vec_ref[5:6] = input_weight[0:1]


def poisson_operator(int_ref, own, band, sine_ref, inverse_ref, onto_ref, side_ref, green_ref, left_ref, right_ref):
    for d in range(DOMS):
        place = jnp.full((1, 128), int_ref[0, d])
        side_ref[0, d : d + 1] = jnp.where(place == own - 1, 1.0, 0.0)
        side_ref[1, d : d + 1] = jnp.where(place == own + 1, 1.0, 0.0)
        right_ref[8 * d : 8 * d + 8] = sine_ref[int_ref[0, d]]
    mine = sine_ref[own]
    onto = onto_ref[band]
    for ky in range(CG):
        part = inverse_ref[8 * ky : 8 * ky + 8] * onto
        for j in range(8):
            at = ky * 64 + j * 8
            left_ref[at : at + 8] = part * mine[j : j + 1]
    green_ref[...] = dot3(left_ref[...], right_ref[...], (((1,), (1,)), ((), ())))


def write_points(chunks, f_ref, poly, out_ref, point_ref, sems):
    poly_high, poly_low = halves(poly)
    dot = functools.partial(jnp.dot, preferred_element_type=F32)
    copies = []
    for c in chunks:
        start, count = 256 * c, min(256, PLANES * GG - 256 * c)
        here = 256 * (c - chunks[0])
        for at in range(0, count, 128):
            high, low = halves(f_ref[:, start + at : start + at + 128].T)
            value = dot(high, poly_high) + (dot(high, poly_low) + dot(low, poly_high))
            point_ref[here + at : here + at + 128] = value
        copy = pltpu.make_async_copy(
            point_ref.at[pl.ds(here, count)], out_ref.at[pl.ds(start, count)], sems.at[c - chunks[0]]
        )
        copy.start()
        copies.append(copy)
    return copies


def density_kernel(
    g_ref, f_ref, weight_ref, din_ref, gather_ref, int_ref, sine_ref, inverse_ref, onto_ref,
    out_ref, coarse_ref, own_ref, edge_ref, vec_ref, side_ref, green_ref, poly_ref,
    point_ref, fresh_ref, rows_ref, left_ref, right_ref, scalar_ref, sems,
):
    scalars = pltpu.make_async_copy(int_ref, scalar_ref, sems.at[7])
    scalars.start()
    total = g_ref[0]
    for k in range(1, BANDS):
        total = total + g_ref[k]
    packed = total[:64]
    row = lax.broadcasted_iota(jnp.int32, (64, NB), 0)
    col = lax.broadcasted_iota(jnp.int32, (64, NB), 1)
    top = jnp.where(col > row, packed, jnp.where(col == row, 0.5 * packed, 0.0))
    low = pltpu.roll(jnp.where(col < row, packed, 0.0), 64, 1)
    low = low + jnp.where(col == row + 64, 0.5 * total[64:65], 0.0)
    half = jnp.concatenate([top, low], 0)
    raw = half + half.T
    norm = jnp.sqrt(jnp.sum(jnp.sum(raw * raw, axis=0, keepdims=True), axis=1, keepdims=True))
    a = raw / norm
    scaling = jnp.sqrt(POINTS / norm)
    eye = jnp.where(
        lax.broadcasted_iota(jnp.int32, (NB, NB), 0) == lax.broadcasted_iota(jnp.int32, (NB, NB), 1), 1.0, 0.0
    )
    square = dot3(a, a)
    tail = dot3(square, 0.0625 * square - 0.5625 * a)
    poly = scaling * (2.25 * eye + (1.6875 * square - 2.4375 * a) + tail)
    poly_high, poly_low = halves(poly)
    dot = functools.partial(jnp.dot, preferred_element_type=F32)

    copies = write_points(EARLY, f_ref, poly, out_ref, point_ref, sems)
    poly_ref[...] = poly

    both = jnp.concatenate([poly_high, poly_low], 1)
    for c in range(SHARE // 256):
        cols = slice(256 * c, 256 * (c + 1))
        high, low = halves(f_ref[:, cols])
        current = dot(both, jnp.concatenate([high, high], 0)) + dot(poly_high, low)
        line = jnp.sum(current * current * weight_ref[...], axis=0, keepdims=True)
        fresh_ref[:, cols] = jnp.broadcast_to(line, (8, 256))
    planes = [fresh_ref[:, p * GG : p * GG + ROW] for p in range(PLANES)]

    rows_ref[...] = jnp.zeros_like(rows_ref)
    rows_ref[0:8, :GG] = (planes[0] + planes[1] + planes[2])[:, :GG]
    rows_ref[8:9, :GG] = din_ref[0] + din_ref[1] + din_ref[2]
    cells = dot3(rows_ref[...], gather_ref[...])
    row = lax.broadcasted_iota(jnp.int32, (8, NB), 0)
    inputs = jnp.broadcast_to(cells[8:9], (8, 256))
    tile = jnp.where(row == 0, cells[:8, :128], cells[:8, 128:])
    tile = jnp.where(row == 2, inputs[:, :128], jnp.where(row == 3, inputs[:, 128:], tile))
    for k in range(BANDS):
        coarse_ref[k] = tile

    scalars.wait()
    if INTERPRET:
        dom, band = scalar_ref[3, 0], scalar_ref[3, 1]
    else:
        dom, band = lax.axis_index("dom"), lax.axis_index("band")
    own = scalar_ref[0, dom]
    lane_weights(scalar_ref, own, vec_ref)
    lane, z = lane_index((8, ROW))
    low_edge = (z < BUFFER - 0.5) & (lane < GG)
    high_edge = (z > G - BUFFER - 0.5) & (lane < GG)
    middle = (z > BUFFER - 0.5) & (z < G - BUFFER - 0.5)
    edges = []
    for p in range(PLANES):
        own_ref[p] = vec_ref[4:5, :GG] * planes[p][0:1, :GG] + vec_ref[5:6, :GG] * din_ref[p]
        edges.append((jnp.where(low_edge, planes[p], 0.0), jnp.where(high_edge, planes[p], 0.0)))
    first = (edges[0][0] + edges[0][1]) + (rolled(edges[1][0], 12) + rolled(edges[1][1], -12))
    last = edges[2][0] + edges[2][1]
    moved = rolled(edges[2][0], 12 - HALF_ROW) + rolled(edges[2][1], -12 - HALF_ROW)
    last = jnp.where(lane < HALF_ROW, jnp.where(middle, moved, last), 0.0)
    first = first + rolled(jnp.where(lane < 64, last, 0.0), GG)
    rest = rolled(last, -64)
    edge_ref[0:1] = jnp.zeros((1, 128), F32)
    for t in range(7):
        source, at = (first, 128 * t) if t < 5 else (rest, 128 * (t - 5))
        edge_ref[t + 1 : t + 2] = source[0:1, at : at + 128]
    poisson_operator(
        scalar_ref, own, band, sine_ref, inverse_ref, onto_ref, side_ref, green_ref, left_ref, right_ref
    )
    for copy in copies:
        copy.wait()


def density_parts(grams, flat, weight, din, gather, integers, sine, inverse, onto):
    if INTERPRET:
        axes = jnp.stack([lax.axis_index("dom"), lax.axis_index("band")])
        integers = integers.at[3, :2].set(axes)
    vmem = pl.BlockSpec(memory_space=pltpu.VMEM)
    return pl.pallas_call(
        density_kernel,
        out_shape=(
            jax.ShapeDtypeStruct((PLANES * GG, NB), F32),
            jax.ShapeDtypeStruct((BANDS, 8, 128), F32),
            jax.ShapeDtypeStruct((PLANES, 1, GG), F32),
            jax.ShapeDtypeStruct((8, 128), F32),
            jax.ShapeDtypeStruct((8, ROW), F32),
            jax.ShapeDtypeStruct((2, DOMS, 128), F32),
            jax.ShapeDtypeStruct((512, 256), F32),
            jax.ShapeDtypeStruct((NB, NB), F32),
        ),
        in_specs=[vmem] * 9,
        out_specs=(pl.BlockSpec(memory_space=pltpu.HBM), *[vmem] * 7),
        scratch_shapes=[
            pltpu.VMEM((256 * len(EARLY), NB), F32),
            pltpu.VMEM((8, SHARE), F32),
            pltpu.VMEM((16, ROW), F32),
            pltpu.VMEM((512, NZC), F32),
            pltpu.VMEM((256, NZC), F32),
            pltpu.SMEM((8, 128), jnp.int32),
            pltpu.SemaphoreType.DMA((8,)),
        ],
        compiler_params=LIMIT,
        interpret=INTERPRET,
        name="density",
    )(grams, flat, weight, din, gather, integers, sine, inverse, onto)


def share_kernel(rows_ref, vec_ref, green_ref, over_x_ref, over_y_ref, edge_ref, out_ref, turn_ref, line_ref):
    fresh = jnp.concatenate([rows_ref[:, 0, :], rows_ref[:, 1, :]], 1)
    inputs = jnp.concatenate([rows_ref[:, 2, :], rows_ref[:, 3, :]], 1)
    cells = fresh * vec_ref[0:1, :256] + inputs * vec_ref[1:2, :256]
    cells = cells + (pltpu.roll(cells, 255, 1) + pltpu.roll(cells, 254, 1))
    modes = over_x_ref[0] * cells[0:1]
    for x in range(1, CG):
        modes = modes + over_x_ref[x] * cells[x : x + 1]
    cells = jnp.zeros((8, 256), F32)
    for ky in range(CG):
        acc = jnp.zeros((8, 256), F32)
        for j in range(8):
            at = ky * 8 + j
            acc = acc + jnp.broadcast_to(modes[:, G * ky + 3 * j : G * ky + 3 * j + 1], (8, 256)) * green_ref[8 * at : 8 * at + 8]
        cells = cells + over_y_ref[ky] * jnp.sum(acc, axis=0, keepdims=True)
    turn_ref[...] = jnp.concatenate([cells, jnp.zeros((120, 256), F32)], 0).T
    line_ref[...] = jnp.zeros_like(line_ref)
    for j in range(CZ):
        line_ref[:, 8 * j : 8 * j + 8] = turn_ref[pl.ds(j, DOMS, stride=8), :][:, :8]
    head = lax.broadcasted_iota(jnp.int32, (8, 128), 0) == 0
    edge = edge_ref[...]
    for d in range(DOMS):
        out_ref[d] = jnp.where(head, line_ref[d : d + 1], edge)


def hartree_shares(rows, vectors, green, over_x, over_y, edges):
    return pl.pallas_call(
        share_kernel,
        out_shape=jax.ShapeDtypeStruct((DOMS, 8, 128), F32),
        scratch_shapes=[pltpu.VMEM((256, 128), F32), pltpu.VMEM((DOMS, 128), F32)],
        compiler_params=LIMIT,
        interpret=INTERPRET,
        name="share",
    )(rows, vectors, green, over_x, over_y, edges)


def final_kernel(
    side_ref, msg_ref, own_ref, vec_ref, f_ref, poly_ref, early_ref, dens_ref, hart_ref, out_ref, point_ref, sems
):
    copies = write_points(LATE, f_ref, poly_ref[...], out_ref, point_ref, sems)
    total = msg_ref[0]
    for d in range(1, DOMS):
        total = total + msg_ref[d]
    for j in range(CZ):
        hart_ref[j] = total[0:1, 8 * j : 8 * j + 8]
    lane = lax.broadcasted_iota(jnp.int32, (8, ROW), 1)

    def picked(side):
        tile = jnp.zeros((8, 128), F32)
        for d in range(DOMS):
            tile = tile + side_ref[side, d : d + 1] * msg_ref[d]
        return tile

    def rows(tile):
        spread = [jnp.broadcast_to(tile[t + 1 : t + 2], (8, 128)) for t in range(7)]
        front = jnp.concatenate(spread[:5], 1)
        back = jnp.concatenate(spread[4:] + spread[5:], 1)
        return front, rolled(back, -64)

    left0, left2 = rows(picked(0))
    right0, right2 = rows(picked(1))
    far = G - BUFFER
    left_last = jnp.where(lane < HALF_ROW, rolled(left2, -far), rolled(left2, HALF_ROW + 12 - far))
    right_last = jnp.where(lane < HALF_ROW, rolled(right2, far), rolled(right2, HALF_ROW - 12 + far))
    left_part = (rolled(left0, -far), rolled(left0, -6), left_last)
    right_part = (rolled(right0, far), rolled(right0, 6), right_last)
    for p in range(PLANES):
        mixed = own_ref[p] + vec_ref[2:3, :GG] * left_part[p][0:1, :GG]
        dens_ref[p] = mixed + vec_ref[3:4, :GG] * right_part[p][0:1, :GG]
    for copy in copies:
        copy.wait()


def final_parts(sides, msg, own, vectors, flat, poly, points):
    vmem = pl.BlockSpec(memory_space=pltpu.VMEM)
    hbm = pl.BlockSpec(memory_space=pltpu.HBM)
    return pl.pallas_call(
        final_kernel,
        out_shape=(
            jax.ShapeDtypeStruct((PLANES, 1, GG), F32),
            jax.ShapeDtypeStruct((CZ, 1, CG), F32),
            jax.ShapeDtypeStruct((PLANES * GG, NB), F32),
        ),
        in_specs=[vmem] * 6 + [hbm],
        out_specs=(vmem, vmem, hbm),
        input_output_aliases={6: 2},
        scratch_shapes=[pltpu.VMEM((256 * len(LATE), NB), F32), pltpu.SemaphoreType.DMA((len(LATE),))],
        compiler_params=LIMIT,
        interpret=INTERPRET,
        name="final",
    )(sides, msg, own, vectors, flat, poly, points)


def exchanged(x, axis):
    return lax.all_to_all(x, axis, split_axis=0, concat_axis=0, tiled=True)


def body(orbitals, potential, density_in, occupation, position, mixing, correlation_weight):
    sine, inverse, onto, gather, over_x, over_y = tables()
    din = jnp.transpose(density_in, (1, 0, 2))
    small = [v.reshape(1, -1) for v in (occupation, position, mixing, correlation_weight)]
    filtered, weight, integers = filtered_shares(orbitals[0], potential[0], *small)
    flat = exchanged(filtered, "band").reshape(NB, SHARE)
    grams = exchanged(packed_grams(flat), "band")
    points, coarse, own, edges, vectors, sides, green, poly = density_parts(
        grams, flat, weight, din, gather, integers, sine, inverse, onto
    )
    rows = exchanged(coarse, "band")
    msg = exchanged(hartree_shares(rows, vectors, green, over_x, over_y, edges), "dom")
    dens, hart, points = final_parts(sides, msg, own, vectors, flat, poly, points)
    orbitals_out = jnp.transpose(points.reshape(PLANES, GG, NB), (2, 0, 1)).reshape(1, NB, PLANES, GG)
    density = jnp.transpose(dens, (1, 0, 2))
    hartree = jnp.transpose(hart, (1, 2, 0)).reshape(1, 1, CG, CZ)
    return orbitals_out, density, hartree


def solution(mesh):
    return jax.shard_map(
        body,
        mesh=mesh,
        in_specs=(
            P("dom", "band", None, None),
            P("dom", None, None),
            P("dom", "band", None),
            P(),
            P(),
            P(),
            P(),
        ),
        out_specs=(
            P("dom", None, "band", None),
            P("dom", "band", None),
            P("dom", "band", None, None),
        ),
        check_vma=False,
    )
```

```python
import functools
import numpy as np
import jax
import jax.numpy as jnp
from jax import lax
from jax.experimental import pallas as pl
from jax.experimental.pallas import tpu as pltpu
from jax.sharding import PartitionSpec as P

NB = 128
G = 24
GG = G * G
BUFFER = 6
CG = 8
CZ = 6
NZC = 192
DOMS = 32
BANDS = 8
LOCAL = NB // BANDS
PLANES = G // BANDS
ROW = 640
SHARE = 1792
PACKED = 72
HALF_ROW = GG // 2
EDGE = GG + HALF_ROW
POINTS = float(G * G * G)
FILTER_LOW = 1.0
FILTER_HIGH = 9.5
CENTER = 0.5 * (FILTER_HIGH + FILTER_LOW)
HALF = 0.5 * (FILTER_HIGH - FILTER_LOW)
HIGHEST = lax.Precision.HIGHEST
F32 = jnp.float32
INTERPRET = False
LIMIT = pltpu.CompilerParams(vmem_limit_bytes=16 << 20)


def tables():
    k = np.arange(CG)
    cosine = np.sqrt(2.0 / CG) * np.cos(np.pi * k[:, None] * (k[None, :] + 0.5) / CG)
    cosine[0] *= np.sqrt(0.5)
    r = np.arange(NZC)
    sine = np.zeros((NZC + 8, NZC))
    sine[:NZC] = np.sqrt(2.0 / (NZC + 1)) * np.sin(np.pi * (r[:, None] + 1) * (r[None, :] + 1) / (NZC + 1))
    level_xy = 4.0 * np.sin(0.5 * np.pi * k / CG) ** 2
    level_z = 4.0 * np.sin(0.5 * np.pi * (r + 1) / (NZC + 1)) ** 2
    inverse = 1.0 / (level_xy[:, None, None] + level_xy[None, :, None] + level_z[None, None, :])
    scale = 8.0 / float(NZC * NZC)
    onto_x = np.broadcast_to((scale * cosine.T)[:, :, None], (CG, CG, NZC))
    lane = np.arange(GG)
    gather = np.zeros((ROW, 256))
    for ky in range(CG):
        gather[lane, ky * G + lane % G] = cosine[ky, (lane // G) // 3]
    over_x = np.broadcast_to(cosine.T[:, :, None], (CG, CG, 256))
    over_y = np.broadcast_to(cosine[:, :, None], (CG, CG, 256))
    sine = np.stack([sine[CZ * place : CZ * place + 8] for place in range(DOMS)])
    as_f32 = lambda a: np.ascontiguousarray(a, dtype=np.float32)
    return tuple(as_f32(a) for a in (sine, inverse.reshape(CG * CG, NZC), onto_x, gather, over_x, over_y))


def halves(x):
    high = x.astype(jnp.bfloat16)
    return high, (x - high.astype(F32)).astype(jnp.bfloat16)


def dot3(x, y, dims=(((1,), (0,)), ((), ()))):
    x_high, x_low = halves(x)
    y_high, y_low = halves(y)
    dot = functools.partial(lax.dot_general, dimension_numbers=dims, preferred_element_type=F32)
    return dot(x_high, y_high) + (dot(x_high, y_low) + dot(x_low, y_high))


def rolled(x, shift):
    return pltpu.roll(x, shift % ROW, 1)


def lane_index(shape):
    lane = lax.broadcasted_iota(jnp.int32, shape, 1).astype(F32)
    return lane, lane - G * jnp.floor((lane + 0.5) * (1.0 / G))


def neighbour_matrix(mat_ref):
    mat_ref[...] = jnp.zeros_like(mat_ref)
    for t in range(ROW // 128):
        top, end = max(0, 128 * t - 32), min(ROW, 128 * t + 160)
        shape = (end - top, 128)
        row = lax.broadcasted_iota(jnp.int32, shape, 0) + top
        col = lax.broadcasted_iota(jnp.int32, (8, 128), 1) + 128 * t
        _, z = lane_index((8, ROW))
        z = z[:, 128 * t : 128 * (t + 1)]
        before = jnp.where(z > 0.5, col - 1, -ROW)[0:1]
        after = jnp.where(z < G - 1.5, col + 1, -ROW)[0:1]
        col = col[0:1]
        hit = (row == before) | (row == after) | (row == col - G) | (row == col + G)
        hit = hit & (row < GG) & (col < GG)
        mat_ref[top:end, 128 * t : 128 * (t + 1)] = jnp.where(hit, 1.0, 0.0).astype(jnp.bfloat16)


def filter_kernel(
    orb_ref, pot_ref, mat_ref, occ_ref, pos_ref, mix_ref, corr_ref,
    out_ref, weight_ref, int_ref, zero_ref, first_ref, side_ref, diag_ref,
):
    eye = lax.broadcasted_iota(jnp.int32, (NB, NB), 0) == lax.broadcasted_iota(jnp.int32, (NB, NB), 1)
    weight = jnp.sum(jnp.where(eye, occ_ref[...] * (1.0 / NB), 0.0), axis=1, keepdims=True)
    weight_ref[...] = jnp.broadcast_to(weight, (NB, 256))
    int_ref[...] = jnp.zeros((8, 128), jnp.int32)
    int_ref[0:1, :DOMS] = pos_ref[...]
    int_ref[1:2, :2] = mix_ref[...]
    int_ref[2:3, :BUFFER] = corr_ref[...]
    diag_ref[:, GG - 64 :] = jnp.zeros((G, 128), F32)
    zero_ref[:, :, GG - 64 :] = jnp.zeros((G, LOCAL, 128), F32)
    diag_ref[:, :GG] = (pot_ref[...] + (3.0 - CENTER)) * 2.0
    dot = functools.partial(jnp.dot, preferred_element_type=F32)

    def sum_sides(source, c):
        high, low = halves(source[8 * c : 8 * c + 8].reshape(8 * LOCAL, ROW))
        stack = jnp.concatenate([high, low], 0)
        for rows, cols in ((slice(0, 384), slice(0, 256)), (slice(128, 640), slice(256, 512)), (slice(384, 640), slice(512, 640))):
            both = dot(stack[:, rows], mat_ref[rows, cols])
            side = both[: 8 * LOCAL] + both[8 * LOCAL :]
            side_ref[8 * c : 8 * c + 8, :, cols] = side.reshape(8, LOCAL, cols.stop - cols.start)

    def applied(source, x):
        v = source[x]
        near = side_ref[x]
        if x > 0:
            near = near + source[x - 1]
        if x + 1 < G:
            near = near + source[x + 1]
        return diag_ref[x : x + 1] * v - near

    for c in range(3):
        for x in range(8 * c, 8 * c + 8):
            zero_ref[x, :, :GG] = orb_ref[:, x, :]
        sum_sides(zero_ref, c)
    for x in range(G):
        first_ref[x] = applied(zero_ref, x)
    for c in range(3):
        sum_sides(first_ref, c)
    for x in range(G):
        second = (0.5 / HALF**2) * applied(first_ref, x) - zero_ref[x]
        p = x % PLANES
        out_ref[x // PLANES, :, p * GG : (p + 1) * GG] = second[:, :GG]
        if p == PLANES - 1:
            out_ref[x // PLANES, :, PLANES * GG :] = jnp.zeros((LOCAL, SHARE - PLANES * GG), F32)


def filtered_shares(orbitals, potential, occupation, *integers):
    matrix = pl.pallas_call(
        neighbour_matrix,
        out_shape=jax.ShapeDtypeStruct((ROW, ROW), jnp.bfloat16),
        cost_estimate=pl.CostEstimate(flops=20_000_000_000, bytes_accessed=4_000_000, transcendentals=0),
        compiler_params=LIMIT,
        interpret=INTERPRET,
        name="matrix",
    )()
    return pl.pallas_call(
        filter_kernel,
        out_shape=(
            jax.ShapeDtypeStruct((BANDS, LOCAL, SHARE), F32),
            jax.ShapeDtypeStruct((NB, 256), F32),
            jax.ShapeDtypeStruct((8, 128), jnp.int32),
        ),
        scratch_shapes=[
            pltpu.VMEM((G, LOCAL, ROW), F32),
            pltpu.VMEM((G, LOCAL, ROW), F32),
            pltpu.VMEM((G, LOCAL, ROW), F32),
            pltpu.VMEM((G, ROW), F32),
        ],
        compiler_params=LIMIT,
        interpret=INTERPRET,
        name="filter",
    )(orbitals, potential, matrix, occupation, *integers)


def gram_kernel(f_ref, out_ref):
    high, low = halves(f_ref[...])
    both = lax.dot_general(
        high, jnp.concatenate([high, low], 0), (((1,), (1,)), ((), ())), preferred_element_type=F32
    )
    cross = both[:, NB:]
    raw = both[:, :NB] + (cross + cross.T)
    row = lax.broadcasted_iota(jnp.int32, (64, NB), 0)
    col = lax.broadcasted_iota(jnp.int32, (64, NB), 1)
    lower = pltpu.roll(raw[64:], 64, 1)
    packed = jnp.where(col >= row, raw[:64], lower)
    diag = jnp.sum(jnp.where(col == row + 64, raw[64:], 0.0), axis=0, keepdims=True)
    diag = jnp.broadcast_to(diag, (8, NB))
    for k in range(BANDS):
        out_ref[k, :64] = packed
        out_ref[k, 64:] = diag


def packed_grams(flat):
    return pl.pallas_call(
        gram_kernel,
        out_shape=jax.ShapeDtypeStruct((BANDS, PACKED, NB), F32),
        cost_estimate=pl.CostEstimate(flops=20_000_000_000, bytes_accessed=4_000_000, transcendentals=0),
        compiler_params=LIMIT,
        interpret=INTERPRET,
        name="gram",
    )(flat)


def lane_weights(int_ref, own, vec_ref):
    shape = (8, ROW)
    _, z = lane_index(shape)
    corr = jnp.zeros(shape, F32)
    for j in range(BUFFER):
        here = (jnp.abs(z - j) < 0.5) | (jnp.abs(z - (G - BUFFER + j)) < 0.5)
        corr = jnp.where(here, int_ref[2, j].astype(F32), corr)
    corr = corr * (1.0 / 16.0)
    fresh_weight = jnp.full(shape, int_ref[1, 0].astype(F32))
    input_weight = jnp.full(shape, int_ref[1, 1].astype(F32))
    both = fresh_weight + input_weight
    fresh_weight = fresh_weight / both
    input_weight = input_weight / both
    has_left = jnp.where(jnp.full(shape, own) > 0, 1.0, 0.0)
    has_right = jnp.where(jnp.full(shape, own) < DOMS - 1, 1.0, 0.0)
    low_z = z < BUFFER - 0.5
    high_z = z > G - BUFFER - 0.5
    from_left = jnp.where(low_z, corr * has_left, 0.0)
    from_right = jnp.where(high_z, (1.0 - corr) * has_right, 0.0)
    keep = 1.0 - from_left - from_right
    cell = 1.0 / 27.0
    vec_ref[0:1] = (cell * fresh_weight * jnp.where(high_z, corr * has_right, keep))[0:1]
    vec_ref[1:2] = jnp.where(high_z, 0.0, cell * input_weight)[0:1]
    vec_ref[2:3] = (fresh_weight * from_left)[0:1]
    vec_ref[3:4] = (fresh_weight * from_right)[0:1]
    vec_ref[4:5] = (fresh_weight * keep)[0:1]
    vec_ref[5:6] = input_weight[0:1]


def poisson_tables(int_ref, own, band, sine_ref, inverse_ref, onto_ref, side_ref, mine_ref, weigh_ref, right_ref, all_ref):
    for d in range(DOMS):
        place = jnp.full((1, 128), int_ref[0, d])
        side_ref[0, d : d + 1] = jnp.where(place == own - 1, 1.0, 0.0)
        side_ref[1, d : d + 1] = jnp.where(place == own + 1, 1.0, 0.0)
        all_ref[8 * d : 8 * d + 8] = sine_ref[int_ref[0, d]]
    mine_ref[...] = sine_ref[own]
    onto = onto_ref[band]
    for ky in range(CG):
        weigh_ref[8 * ky : 8 * ky + 8] = inverse_ref[8 * ky : 8 * ky + 8] * onto
    high, low = halves(all_ref[...])
    right_ref[0] = high
    right_ref[1] = low


def density_kernel(
    g_ref, f_ref, weight_ref, din_ref, gather_ref, int_ref, sine_ref, inverse_ref, onto_ref,
    out_ref, coarse_ref, own_ref, edge_ref, vec_ref, side_ref, mine_ref, weigh_ref, right_ref,
    point_ref, fresh_ref, rows_ref, all_ref, scalar_ref, sems,
):
    scalars = pltpu.make_async_copy(int_ref, scalar_ref, sems.at[7])
    scalars.start()
    total = g_ref[0]
    for k in range(1, BANDS):
        total = total + g_ref[k]
    packed = total[:64]
    row = lax.broadcasted_iota(jnp.int32, (64, NB), 0)
    col = lax.broadcasted_iota(jnp.int32, (64, NB), 1)
    top = jnp.where(col > row, packed, jnp.where(col == row, 0.5 * packed, 0.0))
    low = pltpu.roll(jnp.where(col < row, packed, 0.0), 64, 1)
    low = low + jnp.where(col == row + 64, 0.5 * total[64:65], 0.0)
    half = jnp.concatenate([top, low], 0)
    raw = half + half.T
    norm = jnp.sqrt(jnp.sum(jnp.sum(raw * raw, axis=0, keepdims=True), axis=1, keepdims=True))
    a = raw / norm
    scaling = jnp.sqrt(POINTS / norm)
    eye = jnp.where(
        lax.broadcasted_iota(jnp.int32, (NB, NB), 0) == lax.broadcasted_iota(jnp.int32, (NB, NB), 1), 1.0, 0.0
    )
    square = dot3(a, a)
    tail = dot3(square, 0.0625 * square - 0.5625 * a)
    poly = scaling * (2.25 * eye + (1.6875 * square - 2.4375 * a) + tail)
    poly_high, poly_low = halves(poly)
    dot = functools.partial(jnp.dot, preferred_element_type=F32)

    copies = []
    for c in range(7):
        start, count = 256 * c, min(256, PLANES * GG - 256 * c)
        for at in range(start, start + count, 128):
            high, low = halves(f_ref[:, at : at + 128].T)
            value = dot(high, poly_high) + (dot(high, poly_low) + dot(low, poly_high))
            point_ref[at : at + 128] = value
        part = pl.ds(start, count)
        copies.append(pltpu.make_async_copy(point_ref.at[part], out_ref.at[part], sems.at[c]))
        copies[-1].start()

    both = jnp.concatenate([poly_high, poly_low], 1)
    for c in range(SHARE // 256):
        cols = slice(256 * c, 256 * (c + 1))
        high, low = halves(f_ref[:, cols])
        current = dot(both, jnp.concatenate([high, high], 0)) + dot(poly_high, low)
        line = jnp.sum(current * current * weight_ref[...], axis=0, keepdims=True)
        fresh_ref[:, cols] = jnp.broadcast_to(line, (8, 256))
    planes = [fresh_ref[:, p * GG : p * GG + ROW] for p in range(PLANES)]

    rows_ref[...] = jnp.zeros_like(rows_ref)
    rows_ref[0:8, :GG] = (planes[0] + planes[1] + planes[2])[:, :GG]
    rows_ref[8:9, :GG] = din_ref[0] + din_ref[1] + din_ref[2]
    cells = dot3(rows_ref[...], gather_ref[...])
    row = lax.broadcasted_iota(jnp.int32, (8, NB), 0)
    inputs = jnp.broadcast_to(cells[8:9], (8, 256))
    tile = jnp.where(row == 0, cells[:8, :128], cells[:8, 128:])
    tile = jnp.where(row == 2, inputs[:, :128], jnp.where(row == 3, inputs[:, 128:], tile))
    for k in range(BANDS):
        coarse_ref[k] = tile

    scalars.wait()
    if INTERPRET:
        dom, band = scalar_ref[3, 0], scalar_ref[3, 1]
    else:
        dom, band = lax.axis_index("dom"), lax.axis_index("band")
    own = scalar_ref[0, dom]
    lane_weights(scalar_ref, own, vec_ref)
    lane, z = lane_index((8, ROW))
    low_edge = (z < BUFFER - 0.5) & (lane < GG)
    high_edge = (z > G - BUFFER - 0.5) & (lane < GG)
    middle = (z > BUFFER - 0.5) & (z < G - BUFFER - 0.5)
    edges = []
    for p in range(PLANES):
        own_ref[p] = vec_ref[4:5, :GG] * planes[p][0:1, :GG] + vec_ref[5:6, :GG] * din_ref[p]
        edges.append((jnp.where(low_edge, planes[p], 0.0), jnp.where(high_edge, planes[p], 0.0)))
    first = (edges[0][0] + edges[0][1]) + (rolled(edges[1][0], 12) + rolled(edges[1][1], -12))
    last = edges[2][0] + edges[2][1]
    moved = rolled(edges[2][0], 12 - HALF_ROW) + rolled(edges[2][1], -12 - HALF_ROW)
    last = jnp.where(lane < HALF_ROW, jnp.where(middle, moved, last), 0.0)
    first = first + rolled(jnp.where(lane < 64, last, 0.0), GG)
    rest = rolled(last, -64)
    edge_ref[0:1] = jnp.zeros((1, 128), F32)
    for t in range(7):
        source, at = (first, 128 * t) if t < 5 else (rest, 128 * (t - 5))
        edge_ref[t + 1 : t + 2] = source[0:1, at : at + 128]
    poisson_tables(
        scalar_ref, own, band, sine_ref, inverse_ref, onto_ref, side_ref, mine_ref, weigh_ref, right_ref, all_ref
    )
    for copy in copies:
        copy.wait()


def density_parts(grams, flat, weight, din, gather, integers, sine, inverse, onto):
    if INTERPRET:
        axes = jnp.stack([lax.axis_index("dom"), lax.axis_index("band")])
        integers = integers.at[3, :2].set(axes)
    vmem = pl.BlockSpec(memory_space=pltpu.VMEM)
    return pl.pallas_call(
        density_kernel,
        out_shape=(
            jax.ShapeDtypeStruct((PLANES * GG, NB), F32),
            jax.ShapeDtypeStruct((BANDS, 8, 128), F32),
            jax.ShapeDtypeStruct((PLANES, 1, GG), F32),
            jax.ShapeDtypeStruct((8, 128), F32),
            jax.ShapeDtypeStruct((8, ROW), F32),
            jax.ShapeDtypeStruct((2, DOMS, 128), F32),
            jax.ShapeDtypeStruct((8, NZC), F32),
            jax.ShapeDtypeStruct((CG * CG, NZC), F32),
            jax.ShapeDtypeStruct((2, 256, NZC), jnp.bfloat16),
        ),
        in_specs=[vmem] * 9,
        out_specs=(pl.BlockSpec(memory_space=pltpu.HBM), *[vmem] * 8),
        scratch_shapes=[
            pltpu.VMEM((SHARE, NB), F32),
            pltpu.VMEM((8, SHARE), F32),
            pltpu.VMEM((16, ROW), F32),
            pltpu.VMEM((256, NZC), F32),
            pltpu.SMEM((8, 128), jnp.int32),
            pltpu.SemaphoreType.DMA((8,)),
        ],
        compiler_params=LIMIT,
        interpret=INTERPRET,
        name="density",
    )(grams, flat, weight, din, gather, integers, sine, inverse, onto)


def share_kernel(
    rows_ref, vec_ref, mine_ref, weigh_ref, right_ref, over_x_ref, over_y_ref, edge_ref, out_ref, turn_ref, line_ref
):
    fresh = jnp.concatenate([rows_ref[:, 0, :], rows_ref[:, 1, :]], 1)
    inputs = jnp.concatenate([rows_ref[:, 2, :], rows_ref[:, 3, :]], 1)
    cells = fresh * vec_ref[0:1, :256] + inputs * vec_ref[1:2, :256]
    cells = cells + (pltpu.roll(cells, 255, 1) + pltpu.roll(cells, 254, 1))
    modes = over_x_ref[0] * cells[0:1]
    for x in range(1, CG):
        modes = modes + over_x_ref[x] * cells[x : x + 1]
    spectrum = jnp.zeros((8, NZC), F32)
    for ky in range(CG):
        acc = jnp.zeros((8, NZC), F32)
        for j in range(8):
            at = G * ky + 3 * j
            acc = acc + jnp.broadcast_to(modes[:, at : at + 1], (8, NZC)) * mine_ref[j : j + 1]
        acc = acc * weigh_ref[8 * ky : 8 * ky + 8]
        spectrum = spectrum + over_y_ref[ky, :, :NZC] * jnp.sum(acc, axis=0, keepdims=True)
    high, low = halves(spectrum)
    dot = functools.partial(
        lax.dot_general, dimension_numbers=(((1,), (1,)), ((), ())), preferred_element_type=F32
    )
    cells = dot(high, right_ref[0]) + (dot(high, right_ref[1]) + dot(low, right_ref[0]))
    turn_ref[...] = jnp.concatenate([cells, jnp.zeros((120, 256), F32)], 0).T
    line_ref[...] = jnp.zeros_like(line_ref)
    for j in range(CZ):
        line_ref[:, 8 * j : 8 * j + 8] = turn_ref[pl.ds(j, DOMS, stride=8), :][:, :8]
    head = lax.broadcasted_iota(jnp.int32, (8, 128), 0) == 0
    edge = edge_ref[...]
    for d in range(DOMS):
        out_ref[d] = jnp.where(head, line_ref[d : d + 1], edge)


def hartree_shares(rows, vectors, mine, weigh, right, over_x, over_y, edges):
    return pl.pallas_call(
        share_kernel,
        out_shape=jax.ShapeDtypeStruct((DOMS, 8, 128), F32),
        scratch_shapes=[pltpu.VMEM((256, 128), F32), pltpu.VMEM((DOMS, 128), F32)],
        compiler_params=LIMIT,
        interpret=INTERPRET,
        name="share",
    )(rows, vectors, mine, weigh, right, over_x, over_y, edges)


def final_kernel(side_ref, msg_ref, own_ref, vec_ref, dens_ref, hart_ref):
    total = msg_ref[0]
    for d in range(1, DOMS):
        total = total + msg_ref[d]
    for j in range(CZ):
        hart_ref[j] = total[0:1, 8 * j : 8 * j + 8]
    lane = lax.broadcasted_iota(jnp.int32, (8, ROW), 1)

    def picked(side):
        tile = jnp.zeros((8, 128), F32)
        for d in range(DOMS):
            tile = tile + side_ref[side, d : d + 1] * msg_ref[d]
        return tile

    def rows(tile):
        spread = [jnp.broadcast_to(tile[t + 1 : t + 2], (8, 128)) for t in range(7)]
        front = jnp.concatenate(spread[:5], 1)
        back = jnp.concatenate(spread[4:] + spread[5:], 1)
        return front, rolled(back, -64)

    left0, left2 = rows(picked(0))
    right0, right2 = rows(picked(1))
    far = G - BUFFER
    left_last = jnp.where(lane < HALF_ROW, rolled(left2, -far), rolled(left2, HALF_ROW + 12 - far))
    right_last = jnp.where(lane < HALF_ROW, rolled(right2, far), rolled(right2, HALF_ROW - 12 + far))
    left_part = (rolled(left0, -far), rolled(left0, -6), left_last)
    right_part = (rolled(right0, far), rolled(right0, 6), right_last)
    for p in range(PLANES):
        mixed = own_ref[p] + vec_ref[2:3, :GG] * left_part[p][0:1, :GG]
        dens_ref[p] = mixed + vec_ref[3:4, :GG] * right_part[p][0:1, :GG]


def final_parts(sides, msg, own, vectors):
    return pl.pallas_call(
        final_kernel,
        out_shape=(
            jax.ShapeDtypeStruct((PLANES, 1, GG), F32),
            jax.ShapeDtypeStruct((CZ, 1, CG), F32),
        ),
        compiler_params=LIMIT,
        interpret=INTERPRET,
        name="final",
    )(sides, msg, own, vectors)


def exchanged(x, axis):
    return lax.all_to_all(x, axis, split_axis=0, concat_axis=0, tiled=True)


def body(orbitals, potential, density_in, occupation, position, mixing, correlation_weight):
    sine, inverse, onto, gather, over_x, over_y = tables()
    din = jnp.transpose(density_in, (1, 0, 2))
    small = [v.reshape(1, -1) for v in (occupation, position, mixing, correlation_weight)]
    filtered, weight, integers = filtered_shares(orbitals[0], potential[0], *small)
    flat = exchanged(filtered, "band").reshape(NB, SHARE)
    grams = exchanged(packed_grams(flat), "band")
    points, coarse, own, edges, vectors, sides, mine, weigh, right = density_parts(
        grams, flat, weight, din, gather, integers, sine, inverse, onto
    )
    rows = exchanged(coarse, "band")
    msg = exchanged(hartree_shares(rows, vectors, mine, weigh, right, over_x, over_y, edges), "dom")
    dens, hart = final_parts(sides, msg, own, vectors)
    orbitals_out = jnp.transpose(points.reshape(PLANES, GG, NB), (2, 0, 1)).reshape(1, NB, PLANES, GG)
    density = jnp.transpose(dens, (1, 0, 2))
    hartree = jnp.transpose(hart, (1, 2, 0)).reshape(1, 1, CG, CZ)
    return orbitals_out, density, hartree


def solution(mesh):
    return jax.shard_map(
        body,
        mesh=mesh,
        in_specs=(
            P("dom", "band", None, None),
            P("dom", None, None),
            P("dom", "band", None),
            P(),
            P(),
            P(),
            P(),
        ),
        out_specs=(
            P("dom", None, "band", None),
            P("dom", "band", None),
            P("dom", "band", None, None),
        ),
        check_vma=False,
    )
```

```python
import functools
import numpy as np
import jax
import jax.numpy as jnp
from jax import lax
from jax.experimental import pallas as pl
from jax.experimental.pallas import tpu as pltpu
from jax.sharding import PartitionSpec as P

NB = 128
G = 24
GG = G * G
BUFFER = 6
CG = 8
CZ = 6
NZC = 192
DOMS = 32
BANDS = 8
LOCAL = NB // BANDS
PLANES = G // BANDS
ROW = 640
SHARE = 1792
PACKED = 72
HALF_ROW = GG // 2
EDGE = GG + HALF_ROW
POINTS = float(G * G * G)
FILTER_LOW = 1.0
FILTER_HIGH = 9.5
CENTER = 0.5 * (FILTER_HIGH + FILTER_LOW)
HALF = 0.5 * (FILTER_HIGH - FILTER_LOW)
HIGHEST = lax.Precision.HIGHEST
F32 = jnp.float32
INTERPRET = False
LIMIT = pltpu.CompilerParams(vmem_limit_bytes=16 << 20)


def tables():
    k = np.arange(CG)
    cosine = np.sqrt(2.0 / CG) * np.cos(np.pi * k[:, None] * (k[None, :] + 0.5) / CG)
    cosine[0] *= np.sqrt(0.5)
    r = np.arange(NZC)
    sine = np.zeros((NZC + 8, NZC))
    sine[:NZC] = np.sqrt(2.0 / (NZC + 1)) * np.sin(np.pi * (r[:, None] + 1) * (r[None, :] + 1) / (NZC + 1))
    level_xy = 4.0 * np.sin(0.5 * np.pi * k / CG) ** 2
    level_z = 4.0 * np.sin(0.5 * np.pi * (r + 1) / (NZC + 1)) ** 2
    inverse = 1.0 / (level_xy[:, None, None] + level_xy[None, :, None] + level_z[None, None, :])
    scale = 8.0 / float(NZC * NZC)
    onto_x = np.broadcast_to((scale * cosine.T)[:, :, None], (CG, CG, NZC))
    lane = np.arange(GG)
    gather = np.zeros((ROW, 256))
    for ky in range(CG):
        gather[lane, ky * G + lane % G] = cosine[ky, (lane // G) // 3]
    over_x = np.broadcast_to(cosine.T[:, :, None], (CG, CG, 256))
    over_y = np.broadcast_to(cosine[:, :, None], (CG, CG, 256))
    sine = np.stack([sine[CZ * place : CZ * place + 8] for place in range(DOMS)])
    as_f32 = lambda a: np.ascontiguousarray(a, dtype=np.float32)
    return tuple(as_f32(a) for a in (sine, inverse.reshape(CG * CG, NZC), onto_x, gather, over_x, over_y))


def halves(x):
    high = x.astype(jnp.bfloat16)
    return high, (x - high.astype(F32)).astype(jnp.bfloat16)


def dot3(x, y, dims=(((1,), (0,)), ((), ()))):
    x_high, x_low = halves(x)
    y_high, y_low = halves(y)
    dot = functools.partial(lax.dot_general, dimension_numbers=dims, preferred_element_type=F32)
    return dot(x_high, y_high) + (dot(x_high, y_low) + dot(x_low, y_high))


def rolled(x, shift):
    return pltpu.roll(x, shift % ROW, 1)


def lane_index(shape):
    lane = lax.broadcasted_iota(jnp.int32, shape, 1).astype(F32)
    return lane, lane - G * jnp.floor((lane + 0.5) * (1.0 / G))


def neighbour_matrix(mat_ref):
    mat_ref[...] = jnp.zeros_like(mat_ref)
    for t in range(ROW // 128):
        top, end = max(0, 128 * t - 32), min(ROW, 128 * t + 160)
        shape = (end - top, 128)
        row = lax.broadcasted_iota(jnp.int32, shape, 0) + top
        col = lax.broadcasted_iota(jnp.int32, (8, 128), 1) + 128 * t
        _, z = lane_index((8, ROW))
        z = z[:, 128 * t : 128 * (t + 1)]
        before = jnp.where(z > 0.5, col - 1, -ROW)[0:1]
        after = jnp.where(z < G - 1.5, col + 1, -ROW)[0:1]
        col = col[0:1]
        hit = (row == before) | (row == after) | (row == col - G) | (row == col + G)
        hit = hit & (row < GG) & (col < GG)
        mat_ref[top:end, 128 * t : 128 * (t + 1)] = jnp.where(hit, 1.0, 0.0).astype(jnp.bfloat16)


def filter_kernel(
    orb_ref, pot_ref, mat_ref, occ_ref, pos_ref, mix_ref, corr_ref,
    out_ref, weight_ref, int_ref, zero_ref, first_ref, side_ref, diag_ref,
):
    eye = lax.broadcasted_iota(jnp.int32, (NB, NB), 0) == lax.broadcasted_iota(jnp.int32, (NB, NB), 1)
    weight = jnp.sum(jnp.where(eye, occ_ref[...] * (1.0 / NB), 0.0), axis=1, keepdims=True)
    weight_ref[...] = jnp.broadcast_to(weight, (NB, 256))
    int_ref[...] = jnp.zeros((8, 128), jnp.int32)
    int_ref[0:1, :DOMS] = pos_ref[...]
    int_ref[1:2, :2] = mix_ref[...]
    int_ref[2:3, :BUFFER] = corr_ref[...]
    diag_ref[:, GG - 64 :] = jnp.zeros((G, 128), F32)
    zero_ref[:, :, GG - 64 :] = jnp.zeros((G, LOCAL, 128), F32)
    diag_ref[:, :GG] = (pot_ref[...] + (3.0 - CENTER)) * 2.0
    dot = functools.partial(jnp.dot, preferred_element_type=F32)

    def sum_sides(source, c):
        high, low = halves(source[8 * c : 8 * c + 8].reshape(8 * LOCAL, ROW))
        stack = jnp.concatenate([high, low], 0)
        for rows, cols in ((slice(0, 384), slice(0, 256)), (slice(128, 640), slice(256, 512)), (slice(384, 640), slice(512, 640))):
            both = dot(stack[:, rows], mat_ref[rows, cols])
            side = both[: 8 * LOCAL] + both[8 * LOCAL :]
            side_ref[8 * c : 8 * c + 8, :, cols] = side.reshape(8, LOCAL, cols.stop - cols.start)

    def applied(source, x):
        v = source[x]
        near = side_ref[x]
        if x > 0:
            near = near + source[x - 1]
        if x + 1 < G:
            near = near + source[x + 1]
        return diag_ref[x : x + 1] * v - near

    for c in range(3):
        for x in range(8 * c, 8 * c + 8):
            zero_ref[x, :, :GG] = orb_ref[:, x, :]
        sum_sides(zero_ref, c)
    for x in range(G):
        first_ref[x] = applied(zero_ref, x)
    for c in range(3):
        sum_sides(first_ref, c)
    for x in range(G):
        second = (0.5 / HALF**2) * applied(first_ref, x) - zero_ref[x]
        p = x % PLANES
        out_ref[x // PLANES, :, p * GG : (p + 1) * GG] = second[:, :GG]
        if p == PLANES - 1:
            out_ref[x // PLANES, :, PLANES * GG :] = jnp.zeros((LOCAL, SHARE - PLANES * GG), F32)


def filtered_shares(orbitals, potential, occupation, *integers):
    matrix = pl.pallas_call(
        neighbour_matrix,
        out_shape=jax.ShapeDtypeStruct((ROW, ROW), jnp.bfloat16),
        cost_estimate=pl.CostEstimate(flops=20_000_000_000, bytes_accessed=4_000_000, transcendentals=0),
        compiler_params=LIMIT,
        interpret=INTERPRET,
        name="matrix",
    )()
    return pl.pallas_call(
        filter_kernel,
        out_shape=(
            jax.ShapeDtypeStruct((BANDS, LOCAL, SHARE), F32),
            jax.ShapeDtypeStruct((NB, 256), F32),
            jax.ShapeDtypeStruct((8, 128), jnp.int32),
        ),
        scratch_shapes=[
            pltpu.VMEM((G, LOCAL, ROW), F32),
            pltpu.VMEM((G, LOCAL, ROW), F32),
            pltpu.VMEM((G, LOCAL, ROW), F32),
            pltpu.VMEM((G, ROW), F32),
        ],
        compiler_params=LIMIT,
        interpret=INTERPRET,
        name="filter",
    )(orbitals, potential, matrix, occupation, *integers)


def gram_kernel(f_ref, out_ref):
    high, low = halves(f_ref[...])
    both = lax.dot_general(
        high, jnp.concatenate([high, low], 0), (((1,), (1,)), ((), ())), preferred_element_type=F32
    )
    cross = both[:, NB:]
    raw = both[:, :NB] + (cross + cross.T)
    row = lax.broadcasted_iota(jnp.int32, (64, NB), 0)
    col = lax.broadcasted_iota(jnp.int32, (64, NB), 1)
    lower = pltpu.roll(raw[64:], 64, 1)
    packed = jnp.where(col >= row, raw[:64], lower)
    diag = jnp.sum(jnp.where(col == row + 64, raw[64:], 0.0), axis=0, keepdims=True)
    diag = jnp.broadcast_to(diag, (8, NB))
    for k in range(BANDS):
        out_ref[k, :64] = packed
        out_ref[k, 64:] = diag


def packed_grams(flat):
    return pl.pallas_call(
        gram_kernel,
        out_shape=jax.ShapeDtypeStruct((BANDS, PACKED, NB), F32),
        cost_estimate=pl.CostEstimate(flops=20_000_000_000, bytes_accessed=4_000_000, transcendentals=0),
        compiler_params=LIMIT,
        interpret=INTERPRET,
        name="gram",
    )(flat)


def lane_weights(int_ref, own, vec_ref):
    shape = (8, ROW)
    _, z = lane_index(shape)
    corr = jnp.zeros(shape, F32)
    for j in range(BUFFER):
        here = (jnp.abs(z - j) < 0.5) | (jnp.abs(z - (G - BUFFER + j)) < 0.5)
        corr = jnp.where(here, int_ref[2, j].astype(F32), corr)
    corr = corr * (1.0 / 16.0)
    fresh_weight = jnp.full(shape, int_ref[1, 0].astype(F32))
    input_weight = jnp.full(shape, int_ref[1, 1].astype(F32))
    both = fresh_weight + input_weight
    fresh_weight = fresh_weight / both
    input_weight = input_weight / both
    has_left = jnp.where(jnp.full(shape, own) > 0, 1.0, 0.0)
    has_right = jnp.where(jnp.full(shape, own) < DOMS - 1, 1.0, 0.0)
    low_z = z < BUFFER - 0.5
    high_z = z > G - BUFFER - 0.5
    from_left = jnp.where(low_z, corr * has_left, 0.0)
    from_right = jnp.where(high_z, (1.0 - corr) * has_right, 0.0)
    keep = 1.0 - from_left - from_right
    cell = 1.0 / 27.0
    vec_ref[0:1] = (cell * fresh_weight * jnp.where(high_z, corr * has_right, keep))[0:1]
    vec_ref[1:2] = jnp.where(high_z, 0.0, cell * input_weight)[0:1]
    vec_ref[2:3] = (fresh_weight * from_left)[0:1]
    vec_ref[3:4] = (fresh_weight * from_right)[0:1]
    vec_ref[4:5] = (fresh_weight * keep)[0:1]
    vec_ref[5:6] = input_weight[0:1]


def poisson_tables(int_ref, own, band, sine_ref, inverse_ref, onto_ref, side_ref, mine_ref, weigh_ref, right_ref, all_ref):
    for d in range(DOMS):
        place = jnp.full((1, 128), int_ref[0, d])
        side_ref[0, d : d + 1] = jnp.where(place == own - 1, 1.0, 0.0)
        side_ref[1, d : d + 1] = jnp.where(place == own + 1, 1.0, 0.0)
        all_ref[8 * d : 8 * d + 8] = sine_ref[int_ref[0, d]]
    mine_ref[...] = sine_ref[own]
    onto = onto_ref[band]
    for ky in range(CG):
        weigh_ref[8 * ky : 8 * ky + 8] = inverse_ref[8 * ky : 8 * ky + 8] * onto
    high, low = halves(all_ref[...])
    right_ref[0] = high
    right_ref[1] = low


def density_kernel(
    g_ref, f_ref, weight_ref, din_ref, gather_ref, int_ref, sine_ref, inverse_ref, onto_ref,
    out_ref, coarse_ref, own_ref, edge_ref, vec_ref, side_ref, mine_ref, weigh_ref, right_ref,
    point_ref, fresh_ref, rows_ref, all_ref, scalar_ref, sems,
):
    scalars = pltpu.make_async_copy(int_ref, scalar_ref, sems.at[7])
    scalars.start()
    total = g_ref[0]
    for k in range(1, BANDS):
        total = total + g_ref[k]
    packed = total[:64]
    row = lax.broadcasted_iota(jnp.int32, (64, NB), 0)
    col = lax.broadcasted_iota(jnp.int32, (64, NB), 1)
    top = jnp.where(col > row, packed, jnp.where(col == row, 0.5 * packed, 0.0))
    low = pltpu.roll(jnp.where(col < row, packed, 0.0), 64, 1)
    low = low + jnp.where(col == row + 64, 0.5 * total[64:65], 0.0)
    half = jnp.concatenate([top, low], 0)
    raw = half + half.T
    norm = jnp.sqrt(jnp.sum(jnp.sum(raw * raw, axis=0, keepdims=True), axis=1, keepdims=True))
    a = raw / norm
    scaling = jnp.sqrt(POINTS / norm)
    eye = jnp.where(
        lax.broadcasted_iota(jnp.int32, (NB, NB), 0) == lax.broadcasted_iota(jnp.int32, (NB, NB), 1), 1.0, 0.0
    )
    square = dot3(a, a)
    tail = dot3(square, 0.0625 * square - 0.5625 * a)
    poly = scaling * (2.25 * eye + (1.6875 * square - 2.4375 * a) + tail)
    poly_high, poly_low = halves(poly)
    dot = functools.partial(jnp.dot, preferred_element_type=F32)

    copies = []
    for c in range(7):
        start, count = 256 * c, min(256, PLANES * GG - 256 * c)
        for at in range(start, start + count, 128):
            high, low = halves(f_ref[:, at : at + 128].T)
            value = dot(high, poly_high) + (dot(high, poly_low) + dot(low, poly_high))
            point_ref[at : at + 128] = value
        part = pl.ds(start, count)
        copies.append(pltpu.make_async_copy(point_ref.at[part], out_ref.at[part], sems.at[c]))
        copies[-1].start()

    both = jnp.concatenate([poly_high, poly_low], 1)
    for c in range(SHARE // 256):
        cols = slice(256 * c, 256 * (c + 1))
        high, low = halves(f_ref[:, cols])
        current = dot(both, jnp.concatenate([high, high], 0)) + dot(poly_high, low)
        line = jnp.sum(current * current * weight_ref[...], axis=0, keepdims=True)
        fresh_ref[:, cols] = jnp.broadcast_to(line, (8, 256))
    planes = [fresh_ref[:, p * GG : p * GG + ROW] for p in range(PLANES)]

    rows_ref[...] = jnp.zeros_like(rows_ref)
    rows_ref[0:8, :GG] = (planes[0] + planes[1] + planes[2])[:, :GG]
    rows_ref[8:9, :GG] = din_ref[0] + din_ref[1] + din_ref[2]
    cells = dot3(rows_ref[...], gather_ref[...])
    row = lax.broadcasted_iota(jnp.int32, (8, NB), 0)
    inputs = jnp.broadcast_to(cells[8:9], (8, 256))
    tile = jnp.where(row == 0, cells[:8, :128], cells[:8, 128:])
    tile = jnp.where(row == 2, inputs[:, :128], jnp.where(row == 3, inputs[:, 128:], tile))
    for k in range(BANDS):
        coarse_ref[k] = tile

    scalars.wait()
    if INTERPRET:
        dom, band = scalar_ref[3, 0], scalar_ref[3, 1]
    else:
        dom, band = lax.axis_index("dom"), lax.axis_index("band")
    own = scalar_ref[0, dom]
    lane_weights(scalar_ref, own, vec_ref)
    lane, z = lane_index((8, ROW))
    low_edge = (z < BUFFER - 0.5) & (lane < GG)
    high_edge = (z > G - BUFFER - 0.5) & (lane < GG)
    middle = (z > BUFFER - 0.5) & (z < G - BUFFER - 0.5)
    edges = []
    for p in range(PLANES):
        own_ref[p] = vec_ref[4:5, :GG] * planes[p][0:1, :GG] + vec_ref[5:6, :GG] * din_ref[p]
        edges.append((jnp.where(low_edge, planes[p], 0.0), jnp.where(high_edge, planes[p], 0.0)))
    first = (edges[0][0] + edges[0][1]) + (rolled(edges[1][0], 12) + rolled(edges[1][1], -12))
    last = edges[2][0] + edges[2][1]
    moved = rolled(edges[2][0], 12 - HALF_ROW) + rolled(edges[2][1], -12 - HALF_ROW)
    last = jnp.where(lane < HALF_ROW, jnp.where(middle, moved, last), 0.0)
    first = first + rolled(jnp.where(lane < 64, last, 0.0), GG)
    rest = rolled(last, -64)
    edge_ref[0:1] = jnp.zeros((1, 128), F32)
    for t in range(7):
        source, at = (first, 128 * t) if t < 5 else (rest, 128 * (t - 5))
        edge_ref[t + 1 : t + 2] = source[0:1, at : at + 128]
    poisson_tables(
        scalar_ref, own, band, sine_ref, inverse_ref, onto_ref, side_ref, mine_ref, weigh_ref, right_ref, all_ref
    )
    for copy in copies:
        copy.wait()


def density_parts(grams, flat, weight, din, gather, integers, sine, inverse, onto):
    if INTERPRET:
        axes = jnp.stack([lax.axis_index("dom"), lax.axis_index("band")])
        integers = integers.at[3, :2].set(axes)
    vmem = pl.BlockSpec(memory_space=pltpu.VMEM)
    return pl.pallas_call(
        density_kernel,
        out_shape=(
            jax.ShapeDtypeStruct((PLANES * GG, NB), F32),
            jax.ShapeDtypeStruct((BANDS, 8, 128), F32),
            jax.ShapeDtypeStruct((PLANES, 1, GG), F32),
            jax.ShapeDtypeStruct((8, 128), F32),
            jax.ShapeDtypeStruct((8, ROW), F32),
            jax.ShapeDtypeStruct((2, DOMS, 128), F32),
            jax.ShapeDtypeStruct((8, NZC), F32),
            jax.ShapeDtypeStruct((CG * CG, NZC), F32),
            jax.ShapeDtypeStruct((2, 256, NZC), jnp.bfloat16),
        ),
        in_specs=[vmem] * 9,
        out_specs=(pl.BlockSpec(memory_space=pltpu.HBM), *[vmem] * 8),
        scratch_shapes=[
            pltpu.VMEM((SHARE, NB), F32),
            pltpu.VMEM((8, SHARE), F32),
            pltpu.VMEM((16, ROW), F32),
            pltpu.VMEM((256, NZC), F32),
            pltpu.SMEM((8, 128), jnp.int32),
            pltpu.SemaphoreType.DMA((8,)),
        ],
        compiler_params=LIMIT,
        interpret=INTERPRET,
        name="density",
    )(grams, flat, weight, din, gather, integers, sine, inverse, onto)


def share_kernel(
    rows_ref, vec_ref, mine_ref, weigh_ref, right_ref, over_x_ref, over_y_ref, edge_ref, out_ref, turn_ref, line_ref
):
    fresh = jnp.concatenate([rows_ref[:, 0, :], rows_ref[:, 1, :]], 1)
    inputs = jnp.concatenate([rows_ref[:, 2, :], rows_ref[:, 3, :]], 1)
    cells = fresh * vec_ref[0:1, :256] + inputs * vec_ref[1:2, :256]
    cells = cells + (pltpu.roll(cells, 255, 1) + pltpu.roll(cells, 254, 1))
    modes = over_x_ref[0] * cells[0:1]
    for x in range(1, CG):
        modes = modes + over_x_ref[x] * cells[x : x + 1]
    parts = []
    for ky in range(CG):
        acc = jnp.zeros((8, NZC), F32)
        for j in range(8):
            at = G * ky + 3 * j
            acc = acc + jnp.broadcast_to(modes[:, at : at + 1], (8, NZC)) * mine_ref[j : j + 1]
        acc = acc * weigh_ref[8 * ky : 8 * ky + 8]
        parts.append(over_y_ref[ky, :, :NZC] * jnp.sum(acc, axis=0, keepdims=True))
    while len(parts) > 1:
        parts = [a + b for a, b in zip(parts[::2], parts[1::2])]
    spectrum = parts[0]
    high, low = halves(spectrum)
    dot = functools.partial(
        lax.dot_general, dimension_numbers=(((1,), (1,)), ((), ())), preferred_element_type=F32
    )
    cells = dot(high, right_ref[0]) + (dot(high, right_ref[1]) + dot(low, right_ref[0]))
    turn_ref[:, :8] = cells.T
    line_ref[...] = jnp.zeros_like(line_ref)
    for j in range(CZ):
        line_ref[:, 8 * j : 8 * j + 8] = turn_ref[pl.ds(j, DOMS, stride=8), :][:, :8]
    head = lax.broadcasted_iota(jnp.int32, (8, 128), 0) == 0
    edge = edge_ref[...]
    for d in range(DOMS):
        out_ref[d] = jnp.where(head, line_ref[d : d + 1], edge)


def hartree_shares(rows, vectors, mine, weigh, right, over_x, over_y, edges):
    return pl.pallas_call(
        share_kernel,
        out_shape=jax.ShapeDtypeStruct((DOMS, 8, 128), F32),
        scratch_shapes=[pltpu.VMEM((256, 128), F32), pltpu.VMEM((DOMS, 128), F32)],
        compiler_params=LIMIT,
        interpret=INTERPRET,
        name="share",
    )(rows, vectors, mine, weigh, right, over_x, over_y, edges)


def final_kernel(side_ref, msg_ref, own_ref, vec_ref, dens_ref, hart_ref):
    total = msg_ref[0]
    for d in range(1, DOMS):
        total = total + msg_ref[d]
    for j in range(CZ):
        hart_ref[j] = total[0:1, 8 * j : 8 * j + 8]
    lane = lax.broadcasted_iota(jnp.int32, (8, ROW), 1)

    def picked(side):
        tile = jnp.zeros((8, 128), F32)
        for d in range(DOMS):
            tile = tile + side_ref[side, d : d + 1] * msg_ref[d]
        return tile

    def rows(tile):
        spread = [jnp.broadcast_to(tile[t + 1 : t + 2], (8, 128)) for t in range(7)]
        front = jnp.concatenate(spread[:5], 1)
        back = jnp.concatenate(spread[4:] + spread[5:], 1)
        return front, rolled(back, -64)

    left0, left2 = rows(picked(0))
    right0, right2 = rows(picked(1))
    far = G - BUFFER
    left_last = jnp.where(lane < HALF_ROW, rolled(left2, -far), rolled(left2, HALF_ROW + 12 - far))
    right_last = jnp.where(lane < HALF_ROW, rolled(right2, far), rolled(right2, HALF_ROW - 12 + far))
    left_part = (rolled(left0, -far), rolled(left0, -6), left_last)
    right_part = (rolled(right0, far), rolled(right0, 6), right_last)
    for p in range(PLANES):
        mixed = own_ref[p] + vec_ref[2:3, :GG] * left_part[p][0:1, :GG]
        dens_ref[p] = mixed + vec_ref[3:4, :GG] * right_part[p][0:1, :GG]


def final_parts(sides, msg, own, vectors):
    return pl.pallas_call(
        final_kernel,
        out_shape=(
            jax.ShapeDtypeStruct((PLANES, 1, GG), F32),
            jax.ShapeDtypeStruct((CZ, 1, CG), F32),
        ),
        compiler_params=LIMIT,
        interpret=INTERPRET,
        name="final",
    )(sides, msg, own, vectors)


def exchanged(x, axis):
    return lax.all_to_all(x, axis, split_axis=0, concat_axis=0, tiled=True)


def body(orbitals, potential, density_in, occupation, position, mixing, correlation_weight):
    sine, inverse, onto, gather, over_x, over_y = tables()
    din = jnp.transpose(density_in, (1, 0, 2))
    small = [v.reshape(1, -1) for v in (occupation, position, mixing, correlation_weight)]
    filtered, weight, integers = filtered_shares(orbitals[0], potential[0], *small)
    flat = exchanged(filtered, "band").reshape(NB, SHARE)
    grams = exchanged(packed_grams(flat), "band")
    points, coarse, own, edges, vectors, sides, mine, weigh, right = density_parts(
        grams, flat, weight, din, gather, integers, sine, inverse, onto
    )
    rows = exchanged(coarse, "band")
    msg = exchanged(hartree_shares(rows, vectors, mine, weigh, right, over_x, over_y, edges), "dom")
    dens, hart = final_parts(sides, msg, own, vectors)
    orbitals_out = jnp.transpose(points.reshape(PLANES, GG, NB), (2, 0, 1)).reshape(1, NB, PLANES, GG)
    density = jnp.transpose(dens, (1, 0, 2))
    hartree = jnp.transpose(hart, (1, 2, 0)).reshape(1, 1, CG, CZ)
    return orbitals_out, density, hartree


def solution(mesh):
    return jax.shard_map(
        body,
        mesh=mesh,
        in_specs=(
            P("dom", "band", None, None),
            P("dom", None, None),
            P("dom", "band", None),
            P(),
            P(),
            P(),
            P(),
        ),
        out_specs=(
            P("dom", None, "band", None),
            P("dom", "band", None),
            P("dom", "band", None, None),
        ),
        check_vma=False,
    )
```
